32 devices in a mesh: gz: 8 (over z, y), gy: 4 (over x, core).
Axes of the slice: x: 2, y: 2, z: 4, core: 2. Of those that a mesh axis runs over, the one named last changes fastest.
Arguments:
- order_param: float32 [32, 128, 512], P('gz', 'gy'), may hold values from 0.2 to 1
- orientation: float32 [32, 128, 512], P('gz', 'gy'), may hold values from -1 to 1
- cell_slot: int32 [32, 128, 512], P('gz', 'gy'), may hold values from 0 to 255, as said below
- tile_grains: int32 [8, 4, 256], P('gz', 'gy'), may hold values from 0 to 4095, as said below
Outputs:
- order_out: float32 [32, 128, 512], P('gz', 'gy')
- orientation_out: float32 [32, 128, 512], P('gz', 'gy')
The draws below stay inside these ranges and needn't reach their ends.
Inputs may be any that keep to these rules, and one draw needn't show every extreme that they name: `tile_grains`: each tile lists 256 distinct grain ids; every grain is listed by exactly two tiles, which are neighbours along the periodic z dimension and have the same y index. `cell_slot`: every position of a tile's list is used by at least one cell of that tile; the value is constant over aligned blocks of 1 x 2 x 4 cells along z, y, x.
All inputs are finite; a program needn't handle non-finite values.
Results may differ from the reference program's by a relative error of at most 0.0003.
Values sent between devices are 32-bit elements; how exact they have to be, the bound alone decides.
No kernel may reach another device: no remote copies, remote signals or barrier semaphores. Data moves between devices by JAX's collectives and lax.ppermute only.
A program may use at most 128 MiB of HBM per device.

```python
import math
import jax
import jax.numpy as jnp
from jax import lax

NX = 512
CY = 32
CZ = 4
SLOTS = 256
STEPS = 3
TILES_Z = 8
TILES_Y = 4
NZ = 32
NY = 128
GRAINS = 4096


def draw_cell_slot(key, part):
    first_key, second_key = jax.random.split(jax.random.fold_in(key, 11))
    shape_all = (NZ, NY, NX)
    z_index = lax.broadcasted_iota(jnp.int32, shape_all, 0)
    y_index = lax.broadcasted_iota(jnp.int32, shape_all, 1)
    x_index = lax.broadcasted_iota(jnp.int32, shape_all, 2)
    block_rows = CY // 2
    block_cols = NX // 4
    per_tile = CZ * block_rows * block_cols
    block_index = (z_index % CZ * block_rows + y_index % CY // 2) * block_cols + x_index // 4
    tile_index = z_index // CZ * TILES_Y + y_index // CY
    offsets = jax.random.randint(first_key, (TILES_Z * TILES_Y,), 0, SLOTS)
    covering = (block_index + offsets[tile_index]) % SLOTS
    scattered_all = jax.random.randint(second_key, (TILES_Z * TILES_Y * per_tile,), 0, SLOTS)
    scattered = scattered_all[tile_index * per_tile + block_index]
    return jnp.where(block_index < SLOTS, covering, scattered).astype(jnp.int32)


def draw_tile_grains(key, part):
    first_key, second_key, third_key = jax.random.split(jax.random.fold_in(key, 23), 3)
    tile_count = TILES_Z * TILES_Y
    half_slots = SLOTS // 2
    shuffled = jax.random.permutation(first_key, GRAINS)
    own_block = shuffled.reshape(tile_count, half_slots)
    tile_ids = jnp.arange(tile_count, dtype=jnp.int32)
    z_tile = tile_ids // TILES_Y
    y_tile = tile_ids % TILES_Y
    parity = jax.random.randint(second_key, (TILES_Y,), 0, 2)[y_tile]
    partner_z = (jnp.bitwise_xor((z_tile + parity) % TILES_Z, 1) - parity) % TILES_Z
    partner = partner_z * TILES_Y + y_tile
    borrowed = own_block[partner]
    listed = jnp.concatenate([own_block, borrowed], axis=1)
    listed = jax.random.permutation(third_key, listed, axis=1, independent=True)
    return listed.reshape(TILES_Z, TILES_Y, SLOTS).astype(jnp.int32)


def block_levels(rng, extent, shards, least, top_value):
    def one(axis_at, shards_of):
        heights = jax.random.uniform(jax.random.fold_in(jax.random.fold_in(rng, 6), axis_at), (shards_of,), jnp.float32, least / len(shards), top_value / len(shards))
        return jnp.repeat(jnp.exp(heights), extent[axis_at] // shards_of).reshape((-1,) + (1,) * (len(extent) - axis_at - 1))

    level = one(*shards[0])
    for cut in shards[1:]:
        level = level * one(*cut)
    return level


def setup_inputs(seed: int = 0) -> dict:
    seeds = jax.random.split(jax.random.key(seed), 5)
    return {
        "order_param": jnp.clip(jnp.exp(math.log(1.0) - 1.609438 * jax.random.uniform(seeds[0], (NZ, NY, NX), jnp.float32) ** block_levels(seeds[0], (NZ, NY, NX), ((0, 8), (1, 4)), -0.2, 0.2)), 0.2, 1.0),
        "orientation": jnp.clip(jax.random.uniform(seeds[1], (NZ, NY, NX), jnp.float32, -1.0, 1.0) * block_levels(seeds[1], (NZ, NY, NX), ((0, 8), (1, 4)), -0.4, 0.0), -1.0, 1.0),
        "cell_slot": draw_cell_slot(jax.random.fold_in(seeds[4], 71), 0),
        "tile_grains": draw_tile_grains(jax.random.fold_in(seeds[4], 71), 0),
    }


DIFFUSE = 0.1
BARRIER = 0.5
PENALTY = 0.05
TORSION = 0.1
TRANSLATE = 2.0
ROTATE = 2.0


def neighbour_fields(fields):
    z_plus = jnp.roll(fields, -1, axis=1)
    z_minus = jnp.roll(fields, 1, axis=1)
    padded = jnp.pad(fields, ((0, 0), (0, 0), (1, 1), (0, 0)))
    y_plus = padded[:, :, 2:]
    y_minus = padded[:, :, :-2]
    x_plus = jnp.roll(fields, -1, axis=3)
    x_minus = jnp.roll(fields, 1, axis=3)
    return (x_plus, x_minus, y_plus, y_minus, z_plus, z_minus)


def cell_terms(fields, neighbours):
    phase_field = fields[0]
    grain_angle = fields[1]
    laplace = -6.0 * phase_field
    misfit = jnp.zeros_like(phase_field)
    torque = jnp.zeros_like(phase_field)
    for beside in neighbours:
        other_phase = beside[0]
        mismatch = beside[1] - grain_angle
        laplace = laplace + other_phase
        misfit = misfit + (1.0 - jnp.cos(mismatch))
        torque = torque + other_phase * other_phase * jnp.sin(mismatch)
    gradients = [(neighbours[2 * k] - neighbours[2 * k + 1]) * 0.5 for k in range(3)]
    weight = phase_field * misfit
    densities = jnp.stack([weight * gradients[0][0], weight * gradients[1][0], weight * gradients[2][0], torque, 0.5 + phase_field * phase_field])
    return densities, laplace, misfit, torque, gradients


def grain_motion(totals):
    inverse = 1.0 / totals[4]
    return jnp.stack([TRANSLATE * totals[0] * inverse, TRANSLATE * totals[1] * inverse, TRANSLATE * totals[2] * inverse, ROTATE * totals[3] * inverse])


def advance(fields, laplace, misfit, torque, gradients, motion):
    phase_field = fields[0]
    grain_angle = fields[1]
    carried = motion[0] * gradients[0] + motion[1] * gradients[1] + motion[2] * gradients[2]
    next_phase = phase_field + DIFFUSE * laplace + BARRIER * phase_field * (1.0 - phase_field) * (phase_field - 0.5) - PENALTY * phase_field * misfit - carried[0]
    next_angle = grain_angle + TORSION * torque + motion[3] - carried[1]
    return jnp.stack([next_phase, next_angle])


def reference(order_param, orientation, cell_slot, tile_grains):
    tile_lists = jnp.repeat(jnp.repeat(tile_grains, CZ, axis=0), CY, axis=1)
    grain_id = jnp.take_along_axis(tile_lists, cell_slot, axis=2).astype(jnp.int32)
    flat_grain = grain_id.reshape(-1)
    fields = jnp.stack([order_param, orientation])
    for iteration in range(STEPS):
        neighbours = neighbour_fields(fields)
        densities, laplace, misfit, torque, gradients = cell_terms(fields, neighbours)
        totals = jax.vmap(lambda values: jax.ops.segment_sum(values, flat_grain, num_segments=GRAINS))(densities.reshape(5, -1))
        motion = jnp.take(grain_motion(totals), grain_id, axis=1)
        fields = advance(fields, laplace, misfit, torque, gradients, motion)
    return fields[0], fields[1]
```

```python
import functools

import jax
import jax.numpy as jnp
from jax import lax
from jax.experimental import pallas as pl
from jax.experimental.pallas import tpu as pltpu
from jax.sharding import PartitionSpec as P

STEPS = 3

DIFFUSE = 0.1
BARRIER = 0.5
PENALTY = 0.05
TORSION = 0.1
TRANSLATE = 2.0
ROTATE = 2.0

ROWS = 2
COLS = 4


def split3(value):
    high = value.astype(jnp.bfloat16)
    rest = value - high.astype(jnp.float32)
    middle = rest.astype(jnp.bfloat16)
    low = (rest - middle.astype(jnp.float32)).astype(jnp.bfloat16)
    return high, middle, low


def exact_dot(value, chooser):
    return sum(jnp.dot(part, chooser, preferred_element_type=jnp.float32) for part in split3(value))


def sin_cos(angle):
    turns = jnp.floor(angle * 0.6366197723675814 + 0.5)
    rest = angle - turns * 1.5703125
    rest = rest - turns * 4.837512969970703125e-4
    rest = rest - turns * 7.54978995489188216e-8
    square = rest * rest
    sine = ((-1.9515295891e-4 * square + 8.3321608736e-3) * square - 1.6666654611e-1) * square * rest + rest
    cosine = ((2.443315711809948e-5 * square - 1.388731625493765e-3) * square + 4.166664568298827e-2) * square * square
    cosine = cosine - 0.5 * square + 1.0
    quarter = turns.astype(jnp.int32)
    odd = (quarter & 1) == 1
    sin_value = jnp.where(odd, cosine, sine)
    cos_value = jnp.where(odd, sine, cosine)
    sin_value = jnp.where((quarter & 2) == 2, -sin_value, sin_value)
    cos_value = jnp.where(((quarter + 1) & 2) == 2, -cos_value, cos_value)
    return sin_value, cos_value


def boundary(fields_ref, below_ref, above_ref, first_ref, last_ref, cz, yb):
    for f in range(2):
        for p in range(ROWS):
            for j in range(COLS):
                below_ref[f, p, j] = fields_ref[f, 0, p, j]
                above_ref[f, p, j] = fields_ref[f, cz - 1, p, j]
        for z in range(cz):
            for j in range(COLS):
                at = (f * cz + z) * COLS + j
                first_ref[at : at + 1, :] = fields_ref[f, z, 0, j, 0:1, :]
                last_ref[at : at + 1, :] = fields_ref[f, z, ROWS - 1, j, yb - 1 : yb, :]


def prepare_kernel(e_ref, q_ref, slot_ref, fields_ref, below_ref, above_ref, first_ref, last_ref, block_ref, rows_ref):
    cz, cy, nx = e_ref.shape
    yb, xb = cy // ROWS, nx // COLS
    row = lax.broadcasted_iota(jnp.int32, (nx, nx), 0)
    col = lax.broadcasted_iota(jnp.int32, (nx, nx), 1)
    chooser = jnp.where(row == COLS * (col % xb) + col // xb, 1.0, 0.0).astype(jnp.bfloat16)
    for f, ref in enumerate((e_ref, q_ref)):
        moved = exact_dot(ref[...].reshape(cz * cy, nx), chooser)
        for j in range(COLS):
            rows_ref[j] = moved[:, j * xb : (j + 1) * xb]
        for z in range(cz):
            for p in range(ROWS):
                for j in range(COLS):
                    fields_ref[f, z, p, j] = rows_ref[j, pl.ds(z * cy + p, yb, stride=ROWS), :]
    slots = slot_ref[...].reshape(cz * cy, nx).astype(jnp.float32).astype(jnp.bfloat16)
    rows_ref[0] = jnp.dot(slots, chooser[:, :xb], preferred_element_type=jnp.float32)
    block_ref[...] = rows_ref[0, pl.ds(0, cz * yb, stride=ROWS), :]
    boundary(fields_ref, below_ref, above_ref, first_ref, last_ref, cz, yb)


def onehot_kernel(block_ref, onehot_ref):
    rows, xb = block_ref.shape
    slots = onehot_ref.shape[1]
    slot = lax.broadcasted_iota(jnp.int32, (slots, xb), 0).astype(jnp.float32)
    for r in range(rows):
        hit = jnp.where(slot == block_ref[r : r + 1, :], 1.0, 0.0).astype(jnp.bfloat16)
        onehot_ref[r // 2, :, (r % 2) * xb : (r % 2 + 1) * xb] = hit


def terms_kernel(
    edge_ref, fields_ref, before_z_ref, after_z_ref, before_y_ref, after_y_ref, onehot_ref, ids_ref,
    message_ref, local_ref, grads_ref,
    all_ref, rim_ref, sums_ref, acc_ref,
):
    _, cz, _, _, yb, xb = fields_ref.shape
    slots = ids_ref.shape[1]
    row = lax.broadcasted_iota(jnp.int32, (yb, xb), 0)

    def fill(put, e, q):
        sin_value, cos_value = sin_cos(q)
        square = e * e
        for k, value in enumerate((e, q, cos_value, sin_value, square * cos_value, square * sin_value)):
            put(k, value)

    for side, ref in enumerate((before_y_ref, after_y_ref)):
        n = cz * COLS
        keep = edge_ref[side] == 0
        e = jnp.where(keep, ref[0:n, :], 0.0)
        q = jnp.where(keep, ref[n : 2 * n, :], 0.0)

        def put(k, value, side=side):
            rim_ref[side, k] = value

        fill(put, e, q)
    for z in range(cz + 2):
        for p in range(ROWS):
            for j in range(COLS):
                if z == 0:
                    e, q = before_z_ref[0, p, j], before_z_ref[1, p, j]
                elif z == cz + 1:
                    e, q = after_z_ref[0, p, j], after_z_ref[1, p, j]
                else:
                    e, q = fields_ref[0, z - 1, p, j], fields_ref[1, z - 1, p, j]

                def put(k, value, z=z, p=p, j=j):
                    all_ref[k, z, p, j] = value

                fill(put, e, q)

    def beside(k, z, p, j):
        x_plus = all_ref[k, z, p, j + 1] if j + 1 < COLS else pltpu.roll(all_ref[k, z, p, 0], xb - 1, 1)
        x_minus = all_ref[k, z, p, j - 1] if j > 0 else pltpu.roll(all_ref[k, z, p, COLS - 1], 1, 1)
        at = (z - 1) * COLS + j
        if p + 1 < ROWS:
            y_plus = all_ref[k, z, p + 1, j]
        else:
            y_plus = jnp.where(
                row == yb - 1, rim_ref[1, k, at : at + 1, :], pltpu.roll(all_ref[k, z, 0, j], yb - 1, 0)
            )
        if p > 0:
            y_minus = all_ref[k, z, p - 1, j]
        else:
            y_minus = jnp.where(
                row == 0, rim_ref[0, k, at : at + 1, :], pltpu.roll(all_ref[k, z, ROWS - 1, j], 1, 0)
            )
        return x_plus, x_minus, y_plus, y_minus, all_ref[k, z + 1, p, j], all_ref[k, z - 1, p, j]

    for z in range(1, cz + 1):
        totals = None
        for p in range(ROWS):
            for j in range(COLS):
                e_side = beside(0, z, p, j)
                q_side = beside(1, z, p, j)
                c_sum, s_sum, a_sum, b_sum = (sum(beside(k, z, p, j)) for k in range(2, 6))
                e, q, c, s = (all_ref[k, z, p, j] for k in range(4))
                misfit = 6.0 - c * c_sum - s * s_sum
                torque = c * b_sum - s * a_sum
                e_grads = [(e_side[2 * d] - e_side[2 * d + 1]) * 0.5 for d in range(3)]
                q_grads = [(q_side[2 * d] - q_side[2 * d + 1]) * 0.5 for d in range(3)]
                laplace = sum(e_side) - 6.0 * e
                weight = e * misfit
                values = [weight * g for g in e_grads] + [torque, 0.5 + e * e]
                totals = values if totals is None else [a + b for a, b in zip(totals, values)]
                local_ref[0, z - 1, p, j] = (
                    e + DIFFUSE * laplace + BARRIER * e * (1.0 - e) * (e - 0.5) - PENALTY * weight
                )
                local_ref[1, z - 1, p, j] = q + TORSION * torque
                for d in range(3):
                    grads_ref[d, z - 1, p, j] = e_grads[d]
                    grads_ref[3 + d, z - 1, p, j] = q_grads[d]
        rows = cz * yb
        for k, value in enumerate(totals):
            for part, piece in enumerate(split3(value)):
                at = (part * 5 + k) * rows + (z - 1) * yb
                sums_ref[at : at + yb, :] = piece.astype(jnp.float32)
    rows = cz * yb
    sums_ref[15 * rows : 16 * rows, :] = jnp.zeros((rows, xb), jnp.float32)
    acc = jnp.zeros((16, slots), jnp.float32)
    for pair in range(rows // 2):
        left = jnp.concatenate(
            [sums_ref[pl.ds(2 * pair + h, 16, stride=rows), :] for h in range(2)], axis=1
        ).astype(jnp.bfloat16)
        acc = acc + lax.dot_general(
            left, onehot_ref[pair], (((1,), (1,)), ((), ())), preferred_element_type=jnp.float32
        )
    acc_ref[...] = acc
    message_ref[0:5, :] = acc_ref[0:5, :] + acc_ref[5:10, :] + acc_ref[10:15, :]
    message_ref[5:6, :] = ids_ref[...]
    message_ref[6:8, :] = jnp.zeros((2, slots), jnp.float32)


def stacked(value):
    return jnp.concatenate([part.astype(jnp.float32) for part in split3(value)], axis=0).astype(jnp.bfloat16)


def unstacked(value):
    return value[0:8] + value[8:16] + value[16:24]


def motion_into(message_ref, before_ref, after_ref, onehot_ref, motion_ref):
    slots = message_ref.shape[1]
    rows = motion_ref.shape[0] // 8
    xb = motion_ref.shape[1]
    totals = message_ref[...]
    own = jnp.broadcast_to(message_ref[5:6, :], (slots, slots))
    for ref in (before_ref, after_ref):
        other = jnp.transpose(jnp.broadcast_to(ref[5:6, :], (slots, slots)))
        matches = jnp.where(other == own, 1.0, 0.0).astype(jnp.bfloat16)
        totals = totals + unstacked(jnp.dot(stacked(ref[...]), matches, preferred_element_type=jnp.float32))
    inverse = 1.0 / totals[4:5, :]
    velocity = stacked(TRANSLATE * totals * inverse)
    for pair in range(rows // 2):
        moved = unstacked(jnp.dot(velocity, onehot_ref[pair], preferred_element_type=jnp.float32))
        for h in range(2):
            motion_ref[pl.ds(2 * pair + h, 8, stride=rows), :] = moved[:, h * xb : (h + 1) * xb]


def advanced(local_ref, grads_ref, motion_ref, z, p, j):
    _, cz, _, _, yb, _ = local_ref.shape
    rows = cz * yb
    vx, vy, vz, turn = (motion_ref[k * rows + z * yb : k * rows + (z + 1) * yb, :] for k in range(4))
    g = [grads_ref[k, z, p, j] for k in range(6)]
    e = local_ref[0, z, p, j] - (vx * g[0] + vy * g[1] + vz * g[2])
    q = local_ref[1, z, p, j] + turn - (vx * g[3] + vy * g[4] + vz * g[5])
    return e, q


def advance_kernel(
    message_ref, before_ref, after_ref, onehot_ref, local_ref, grads_ref,
    fields_ref, below_ref, above_ref, first_ref, last_ref,
    motion_ref,
):
    _, cz, _, _, yb, xb = local_ref.shape
    motion_into(message_ref, before_ref, after_ref, onehot_ref, motion_ref)
    for z in range(cz):
        for p in range(ROWS):
            for j in range(COLS):
                fields_ref[0, z, p, j], fields_ref[1, z, p, j] = advanced(
                    local_ref, grads_ref, motion_ref, z, p, j
                )
    boundary(fields_ref, below_ref, above_ref, first_ref, last_ref, cz, yb)


def finish_kernel(
    message_ref, before_ref, after_ref, onehot_ref, local_ref, grads_ref,
    e_ref, q_ref,
    motion_ref, rows_ref,
):
    _, cz, _, _, yb, xb = local_ref.shape
    nx = COLS * xb
    motion_into(message_ref, before_ref, after_ref, onehot_ref, motion_ref)
    for z in range(cz):
        for p in range(ROWS):
            at = pl.ds(z * ROWS * yb + p, yb, stride=ROWS)
            for j in range(COLS):
                rows_ref[0, j, at, :], rows_ref[1, j, at, :] = advanced(local_ref, grads_ref, motion_ref, z, p, j)
    row = lax.broadcasted_iota(jnp.int32, (nx, nx), 0)
    col = lax.broadcasted_iota(jnp.int32, (nx, nx), 1)
    chooser = jnp.where(col == COLS * (row % xb) + row // xb, 1.0, 0.0).astype(jnp.bfloat16)
    for f, ref in enumerate((e_ref, q_ref)):
        moved = exact_dot(jnp.concatenate([rows_ref[f, j] for j in range(COLS)], axis=1), chooser)
        ref[...] = moved.reshape(ref.shape)


VMEM = pl.BlockSpec(memory_space=pltpu.VMEM)
SMEM = pl.BlockSpec(memory_space=pltpu.SMEM)


def call(kernel, name, outs, scratch=(), scalars=0):
    def run(*args):
        return pl.pallas_call(
            kernel,
            name=name,
            in_specs=[SMEM] * scalars + [VMEM] * (len(args) - scalars),
            out_specs=[VMEM] * len(outs),
            out_shape=[jax.ShapeDtypeStruct(shape, dtype) for shape, dtype in outs],
            scratch_shapes=list(scratch),
            compiler_params=pltpu.CompilerParams(vmem_limit_bytes=32 * 1024 * 1024),
        )(*args)

    return run


def shift(array, axis, step):
    size = lax.axis_size(axis)
    return lax.ppermute(array, axis, [(i, (i + step) % size) for i in range(size)])


def shards(order_param, orientation, cell_slot, tile_grains):
    cz, cy, nx = order_param.shape
    slots = tile_grains.shape[-1]
    yb, xb = cy // ROWS, nx // COLS
    rows = cz * yb
    f32 = jnp.float32
    ids = tile_grains.reshape(1, slots).astype(f32)
    at_y = lax.axis_index("gy")
    edge = jnp.stack([at_y == 0, at_y == lax.axis_size("gy") - 1]).astype(jnp.int32)
    cells = (cz, ROWS, COLS, yb, xb)
    fields_out = [
        ((2,) + cells, f32),
        ((2,) + cells[1:], f32),
        ((2,) + cells[1:], f32),
        ((2 * cz * COLS, xb), f32),
        ((2 * cz * COLS, xb), f32),
    ]
    motion = pltpu.VMEM((8 * rows, xb), f32)
    prepare = call(prepare_kernel, "prepare", fields_out + [((rows, xb), f32)], [pltpu.VMEM((COLS, cz * cy, xb), f32)])
    onehots = call(onehot_kernel, "onehots", [((rows // 2, slots, 2 * xb), jnp.bfloat16)])
    terms = call(
        terms_kernel,
        "terms",
        [((8, slots), f32), ((2,) + cells, f32), ((6,) + cells, f32)],
        [
            pltpu.VMEM((6, cz + 2) + cells[1:], f32),
            pltpu.VMEM((2, 6, cz * COLS, xb), f32),
            pltpu.VMEM((16 * rows, xb), f32),
            pltpu.VMEM((16, slots), f32),
        ],
        scalars=1,
    )
    advance = call(advance_kernel, "advance", fields_out, [motion])
    finish = call(
        finish_kernel, "finish", [((cz, cy, nx), f32)] * 2, [motion, pltpu.VMEM((2, COLS, cz * cy, xb), f32)]
    )

    fields, below, above, first, last, block = prepare(order_param, orientation, cell_slot)
    (onehot,) = onehots(block)
    for step in range(STEPS):
        before_z = shift(above, "gz", 1)
        after_z = shift(below, "gz", -1)
        before_y = shift(last, "gy", 1)
        after_y = shift(first, "gy", -1)
        message, local, grads = terms(edge, fields, before_z, after_z, before_y, after_y, onehot, ids)
        before = shift(message, "gz", 1)
        after = shift(message, "gz", -1)
        operands = (message, before, after, onehot, local, grads)
        if step < STEPS - 1:
            fields, below, above, first, last = advance(*operands)
        else:
            return tuple(finish(*operands))


def solution(mesh):
    spec = P("gz", "gy", None)
    return jax.shard_map(shards, mesh=mesh, in_specs=(spec,) * 4, out_specs=(spec,) * 2, check_vma=False)
```

```python
import functools

import jax
import jax.numpy as jnp
from jax import lax
from jax.experimental import pallas as pl
from jax.experimental.pallas import tpu as pltpu
from jax.sharding import PartitionSpec as P

STEPS = 3

DIFFUSE = 0.1
BARRIER = 0.5
PENALTY = 0.05
TORSION = 0.1
TRANSLATE = 2.0
ROTATE = 2.0

ROWS = 2
COLS = 4


def split3(value):
    high = value.astype(jnp.bfloat16)
    rest = value - high.astype(jnp.float32)
    middle = rest.astype(jnp.bfloat16)
    low = (rest - middle.astype(jnp.float32)).astype(jnp.bfloat16)
    return high, middle, low


def exact_dot(value, chooser):
    return sum(jnp.dot(part, chooser, preferred_element_type=jnp.float32) for part in split3(value))


def sin_cos(angle):
    turns = jnp.floor(angle * 0.6366197723675814 + 0.5)
    rest = angle - turns * 1.5703125
    rest = rest - turns * 4.837512969970703125e-4
    rest = rest - turns * 7.54978995489188216e-8
    square = rest * rest
    sine = ((-1.9515295891e-4 * square + 8.3321608736e-3) * square - 1.6666654611e-1) * square * rest + rest
    cosine = ((2.443315711809948e-5 * square - 1.388731625493765e-3) * square + 4.166664568298827e-2) * square * square
    cosine = cosine - 0.5 * square + 1.0
    quarter = turns.astype(jnp.int32)
    odd = (quarter & 1) == 1
    sin_value = jnp.where(odd, cosine, sine)
    cos_value = jnp.where(odd, sine, cosine)
    sin_value = jnp.where((quarter & 2) == 2, -sin_value, sin_value)
    cos_value = jnp.where(((quarter + 1) & 2) == 2, -cos_value, cos_value)
    return sin_value, cos_value


def odd(axis):
    return (lax.axis_index(axis) & 1) == 1


def layer(outer_ref, inner_ref, k, z, p, j):
    cz = inner_ref.shape[1] + 2
    if z == 0:
        return outer_ref[k, 0, p, j]
    if z == cz - 1:
        return outer_ref[k, 1, p, j]
    return inner_ref[k, z - 1, p, j]


def put_z_edges(outer_ref, near_ref, far_ref):
    first_to_near = odd("gz").astype(jnp.int32)
    for f in range(2):
        for p in range(ROWS):
            for j in range(COLS):
                near_ref[f, p, j] = outer_ref[f, 1 - first_to_near, p, j]
                far_ref[f, p, j] = outer_ref[f, first_to_near, p, j]


def put_y_edges(outer_ref, inner_ref, near_ref, far_ref):
    cz, yb = inner_ref.shape[1] + 2, inner_ref.shape[4]
    first_to_near = odd("gy")
    for f in range(2):
        for z in range(cz):
            for j in range(COLS):
                at = (f * cz + z) * COLS + j
                first = layer(outer_ref, inner_ref, f, z, 0, j)[0:1]
                last = layer(outer_ref, inner_ref, f, z, ROWS - 1, j)[yb - 1 : yb]
                near_ref[at : at + 1, :] = jnp.where(first_to_near, first, last)
                far_ref[at : at + 1, :] = jnp.where(first_to_near, last, first)


def x_chooser(nx, xb, back=False):
    first = lax.broadcasted_iota(jnp.int32, (nx, nx), 1 if back else 0)
    second = lax.broadcasted_iota(jnp.int32, (nx, nx), 0 if back else 1)
    return jnp.where(first == COLS * (second % xb) + second // xb, 1.0, 0.0).astype(jnp.bfloat16)


def prepare_kernel(
    e_hbm, q_hbm,
    outer_ref, inner_ref, z_near_ref, z_far_ref, y_near_ref, y_far_ref,
    in_ref, rows_ref, sems,
):
    _, cz, cy, nx = in_ref.shape
    yb, xb = cy // ROWS, nx // COLS
    copies = [pltpu.make_async_copy(ref, in_ref.at[f], sems.at[f]) for f, ref in enumerate((e_hbm, q_hbm))]
    for copy in copies:
        copy.start()
    chooser = x_chooser(nx, xb)
    for f in range(2):
        copies[f].wait()
        moved = exact_dot(in_ref[f].reshape(cz * cy, nx), chooser)
        for j in range(COLS):
            rows_ref[j] = moved[:, j * xb : (j + 1) * xb]
        for z in range(cz):
            for p in range(ROWS):
                for j in range(COLS):
                    value = rows_ref[j, pl.ds(z * cy + p, yb, stride=ROWS), :]
                    if z == 0:
                        outer_ref[f, 0, p, j] = value
                    elif z == cz - 1:
                        outer_ref[f, 1, p, j] = value
                    else:
                        inner_ref[f, z - 1, p, j] = value
    put_z_edges(outer_ref, z_near_ref, z_far_ref)
    put_y_edges(outer_ref, inner_ref, y_near_ref, y_far_ref)


def onehot_kernel(slot_hbm, onehot_ref, slot_ref, rows_ref, sem):
    cz, cy, nx = slot_ref.shape
    yb, xb = cy // ROWS, nx // COLS
    slots = onehot_ref.shape[1]
    copy = pltpu.make_async_copy(slot_hbm, slot_ref, sem)
    copy.start()
    chooser = jnp.where(
        lax.broadcasted_iota(jnp.int32, (nx, xb), 0) == COLS * lax.broadcasted_iota(jnp.int32, (nx, xb), 1), 1.0, 0.0
    ).astype(jnp.bfloat16)
    slot = lax.broadcasted_iota(jnp.int32, (slots, xb), 0).astype(jnp.float32)
    copy.wait()
    values = slot_ref[...].reshape(cz * cy, nx).astype(jnp.float32).astype(jnp.bfloat16)
    rows_ref[...] = jnp.dot(values, chooser, preferred_element_type=jnp.float32)
    for r in range(cz * yb):
        hit = jnp.where(slot == rows_ref[ROWS * r : ROWS * r + 1, :], 1.0, 0.0).astype(jnp.bfloat16)
        onehot_ref[r // 2, :, (r % 2) * xb : (r % 2 + 1) * xb] = hit


def derived(e, q):
    sin_value, cos_value = sin_cos(q)
    square = e * e
    return cos_value, sin_value, square * cos_value, square * sin_value


def trig_kernel(outer_ref, inner_ref, trig_ref):
    _, cz, rows, cols, _, _ = trig_ref.shape
    for z in range(cz):
        for p in range(rows):
            for j in range(cols):
                e, q = (layer(outer_ref, inner_ref, f, z, p, j) for f in range(2))
                for k, value in enumerate(derived(e, q)):
                    trig_ref[k, z, p, j] = value


def cell_terms(get, rim_ref, z, p, j):
    yb, xb = get(0, z, p, j).shape
    row = lax.broadcasted_iota(jnp.int32, (yb, xb), 0)
    at = z * COLS + j

    def beside(k):
        x_plus = get(k, z, p, j + 1) if j + 1 < COLS else pltpu.roll(get(k, z, p, 0), xb - 1, 1)
        x_minus = get(k, z, p, j - 1) if j > 0 else pltpu.roll(get(k, z, p, COLS - 1), 1, 1)
        if p + 1 < ROWS:
            y_plus = get(k, z, p + 1, j)
        else:
            y_plus = jnp.where(row == yb - 1, rim_ref[1, k, at : at + 1, :], pltpu.roll(get(k, z, 0, j), yb - 1, 0))
        if p > 0:
            y_minus = get(k, z, p - 1, j)
        else:
            y_minus = jnp.where(row == 0, rim_ref[0, k, at : at + 1, :], pltpu.roll(get(k, z, ROWS - 1, j), 1, 0))
        return x_plus, x_minus, y_plus, y_minus, get(k, z + 1, p, j), get(k, z - 1, p, j)

    e_side, q_side = beside(0), beside(1)
    c_sum, s_sum, a_sum, b_sum = (sum(beside(k)) for k in range(2, 6))
    e, q, c, s = (get(k, z, p, j) for k in range(4))
    misfit = 6.0 - c * c_sum - s * s_sum
    torque = c * b_sum - s * a_sum
    grads = [(side[2 * d] - side[2 * d + 1]) * 0.5 for side in (e_side, q_side) for d in range(3)]
    laplace = sum(e_side) - 6.0 * e
    weight = e * misfit
    densities = [weight * g for g in grads[:3]] + [torque, 0.5 + e * e]
    e_local = e + DIFFUSE * laplace + BARRIER * e * (1.0 - e) * (e - 0.5) - PENALTY * weight
    return [e_local, q + TORSION * torque] + grads, densities


def layer_terms(get, rim_ref, z, local_ref, at, sums_ref):
    totals = None
    for p in range(ROWS):
        for j in range(COLS):
            local, densities = cell_terms(get, rim_ref, z, p, j)
            totals = densities if totals is None else [a + b for a, b in zip(totals, densities)]
            for k, value in enumerate(local):
                local_ref[k, at, p, j] = value
    rows = sums_ref.shape[0] // 16
    yb = rows // local_ref.shape[1]
    for k, value in enumerate(totals):
        for part, piece in enumerate(split3(value)):
            start = (part * 5 + k) * rows + at * yb
            sums_ref[start : start + yb, :] = piece.astype(jnp.float32)


def slot_sums(acc, sums_ref, onehot_ref, pairs):
    rows = sums_ref.shape[0] // 16
    for i, pair in enumerate(pairs):
        left = jnp.concatenate(
            [sums_ref[pl.ds(2 * i + h, 16, stride=rows), :] for h in range(2)], axis=1
        ).astype(jnp.bfloat16)
        acc = acc + lax.dot_general(
            left, onehot_ref[pair], (((1,), (1,)), ((), ())), preferred_element_type=jnp.float32
        )
    return acc


def inner_kernel(
    outer_ref, inner_ref, trig_ref, y_near_ref, y_far_ref, onehot_ref,
    rim_ref, local_ref, acc_ref,
    sums_ref,
):
    _, cz, _, _, yb, xb = trig_ref.shape
    n = cz * COLS
    last = lax.axis_size("gy") - 1
    for side in range(2):
        inside = lax.axis_index("gy") != (0, last)[side]
        from_near = odd("gy") if side == 0 else jnp.logical_not(odd("gy"))
        e, q = (
            jnp.where(inside, jnp.where(from_near, y_near_ref[f * n : f * n + n, :], y_far_ref[f * n : f * n + n, :]), 0.0)
            for f in range(2)
        )
        for k, value in enumerate((e, q) + derived(e, q)):
            rim_ref[side, k] = value

    def get(k, z, p, j):
        return layer(outer_ref, inner_ref, k, z, p, j) if k < 2 else trig_ref[k - 2, z, p, j]

    for z in range(1, cz - 1):
        layer_terms(get, rim_ref, z, local_ref, z - 1, sums_ref)
    rows = (cz - 2) * yb
    sums_ref[15 * rows : 16 * rows, :] = jnp.zeros((rows, xb), jnp.float32)
    pairs = [yb // 2 + i for i in range(rows // 2)]
    acc_ref[...] = slot_sums(jnp.zeros(acc_ref.shape, jnp.float32), sums_ref, onehot_ref, pairs)


def outer_kernel(
    outer_ref, inner_ref, trig_ref, rim_ref, z_near_ref, z_far_ref, onehot_ref, acc_ref, ids_ref,
    message_ref, local_ref,
    halo_ref, sums_ref, total_ref,
):
    _, cz, _, _, yb, xb = trig_ref.shape
    for side in range(2):
        from_near = odd("gz") if side == 0 else jnp.logical_not(odd("gz"))
        for p in range(ROWS):
            for j in range(COLS):
                e, q = (jnp.where(from_near, z_near_ref[f, p, j], z_far_ref[f, p, j]) for f in range(2))
                for k, value in enumerate((e, q) + derived(e, q)):
                    halo_ref[side, k, p, j] = value

    def get(k, z, p, j):
        if z < 0 or z == cz:
            return halo_ref[int(z == cz), k, p, j]
        return layer(outer_ref, inner_ref, k, z, p, j) if k < 2 else trig_ref[k - 2, z, p, j]

    for at, z in enumerate((0, cz - 1)):
        layer_terms(get, rim_ref, z, local_ref, at, sums_ref)
    rows = 2 * yb
    sums_ref[15 * rows : 16 * rows, :] = jnp.zeros((rows, xb), jnp.float32)
    half = yb // 2
    pairs = list(range(half)) + list(range((cz - 1) * half, cz * half))
    total_ref[...] = slot_sums(acc_ref[...], sums_ref, onehot_ref, pairs)
    message_ref[0:5, :] = total_ref[0:5, :] + total_ref[5:10, :] + total_ref[10:15, :]
    message_ref[5:6, :] = ids_ref[...].astype(jnp.float32)
    message_ref[6:8, :] = jnp.zeros((2, message_ref.shape[1]), jnp.float32)


def stacked(value):
    return jnp.concatenate([part.astype(jnp.float32) for part in split3(value)], axis=0).astype(jnp.bfloat16)


def unstacked(value):
    return value[0:8] + value[8:16] + value[16:24]


def slot_motion(message_ref, near_ref, far_ref):
    slots = message_ref.shape[1]
    totals = message_ref[...]
    own = jnp.broadcast_to(message_ref[5:6, :], (slots, slots))
    for ref in (near_ref, far_ref):
        other = jnp.transpose(jnp.broadcast_to(ref[5:6, :], (slots, slots)))
        matches = jnp.where(other == own, 1.0, 0.0).astype(jnp.bfloat16)
        totals = totals + unstacked(jnp.dot(stacked(ref[...]), matches, preferred_element_type=jnp.float32))
    inverse = 1.0 / totals[4:5, :]
    return stacked(TRANSLATE * totals * inverse)


def block_motion(velocity, onehot_ref, motion_ref, pairs):
    rows = motion_ref.shape[0] // 8
    xb = motion_ref.shape[1]
    for i, pair in enumerate(pairs):
        moved = unstacked(jnp.dot(velocity, onehot_ref[pair], preferred_element_type=jnp.float32))
        for h in range(2):
            motion_ref[pl.ds(2 * i + h, 8, stride=rows), :] = moved[:, h * xb : (h + 1) * xb]


def advanced(local_ref, motion_ref, at, p, j):
    layers, yb = local_ref.shape[1], local_ref.shape[4]
    rows = layers * yb
    vx, vy, vz, turn = (motion_ref[k * rows + at * yb : k * rows + (at + 1) * yb, :] for k in range(4))
    g = [local_ref[k, at, p, j] for k in range(2, 8)]
    e = local_ref[0, at, p, j] - (vx * g[0] + vy * g[1] + vz * g[2])
    q = local_ref[1, at, p, j] + turn - (vx * g[3] + vy * g[4] + vz * g[5])
    return e, q


def outer_pairs(cz, yb):
    half = yb // 2
    return list(range(half)) + list(range((cz - 1) * half, cz * half))


def inner_pairs(cz, yb):
    return list(range(yb // 2, (cz - 1) * yb // 2))


def advance_outer_kernel(
    message_ref, near_ref, far_ref, onehot_ref, local_ref,
    velocity_ref, outer_ref, z_near_ref, z_far_ref,
    motion_ref,
):
    yb = local_ref.shape[4]
    cz = 2 * onehot_ref.shape[0] // yb
    velocity = slot_motion(message_ref, near_ref, far_ref)
    velocity_ref[...] = velocity
    block_motion(velocity, onehot_ref, motion_ref, outer_pairs(cz, yb))
    for at in range(2):
        for p in range(ROWS):
            for j in range(COLS):
                outer_ref[0, at, p, j], outer_ref[1, at, p, j] = advanced(local_ref, motion_ref, at, p, j)
    put_z_edges(outer_ref, z_near_ref, z_far_ref)


def advance_inner_kernel(
    velocity_ref, onehot_ref, local_ref, outer_ref,
    inner_ref, y_near_ref, y_far_ref,
    motion_ref,
):
    _, layers, _, _, yb, _ = local_ref.shape
    block_motion(velocity_ref[...], onehot_ref, motion_ref, inner_pairs(layers + 2, yb))
    for at in range(layers):
        for p in range(ROWS):
            for j in range(COLS):
                inner_ref[0, at, p, j], inner_ref[1, at, p, j] = advanced(local_ref, motion_ref, at, p, j)
    put_y_edges(outer_ref, inner_ref, y_near_ref, y_far_ref)


def finish_kernel(
    message_ref, near_ref, far_ref, onehot_ref, outer_local_ref, inner_local_ref,
    e_hbm, q_hbm,
    outer_motion_ref, inner_motion_ref, rows_ref, out_ref, sems,
):
    yb, xb = outer_local_ref.shape[4:]
    _, cz, cy, nx = out_ref.shape
    velocity = slot_motion(message_ref, near_ref, far_ref)
    block_motion(velocity, onehot_ref, outer_motion_ref, outer_pairs(cz, yb))
    block_motion(velocity, onehot_ref, inner_motion_ref, inner_pairs(cz, yb))
    for z in range(cz):
        for p in range(ROWS):
            to = pl.ds(z * cy + p, yb, stride=ROWS)
            for j in range(COLS):
                if z in (0, cz - 1):
                    e, q = advanced(outer_local_ref, outer_motion_ref, int(z > 0), p, j)
                else:
                    e, q = advanced(inner_local_ref, inner_motion_ref, z - 1, p, j)
                rows_ref[0, j, to, :] = e
                rows_ref[1, j, to, :] = q
    chooser = x_chooser(nx, xb, back=True)
    copies = []
    for f, ref in enumerate((e_hbm, q_hbm)):
        moved = exact_dot(jnp.concatenate([rows_ref[f, j] for j in range(COLS)], axis=1), chooser)
        out_ref[f] = moved.reshape(out_ref.shape[1:])
        copies.append(pltpu.make_async_copy(out_ref.at[f], ref, sems.at[f]))
        copies[f].start()
    for copy in copies:
        copy.wait()


VMEM = pl.BlockSpec(memory_space=pltpu.VMEM)
HBM = pl.BlockSpec(memory_space=pltpu.HBM)


def call(kernel, name, outs, scratch=(), cycles=1000, in_spec=VMEM, out_spec=VMEM):
    def run(*args):
        return pl.pallas_call(
            kernel,
            name=name,
            in_specs=[in_spec] * len(args),
            out_specs=[out_spec] * len(outs),
            out_shape=[jax.ShapeDtypeStruct(shape, dtype) for shape, dtype in outs],
            scratch_shapes=list(scratch),
            compiler_params=pltpu.CompilerParams(vmem_limit_bytes=24 * 1024 * 1024),
            cost_estimate=pl.CostEstimate(flops=cycles * 4096, bytes_accessed=cycles * 1024, transcendentals=0),
        )(*args)

    return run


def swap(array, axis, far):
    size = lax.axis_size(axis)
    pairs = [(i, (((i + 1) ^ 1) - 1) % size if far else i ^ 1) for i in range(size)]
    return lax.ppermute(array, axis, pairs)


def both(near, far, axis):
    far = swap(far, axis, True)
    return swap(near, axis, False), far


def shards(order_param, orientation, cell_slot, tile_grains):
    cz, cy, nx = order_param.shape
    slots = tile_grains.shape[-1]
    yb, xb = cy // ROWS, nx // COLS
    rows = cz * yb
    f32, bf16 = jnp.float32, jnp.bfloat16
    ids = tile_grains.reshape(1, slots)
    block = (ROWS, COLS, yb, xb)
    outer_out, inner_out = ((2, 2) + block, f32), ((2, cz - 2) + block, f32)
    z_out, y_out = [((2,) + block, f32)] * 2, [((2 * cz * COLS, xb), f32)] * 2
    outer_motion = pltpu.VMEM((8 * 2 * yb, xb), f32)
    inner_motion = pltpu.VMEM((8 * (cz - 2) * yb, xb), f32)
    outer_sums = pltpu.VMEM((16 * 2 * yb, xb), f32)
    inner_sums = pltpu.VMEM((16 * (cz - 2) * yb, xb), f32)
    acc = pltpu.VMEM((16, slots), f32)
    tile2 = pltpu.VMEM((2, cz, cy, nx), f32)
    prepare = call(
        prepare_kernel, "prepare", [outer_out, inner_out] + z_out + y_out,
        [tile2, pltpu.VMEM((COLS, cz * cy, xb), f32), pltpu.SemaphoreType.DMA((2,))], in_spec=HBM,
    )
    onehots = call(
        onehot_kernel, "onehots", [((rows // 2, slots, 2 * xb), bf16)],
        [pltpu.VMEM((cz, cy, nx), jnp.int32), pltpu.VMEM((cz * cy, xb), f32), pltpu.SemaphoreType.DMA(())], in_spec=HBM,
    )
    trigs = call(trig_kernel, "trigs", [((4, cz) + block, f32)])
    inner_terms = call(
        inner_kernel, "inner_terms",
        [((2, 6, cz * COLS, xb), f32), ((8, cz - 2) + block, f32), ((16, slots), f32)], [inner_sums],
    )
    outer_terms = call(
        outer_kernel, "outer_terms", [((8, slots), f32), ((8, 2) + block, f32)],
        [pltpu.VMEM((2, 6) + block, f32), outer_sums, acc],
    )
    advance_outer = call(
        advance_outer_kernel, "advance_outer", [((24, slots), bf16), outer_out] + z_out, [outer_motion]
    )
    advance_inner = call(advance_inner_kernel, "advance_inner", [inner_out] + y_out, [inner_motion])
    finish = call(
        finish_kernel, "finish", [((cz, cy, nx), f32)] * 2,
        [outer_motion, inner_motion, pltpu.VMEM((2, COLS, cz * cy, xb), f32), tile2, pltpu.SemaphoreType.DMA((2,))],
        out_spec=HBM,
    )

    outer, inner, z_near, z_far, y_near, y_far = prepare(order_param, orientation)
    for step in range(STEPS):
        z_near, z_far = both(z_near, z_far, "gz")
        if step > 0:
            inner, y_near, y_far = advance_inner(velocity, onehot, inner_local, outer)
        y_near, y_far = both(y_near, y_far, "gy")
        if step == 0:
            (onehot,) = onehots(cell_slot)
        (trig,) = trigs(outer, inner)
        rim, inner_local, sums = inner_terms(outer, inner, trig, y_near, y_far, onehot)
        message, outer_local = outer_terms(outer, inner, trig, rim, z_near, z_far, onehot, sums, ids)
        near, far = both(message, message, "gz")
        if step < STEPS - 1:
            velocity, outer, z_near, z_far = advance_outer(message, near, far, onehot, outer_local)
    return tuple(finish(message, near, far, onehot, outer_local, inner_local))


def solution(mesh):
    spec = P("gz", "gy", None)
    return jax.shard_map(shards, mesh=mesh, in_specs=(spec,) * 4, out_specs=(spec,) * 2, check_vma=False)
```

```python
import functools

import jax
import jax.numpy as jnp
from jax import lax
from jax.experimental import pallas as pl
from jax.experimental.pallas import tpu as pltpu
from jax.sharding import PartitionSpec as P

STEPS = 3

DIFFUSE = 0.1
BARRIER = 0.5
PENALTY = 0.05
TORSION = 0.1
TRANSLATE = 2.0
ROTATE = 2.0

ROWS = 2
COLS = 4


def split3(value):
    high = value.astype(jnp.bfloat16)
    rest = value - high.astype(jnp.float32)
    middle = rest.astype(jnp.bfloat16)
    low = (rest - middle.astype(jnp.float32)).astype(jnp.bfloat16)
    return high, middle, low


def exact_dot(value, chooser):
    rows = value.shape[0]
    parts = jnp.dot(jnp.concatenate(split3(value), axis=0), chooser, preferred_element_type=jnp.float32)
    return parts[:rows] + parts[rows : 2 * rows] + parts[2 * rows :]


def sin_cos(angle):
    turns = jnp.floor(angle * 0.6366197723675814 + 0.5)
    rest = angle - turns * 1.5703125
    rest = rest - turns * 4.837512969970703125e-4
    rest = rest - turns * 7.54978995489188216e-8
    square = rest * rest
    sine = ((-1.9515295891e-4 * square + 8.3321608736e-3) * square - 1.6666654611e-1) * square * rest + rest
    cosine = ((2.443315711809948e-5 * square - 1.388731625493765e-3) * square + 4.166664568298827e-2) * square * square
    cosine = cosine - 0.5 * square + 1.0
    quarter = turns.astype(jnp.int32)
    odd = (quarter & 1) == 1
    sin_value = jnp.where(odd, cosine, sine)
    cos_value = jnp.where(odd, sine, cosine)
    sin_value = jnp.where((quarter & 2) == 2, -sin_value, sin_value)
    cos_value = jnp.where(((quarter + 1) & 2) == 2, -cos_value, cos_value)
    return sin_value, cos_value


def is_odd(axis):
    return lax.axis_index(axis) & 1


def place(layer, cz):
    odd = is_odd("gz")
    if layer == 0:
        return (1 - odd) * (cz - 1)
    if layer == 1:
        return odd * (cz - 1)
    return layer - 1


def facing(layer, layers):
    odd = is_odd("gz")
    return ((1 - odd) if layer == 0 else odd) * (layers - 1)


def upward(layer):
    half = 0.5 - is_odd("gz").astype(jnp.float32)
    return half if layer == 0 else -half


def tile(f, p, j):
    return (f * ROWS + p) * COLS + j


def put_y_edges(near_ref, far_ref, inner_ref, y_near_ref, y_far_ref):
    layers, yb = inner_ref.shape[1], inner_ref.shape[4]
    cz = layers + 2
    first_to_near = is_odd("gy") == 1
    for f in range(2):
        for layer in range(cz):
            for j in range(COLS):
                at = (f * cz + layer) * COLS + j
                if layer < 2:
                    ref = (near_ref, far_ref)[layer]
                    first, last = ref[tile(f, 0, j), 0:1], ref[tile(f, ROWS - 1, j), yb - 1 : yb]
                else:
                    first = inner_ref[f, layer - 2, 0, j, 0:1]
                    last = inner_ref[f, layer - 2, ROWS - 1, j, yb - 1 : yb]
                y_near_ref[at : at + 1, :] = jnp.where(first_to_near, first, last)
                y_far_ref[at : at + 1, :] = jnp.where(first_to_near, last, first)


def x_chooser(nx, xb, back=False):
    first = lax.broadcasted_iota(jnp.int32, (nx, nx), 1 if back else 0)
    second = lax.broadcasted_iota(jnp.int32, (nx, nx), 0 if back else 1)
    return jnp.where(first == COLS * (second % xb) + second // xb, 1.0, 0.0).astype(jnp.bfloat16)


def spread(in_ref, chooser, rows_ref, put):
    _, layers, cy, nx = in_ref.shape
    yb, xb = cy // ROWS, nx // COLS
    moved = exact_dot(in_ref[...].reshape(2 * layers * cy, nx), chooser)
    for j in range(COLS):
        rows_ref[j] = moved[:, j * xb : (j + 1) * xb]
    for f in range(2):
        for at in range(layers):
            for p in range(ROWS):
                for j in range(COLS):
                    start = (f * layers + at) * cy + p
                    put(f, at, p, j, rows_ref[j, pl.ds(start, yb, stride=ROWS), :])


def prepare_outer_kernel(
    e_hbm, q_hbm, slot_hbm, ids_hbm,
    near_ref, far_ref, raw_ref, slot_ref, ids_ref,
    in_ref, rows_ref, sems, raw_sems,
):
    cz = e_hbm.shape[0]
    _, _, cy, nx = in_ref.shape
    yb, xb = cy // ROWS, nx // COLS
    copies = [
        pltpu.make_async_copy(ref.at[place(at, cz)], in_ref.at[f, at], sems.at[f, at])
        for f, ref in enumerate((e_hbm, q_hbm))
        for at in range(2)
    ]
    copies.append(pltpu.make_async_copy(ids_hbm, ids_ref, raw_sems.at[0]))
    later = [
        pltpu.make_async_copy(e_hbm.at[1 : cz - 1], raw_ref.at[0], raw_sems.at[1]),
        pltpu.make_async_copy(q_hbm.at[1 : cz - 1], raw_ref.at[1], raw_sems.at[2]),
        pltpu.make_async_copy(slot_hbm, slot_ref, raw_sems.at[3]),
    ]
    for copy in copies + later:
        copy.start()
    chooser = x_chooser(nx, xb)
    for copy in copies:
        copy.wait()
    for ref in (near_ref, far_ref):
        ref[2 * ROWS * COLS] = jnp.zeros((yb, xb), jnp.float32)
        for half in range(ids_ref.shape[1] // xb):
            ref[2 * ROWS * COLS, half : half + 1, :] = ids_ref[:, half * xb : (half + 1) * xb].astype(jnp.float32)

    def put(f, at, p, j, value):
        (near_ref, far_ref)[at][tile(f, p, j)] = value

    spread(in_ref, chooser, rows_ref, put)
    for copy in later:
        copy.wait()


def prepare_inner_kernel(
    raw_ref, slot_ref, near_ref, far_ref,
    inner_ref, y_near_ref, y_far_ref, block_ref,
    rows_ref, slot_rows_ref,
):
    _, layers, cy, nx = raw_ref.shape
    cz = layers + 2
    yb, xb = cy // ROWS, nx // COLS
    chooser = x_chooser(nx, xb)

    def put(f, at, p, j, value):
        inner_ref[f, at, p, j] = value

    spread(raw_ref, chooser, rows_ref, put)
    put_y_edges(near_ref, far_ref, inner_ref, y_near_ref, y_far_ref)
    values = jnp.concatenate([slot_ref[place(layer, cz)] for layer in range(cz)], axis=0)
    values = values.astype(jnp.float32).astype(jnp.bfloat16)
    slot_rows_ref[...] = jnp.dot(values, chooser[:, :xb], preferred_element_type=jnp.float32)
    block_ref[...] = slot_rows_ref[pl.ds(0, cz * yb, stride=ROWS), :]


def onehot_kernel(block_ref, onehot_ref):
    rows, xb = block_ref.shape
    slots = onehot_ref.shape[1]
    slot = lax.broadcasted_iota(jnp.int32, (slots, xb), 0).astype(jnp.float32)
    for r in range(rows):
        hit = jnp.where(slot == block_ref[r : r + 1, :], 1.0, 0.0).astype(jnp.bfloat16)
        onehot_ref[r // 2, :, (r % 2) * xb : (r % 2 + 1) * xb] = hit


def derived(e, q):
    sin_value, cos_value = sin_cos(q)
    square = e * e
    return cos_value, sin_value, square * cos_value, square * sin_value


def trig_kernel(near_ref, far_ref, inner_ref, trig_ref):
    cz = trig_ref.shape[1]
    for layer in range(cz):
        for p in range(ROWS):
            for j in range(COLS):
                if layer < 2:
                    e, q = ((near_ref, far_ref)[layer][tile(f, p, j)] for f in range(2))
                else:
                    e, q = (inner_ref[f, layer - 2, p, j] for f in range(2))
                for k, value in enumerate(derived(e, q)):
                    trig_ref[k, layer, p, j] = value


def beside(get, up, down, rim_ref, layer, k, p, j):
    here = get(k, p, j)
    yb, xb = here.shape
    row = lax.broadcasted_iota(jnp.int32, (yb, xb), 0)
    at = layer * COLS + j
    x_plus = get(k, p, j + 1) if j + 1 < COLS else pltpu.roll(get(k, p, 0), xb - 1, 1)
    x_minus = get(k, p, j - 1) if j > 0 else pltpu.roll(get(k, p, COLS - 1), 1, 1)
    if p + 1 < ROWS:
        y_plus = get(k, p + 1, j)
    else:
        y_plus = jnp.where(row == yb - 1, rim_ref[1, k, at : at + 1, :], pltpu.roll(get(k, 0, j), yb - 1, 0))
    if p > 0:
        y_minus = get(k, p - 1, j)
    else:
        y_minus = jnp.where(row == 0, rim_ref[0, k, at : at + 1, :], pltpu.roll(get(k, ROWS - 1, j), 1, 0))
    return x_plus, x_minus, y_plus, y_minus, up(k, p, j), down(k, p, j)


def gradients(side, z_half):
    halves = (0.5, 0.5, z_half)
    return [(side[2 * d] - side[2 * d + 1]) * halves[d] for d in range(3)]


def cell_densities(get, up, down, rim_ref, layer, z_half, p, j):
    sides = [beside(get, up, down, rim_ref, layer, k, p, j) for k in (0, 2, 3, 4, 5)]
    e, c, s = get(0, p, j), get(2, p, j), get(3, p, j)
    c_sum, s_sum, a_sum, b_sum = (sum(side) for side in sides[1:])
    misfit = 6.0 - c * c_sum - s * s_sum
    torque = c * b_sum - s * a_sum
    weight = e * misfit
    grads = gradients(sides[0], z_half)
    return [weight * g for g in grads] + [torque, 0.5 + e * e], weight, torque


def cell_locals(get, up, down, rim_ref, layer, z_half, p, j, weight, torque):
    e_side, q_side = (beside(get, up, down, rim_ref, layer, k, p, j) for k in range(2))
    e, q = get(0, p, j), get(1, p, j)
    laplace = sum(e_side) - 6.0 * e
    e_local = e + DIFFUSE * laplace + BARRIER * e * (1.0 - e) * (e - 0.5) - PENALTY * weight
    return [e_local, q + TORSION * torque] + gradients(e_side, z_half) + gradients(q_side, z_half)


def put_sums(totals, at, yb, sums_ref):
    rows = sums_ref.shape[0] // 16
    for k, value in enumerate(totals):
        for part, piece in enumerate(split3(value)):
            start = (part * 5 + k) * rows + at * yb
            sums_ref[start : start + yb, :] = piece.astype(jnp.float32)


def slot_sums(sums_ref, onehot_ref, first_pair):
    rows = sums_ref.shape[0] // 16
    sums_ref[15 * rows : 16 * rows, :] = jnp.zeros((rows, sums_ref.shape[1]), jnp.float32)
    acc = jnp.zeros((16, onehot_ref.shape[1]), jnp.float32)
    for i in range(rows // 2):
        left = jnp.concatenate(
            [sums_ref[pl.ds(2 * i + h, 16, stride=rows), :] for h in range(2)], axis=1
        ).astype(jnp.bfloat16)
        acc = acc + lax.dot_general(
            left, onehot_ref[first_pair + i], (((1,), (1,)), ((), ())), preferred_element_type=jnp.float32
        )
    return acc


def inner_kernel(
    near_ref, far_ref, inner_ref, trig_ref, y_near_ref, y_far_ref, onehot_ref,
    rim_ref, local_ref, acc_ref,
    sums_ref,
):
    _, cz, _, _, yb, xb = trig_ref.shape
    n = cz * COLS
    last = lax.axis_size("gy") - 1
    for side in range(2):
        inside = lax.axis_index("gy") != (0, last)[side]
        from_near = is_odd("gy") == 1 - side
        e, q = (
            jnp.where(
                inside, jnp.where(from_near, y_near_ref[f * n : f * n + n, :], y_far_ref[f * n : f * n + n, :]), 0.0
            )
            for f in range(2)
        )
        for k, value in enumerate((e, q) + derived(e, q)):
            rim_ref[side, k] = value

    def inner(at, k, p, j):
        return inner_ref[k, at, p, j] if k < 2 else trig_ref[k - 2, at + 2, p, j]

    def outer(top, k, p, j):
        is_near = is_odd("gz") == (0 if top else 1)
        if k < 2:
            return jnp.where(is_near, near_ref[tile(k, p, j)], far_ref[tile(k, p, j)])
        return trig_ref[k - 2, jnp.where(is_near, 0, 1), p, j]

    for at in range(cz - 2):
        get = functools.partial(inner, at)
        up = functools.partial(inner, at + 1) if at + 1 < cz - 2 else functools.partial(outer, True)
        down = functools.partial(inner, at - 1) if at > 0 else functools.partial(outer, False)
        totals = None
        for p in range(ROWS):
            for j in range(COLS):
                densities, weight, torque = cell_densities(get, up, down, rim_ref, at + 2, 0.5, p, j)
                totals = densities if totals is None else [a + b for a, b in zip(totals, densities)]
                local = cell_locals(get, up, down, rim_ref, at + 2, 0.5, p, j, weight, torque)
                for k, value in enumerate(local):
                    local_ref[k, at, p, j] = value
        put_sums(totals, at, yb, sums_ref)
    acc_ref[...] = slot_sums(sums_ref, onehot_ref, yb)


def outer_getters(layer, own_ref, inner_ref, trig_ref, halo):
    beside_at = facing(layer, inner_ref.shape[1])

    def get(k, p, j):
        return own_ref[tile(k, p, j)] if k < 2 else trig_ref[k - 2, layer, p, j]

    def inward(k, p, j):
        return inner_ref[k, beside_at, p, j] if k < 2 else trig_ref[k - 2, beside_at + 2, p, j]

    return get, halo, inward


def outer_densities(layer, own_ref, inner_ref, trig_ref, rim_ref, halo_ref, onehot_ref, mixed_ref, trig_halo_ref, sums_ref):
    yb = trig_ref.shape[4]
    for p in range(ROWS):
        for j in range(COLS):
            for k, value in enumerate(derived(*(halo_ref[tile(f, p, j)] for f in range(2)))):
                trig_halo_ref[k, p, j] = value

    def halo(k, p, j):
        return halo_ref[tile(k, p, j)] if k < 2 else trig_halo_ref[k - 2, p, j]

    get, out, inward = outer_getters(layer, own_ref, inner_ref, trig_ref, halo)
    z_half = upward(layer)
    totals = None
    for p in range(ROWS):
        for j in range(COLS):
            densities, weight, torque = cell_densities(get, out, inward, rim_ref, layer, z_half, p, j)
            totals = densities if totals is None else [a + b for a, b in zip(totals, densities)]
            mixed_ref[0, p, j] = weight
            mixed_ref[1, p, j] = torque
    put_sums(totals, 0, yb, sums_ref)
    return slot_sums(sums_ref, onehot_ref, layer * yb // 2)


def near_kernel(
    near_ref, inner_ref, trig_ref, rim_ref, halo_ref, onehot_ref, before_ref,
    mixed_ref, acc_ref,
    trig_halo_ref, sums_ref,
):
    acc_ref[...] = before_ref[...] + outer_densities(
        0, near_ref, inner_ref, trig_ref, rim_ref, halo_ref, onehot_ref, mixed_ref, trig_halo_ref, sums_ref
    )


def far_kernel(
    far_ref, inner_ref, trig_ref, rim_ref, halo_ref, onehot_ref, before_ref,
    mixed_ref, message_ref,
    trig_halo_ref, sums_ref, acc_ref,
):
    acc_ref[...] = before_ref[...] + outer_densities(
        1, far_ref, inner_ref, trig_ref, rim_ref, halo_ref, onehot_ref, mixed_ref, trig_halo_ref, sums_ref
    )
    message_ref[0:5, :] = acc_ref[0:5, :] + acc_ref[5:10, :] + acc_ref[10:15, :]
    message_ref[5:8, :] = jnp.zeros((3, message_ref.shape[1]), jnp.float32)


def outer_local_kernel(
    near_ref, far_ref, inner_ref, trig_ref, rim_ref, near_halo_ref, far_halo_ref, near_mixed_ref, far_mixed_ref, local_ref
):
    for layer in range(2):
        halo_ref = (near_halo_ref, far_halo_ref)[layer]
        mixed_ref = (near_mixed_ref, far_mixed_ref)[layer]

        def halo(k, p, j, halo_ref=halo_ref):
            return halo_ref[tile(k, p, j)]

        get, out, inward = outer_getters(layer, (near_ref, far_ref)[layer], inner_ref, trig_ref, halo)
        z_half = upward(layer)
        for p in range(ROWS):
            for j in range(COLS):
                local = cell_locals(
                    get, out, inward, rim_ref, layer, z_half, p, j, mixed_ref[0, p, j], mixed_ref[1, p, j]
                )
                for k, value in enumerate(local):
                    local_ref[k, layer, p, j] = value


def match_kernel(ids_ref, near_halo_ref, far_halo_ref, match_ref):
    slots = ids_ref.shape[1]
    xb = near_halo_ref.shape[2]
    own = jnp.broadcast_to(ids_ref[...].astype(jnp.float32), (xb, slots))
    for side, ref in enumerate((near_halo_ref, far_halo_ref)):
        for half in range(slots // xb):
            line = ref[2 * ROWS * COLS, half : half + 1, :]
            other = jnp.transpose(jnp.broadcast_to(line, (xb, xb)))
            other = jnp.concatenate([other] * (slots // xb), axis=1)
            start = side * slots + half * xb
            match_ref[start : start + xb, :] = jnp.where(other == own, 1.0, 0.0).astype(jnp.bfloat16)


def stacked(value):
    return jnp.concatenate([part.astype(jnp.float32) for part in split3(value)], axis=0).astype(jnp.bfloat16)


def unstacked(value):
    return value[0:8] + value[8:16] + value[16:24]


def slot_motion(message_ref, near_ref, far_ref, match_ref):
    others = jnp.concatenate([stacked(near_ref[...]), stacked(far_ref[...])], axis=1)
    totals = message_ref[...] + unstacked(jnp.dot(others, match_ref[...], preferred_element_type=jnp.float32))
    inverse = 1.0 / totals[4:5, :]
    return stacked(TRANSLATE * totals * inverse)


def block_motion(velocity, onehot_ref, motion_ref, first_pair):
    rows = motion_ref.shape[0] // 8
    xb = motion_ref.shape[1]
    for i in range(rows // 2):
        moved = unstacked(jnp.dot(velocity, onehot_ref[first_pair + i], preferred_element_type=jnp.float32))
        for h in range(2):
            motion_ref[pl.ds(2 * i + h, 8, stride=rows), :] = moved[:, h * xb : (h + 1) * xb]


def advanced(local_ref, motion_ref, at, p, j):
    layers, yb = local_ref.shape[1], local_ref.shape[4]
    rows = layers * yb
    vx, vy, vz, turn = (motion_ref[k * rows + at * yb : k * rows + (at + 1) * yb, :] for k in range(4))
    g = [local_ref[k, at, p, j] for k in range(2, 8)]
    e = local_ref[0, at, p, j] - (vx * g[0] + vy * g[1] + vz * g[2])
    q = local_ref[1, at, p, j] + turn - (vx * g[3] + vy * g[4] + vz * g[5])
    return e, q


def advance_outer_kernel(
    message_ref, near_message_ref, far_message_ref, match_ref, onehot_ref, local_ref,
    velocity_ref, near_ref, far_ref,
    motion_ref,
):
    velocity = slot_motion(message_ref, near_message_ref, far_message_ref, match_ref)
    velocity_ref[...] = velocity
    block_motion(velocity, onehot_ref, motion_ref, 0)
    for layer, ref in enumerate((near_ref, far_ref)):
        for p in range(ROWS):
            for j in range(COLS):
                ref[tile(0, p, j)], ref[tile(1, p, j)] = advanced(local_ref, motion_ref, layer, p, j)


def advance_inner_kernel(
    velocity_ref, onehot_ref, local_ref, near_ref, far_ref,
    inner_ref, y_near_ref, y_far_ref,
    motion_ref,
):
    layers, yb = local_ref.shape[1], local_ref.shape[4]
    block_motion(velocity_ref[...], onehot_ref, motion_ref, yb)
    for at in range(layers):
        for p in range(ROWS):
            for j in range(COLS):
                inner_ref[0, at, p, j], inner_ref[1, at, p, j] = advanced(local_ref, motion_ref, at, p, j)
    put_y_edges(near_ref, far_ref, inner_ref, y_near_ref, y_far_ref)


def finish_kernel(
    message_ref, near_message_ref, far_message_ref, match_ref, onehot_ref, outer_local_ref, inner_local_ref,
    e_hbm, q_hbm,
    motion_ref, rows_ref, out_ref, sems,
):
    yb, xb = outer_local_ref.shape[4:]
    _, cz, cy, nx = out_ref.shape
    velocity = slot_motion(message_ref, near_message_ref, far_message_ref, match_ref)
    chooser = x_chooser(nx, xb, back=True)
    copies = []
    for part, local_ref in enumerate((outer_local_ref, inner_local_ref)):
        layers = local_ref.shape[1]
        block_motion(velocity, onehot_ref, motion_ref, part * yb)
        for at in range(layers):
            for p in range(ROWS):
                to = pl.ds(at * cy + p, yb, stride=ROWS)
                for j in range(COLS):
                    e, q = advanced(local_ref, motion_ref, at, p, j)
                    rows_ref[0, j, to, :] = e
                    rows_ref[1, j, to, :] = q
        moved = exact_dot(
            jnp.concatenate(
                [jnp.concatenate([rows_ref[f, j] for j in range(COLS)], axis=1) for f in range(2)], axis=0
            ),
            chooser,
        )
        for f, ref in enumerate((e_hbm, q_hbm)):
            for at in range(layers):
                layer = 2 * part + at
                start = (f * layers + at) * cy
                out_ref[f, layer] = moved[start : start + cy]
                copies.append(
                    pltpu.make_async_copy(out_ref.at[f, layer], ref.at[place(layer, cz)], sems.at[f, layer])
                )
                copies[-1].start()
    for copy in copies:
        copy.wait()


VMEM = pl.BlockSpec(memory_space=pltpu.VMEM)
HBM = pl.BlockSpec(memory_space=pltpu.HBM)
MIB = 1024 * 1024


def call(kernel, name, outs, scratch=(), hbm_in=0, hbm_out=False, limit=24):
    def run(*args):
        return pl.pallas_call(
            kernel,
            name=name,
            in_specs=[HBM] * hbm_in + [VMEM] * (len(args) - hbm_in),
            out_specs=[HBM if hbm_out else VMEM] * len(outs),
            out_shape=[jax.ShapeDtypeStruct(shape, dtype) for shape, dtype in outs],
            scratch_shapes=list(scratch),
            compiler_params=pltpu.CompilerParams(vmem_limit_bytes=limit * MIB),
            cost_estimate=pl.CostEstimate(flops=4 * MIB, bytes_accessed=MIB, transcendentals=0),
        )(*args)

    return run


def swap(array, axis, far):
    size = lax.axis_size(axis)
    pairs = [(i, (((i + 1) ^ 1) - 1) % size if far else i ^ 1) for i in range(size)]
    return lax.ppermute(array, axis, pairs)


def both(near, far, axis):
    far = swap(far, axis, True)
    return swap(near, axis, False), far


def shards(order_param, orientation, cell_slot, tile_grains):
    cz, cy, nx = order_param.shape
    slots = tile_grains.shape[-1]
    yb, xb = cy // ROWS, nx // COLS
    rows = cz * yb
    f32, bf16 = jnp.float32, jnp.bfloat16
    block = (ROWS, COLS, yb, xb)
    side_out = ((2 * ROWS * COLS, yb, xb), f32)
    first_side_out = ((2 * ROWS * COLS + 1, yb, xb), f32)
    inner_out = ((2, cz - 2) + block, f32)
    y_out = [((2 * cz * COLS, xb), f32)] * 2
    acc_out = ((16, slots), f32)
    mixed_out = ((2,) + block, f32)
    outer_motion = pltpu.VMEM((8 * 2 * yb, xb), f32)
    inner_motion = pltpu.VMEM((8 * (cz - 2) * yb, xb), f32)
    layer_scratch = [pltpu.VMEM((4,) + block, f32), pltpu.VMEM((16 * yb, xb), f32)]
    dma = pltpu.SemaphoreType.DMA
    prepare_outer = call(
        prepare_outer_kernel, "prepare_outer",
        [
            first_side_out, first_side_out, ((2, cz - 2, cy, nx), f32),
            ((cz, cy, nx), jnp.int32), ((1, slots), jnp.int32),
        ],
        [pltpu.VMEM((2, 2, cy, nx), f32), pltpu.VMEM((COLS, 4 * cy, xb), f32), dma((2, 2)), dma((4,))],
        hbm_in=4,
    )
    prepare_inner = call(
        prepare_inner_kernel, "prepare_inner", [inner_out] + y_out + [((rows, xb), f32)],
        [pltpu.VMEM((COLS, 2 * (cz - 2) * cy, xb), f32), pltpu.VMEM((cz * cy, xb), f32)],
    )
    onehots = call(onehot_kernel, "onehots", [((rows // 2, slots, 2 * xb), bf16)])
    trigs = call(trig_kernel, "trigs", [((4, cz) + block, f32)])
    inner_terms = call(
        inner_kernel, "inner_terms", [((2, 6, cz * COLS, xb), f32), ((8, cz - 2) + block, f32), acc_out],
        [pltpu.VMEM((16 * (cz - 2) * yb, xb), f32)],
    )
    near_terms = call(near_kernel, "near_terms", [mixed_out, acc_out], layer_scratch)
    far_terms = call(
        far_kernel, "far_terms", [mixed_out, ((8, slots), f32)], layer_scratch + [pltpu.VMEM((16, slots), f32)]
    )
    outer_locals = call(outer_local_kernel, "outer_locals", [((8, 2) + block, f32)])
    matches = call(match_kernel, "matches", [((2 * slots, slots), bf16)])
    advance_outer = call(
        advance_outer_kernel, "advance_outer", [((24, slots), bf16), side_out, side_out], [outer_motion]
    )
    advance_inner = call(advance_inner_kernel, "advance_inner", [inner_out] + y_out, [inner_motion])
    finish = call(
        finish_kernel, "finish", [((cz, cy, nx), f32)] * 2,
        [
            outer_motion, pltpu.VMEM((2, COLS, 2 * cy, xb), f32), pltpu.VMEM((2, cz, cy, nx), f32), dma((2, cz)),
        ],
        hbm_out=True,
    )

    inputs = (order_param, orientation, cell_slot, tile_grains.reshape(1, slots))
    near, far, raw, raw_slots, ids = prepare_outer(
        *(pltpu.with_memory_space_constraint(array, pltpu.HBM) for array in inputs)
    )
    for step in range(STEPS):
        near_halo, far_halo = both(near, far, "gz")
        if step == 0:
            inner, y_near, y_far, blocks = prepare_inner(raw, raw_slots, near, far)
        else:
            inner, y_near, y_far = advance_inner(velocity, onehot, inner_local, near, far)
        y_near, y_far = both(y_near, y_far, "gy")
        if step == 0:
            (onehot,) = onehots(blocks)
        (trig,) = trigs(near, far, inner)
        rim, inner_local, acc = inner_terms(near, far, inner, trig, y_near, y_far, onehot)
        near_mixed, acc = near_terms(near, inner, trig, rim, near_halo, onehot, acc)
        far_mixed, message = far_terms(far, inner, trig, rim, far_halo, onehot, acc)
        near_message, far_message = both(message, message, "gz")
        if step == 0:
            (match,) = matches(ids, near_halo, far_halo)
        (outer_local,) = outer_locals(near, far, inner, trig, rim, near_halo, far_halo, near_mixed, far_mixed)
        if step < STEPS - 1:
            velocity, near, far = advance_outer(message, near_message, far_message, match, onehot, outer_local)
    return tuple(finish(message, near_message, far_message, match, onehot, outer_local, inner_local))


def solution(mesh):
    spec = P("gz", "gy", None)
    return jax.shard_map(shards, mesh=mesh, in_specs=(spec,) * 4, out_specs=(spec,) * 2, check_vma=False)
```

```python
import functools

import jax
import jax.numpy as jnp
from jax import lax
from jax.experimental import pallas as pl
from jax.experimental.pallas import tpu as pltpu
from jax.sharding import PartitionSpec as P

STEPS = 3

DIFFUSE = 0.1
BARRIER = 0.5
PENALTY = 0.05
TORSION = 0.1
TRANSLATE = 2.0
ROTATE = 2.0

ROWS = 2
COLS = 4


def split3(value):
    high = value.astype(jnp.bfloat16)
    rest = value - high.astype(jnp.float32)
    middle = rest.astype(jnp.bfloat16)
    low = (rest - middle.astype(jnp.float32)).astype(jnp.bfloat16)
    return high, middle, low


def exact_dot(value, chooser):
    rows = value.shape[0]
    parts = jnp.dot(jnp.concatenate(split3(value), axis=0), chooser, preferred_element_type=jnp.float32)
    return parts[:rows] + parts[rows : 2 * rows] + parts[2 * rows :]


def sin_cos(angle):
    turns = jnp.floor(angle * 0.6366197723675814 + 0.5)
    rest = angle - turns * 1.5703125
    rest = rest - turns * 4.837512969970703125e-4
    rest = rest - turns * 7.54978995489188216e-8
    square = rest * rest
    sine = ((-1.9515295891e-4 * square + 8.3321608736e-3) * square - 1.6666654611e-1) * square * rest + rest
    cosine = ((2.443315711809948e-5 * square - 1.388731625493765e-3) * square + 4.166664568298827e-2) * square * square
    cosine = cosine - 0.5 * square + 1.0
    quarter = turns.astype(jnp.int32)
    odd = (quarter & 1) == 1
    sin_value = jnp.where(odd, cosine, sine)
    cos_value = jnp.where(odd, sine, cosine)
    sin_value = jnp.where((quarter & 2) == 2, -sin_value, sin_value)
    cos_value = jnp.where(((quarter + 1) & 2) == 2, -cos_value, cos_value)
    return sin_value, cos_value


def is_odd(axis):
    return lax.axis_index(axis) & 1


def place(layer, cz):
    odd = is_odd("gz")
    if layer == 0:
        return (1 - odd) * (cz - 1)
    if layer == 1:
        return odd * (cz - 1)
    return layer - 1


def facing(layer, layers):
    odd = is_odd("gz")
    return ((1 - odd) if layer == 0 else odd) * (layers - 1)


def upward(layer):
    half = 0.5 - is_odd("gz").astype(jnp.float32)
    return half if layer == 0 else -half


def tile(f, p, j):
    return (f * ROWS + p) * COLS + j


def put_y_edges(near_ref, far_ref, inner_ref, y_near_ref, y_far_ref):
    layers, yb = inner_ref.shape[1], inner_ref.shape[4]
    cz = layers + 2
    first_to_near = is_odd("gy") == 1
    for f in range(2):
        for layer in range(cz):
            for j in range(COLS):
                at = (f * cz + layer) * COLS + j
                if layer < 2:
                    ref = (near_ref, far_ref)[layer]
                    first, last = ref[tile(f, 0, j), 0:1], ref[tile(f, ROWS - 1, j), yb - 1 : yb]
                else:
                    first = inner_ref[f, layer - 2, 0, j, 0:1]
                    last = inner_ref[f, layer - 2, ROWS - 1, j, yb - 1 : yb]
                y_near_ref[at : at + 1, :] = jnp.where(first_to_near, first, last)
                y_far_ref[at : at + 1, :] = jnp.where(first_to_near, last, first)


def x_chooser(nx, xb, back=False):
    first = lax.broadcasted_iota(jnp.int32, (nx, nx), 1 if back else 0)
    second = lax.broadcasted_iota(jnp.int32, (nx, nx), 0 if back else 1)
    return jnp.where(first == COLS * (second & (xb - 1)) + (second >> (xb.bit_length() - 1)), 1.0, 0.0).astype(jnp.bfloat16)


def spread(in_ref, chooser, rows_ref, put):
    _, layers, cy, nx = in_ref.shape
    yb, xb = cy // ROWS, nx // COLS
    moved = exact_dot(in_ref[...].reshape(2 * layers * cy, nx), chooser)
    for j in range(COLS):
        rows_ref[j] = moved[:, j * xb : (j + 1) * xb]
    for f in range(2):
        for at in range(layers):
            for p in range(ROWS):
                for j in range(COLS):
                    start = (f * layers + at) * cy + p
                    put(f, at, p, j, rows_ref[j, pl.ds(start, yb, stride=ROWS), :])


def prepare_outer_kernel(
    e_hbm, q_hbm, slot_hbm, ids_hbm,
    near_ref, far_ref, raw_ref, slot_ref, ids_ref,
    in_ref, rows_ref, sems, raw_sems,
):
    cz = e_hbm.shape[0]
    _, _, cy, nx = in_ref.shape
    yb, xb = cy // ROWS, nx // COLS
    copies = [
        pltpu.make_async_copy(ref.at[place(at, cz)], in_ref.at[f, at], sems.at[f, at])
        for f, ref in enumerate((e_hbm, q_hbm))
        for at in range(2)
    ]
    copies.append(pltpu.make_async_copy(ids_hbm, ids_ref, raw_sems.at[0]))
    later = [
        pltpu.make_async_copy(e_hbm.at[1 : cz - 1], raw_ref.at[0], raw_sems.at[1]),
        pltpu.make_async_copy(q_hbm.at[1 : cz - 1], raw_ref.at[1], raw_sems.at[2]),
        pltpu.make_async_copy(slot_hbm, slot_ref, raw_sems.at[3]),
    ]
    for copy in copies + later:
        copy.start()
    chooser = x_chooser(nx, xb)
    for copy in copies:
        copy.wait()
    for ref in (near_ref, far_ref):
        ref[2 * ROWS * COLS] = jnp.zeros((yb, xb), jnp.float32)
        for half in range(ids_ref.shape[1] // xb):
            ref[2 * ROWS * COLS, half : half + 1, :] = ids_ref[:, half * xb : (half + 1) * xb].astype(jnp.float32)

    def put(f, at, p, j, value):
        (near_ref, far_ref)[at][tile(f, p, j)] = value

    spread(in_ref, chooser, rows_ref, put)
    for copy in later:
        copy.wait()


def prepare_inner_kernel(
    raw_ref, slot_ref, near_ref, far_ref,
    inner_ref, y_near_ref, y_far_ref, block_ref,
    rows_ref, slot_rows_ref,
):
    _, layers, cy, nx = raw_ref.shape
    cz = layers + 2
    yb, xb = cy // ROWS, nx // COLS
    chooser = x_chooser(nx, xb)

    def put(f, at, p, j, value):
        inner_ref[f, at, p, j] = value

    spread(raw_ref, chooser, rows_ref, put)
    put_y_edges(near_ref, far_ref, inner_ref, y_near_ref, y_far_ref)
    values = jnp.concatenate([slot_ref[place(layer, cz)] for layer in range(cz)], axis=0)
    values = values.astype(jnp.float32).astype(jnp.bfloat16)
    slot_rows_ref[...] = jnp.dot(values, chooser[:, :xb], preferred_element_type=jnp.float32)
    block_ref[...] = slot_rows_ref[pl.ds(0, cz * yb, stride=ROWS), :]


def onehot_kernel(block_ref, onehot_ref, chooser_ref):
    rows, xb = block_ref.shape
    slots = onehot_ref.shape[1]
    one, zero = jnp.ones((), jnp.bfloat16), jnp.zeros((), jnp.bfloat16)
    down = lax.broadcasted_iota(jnp.int32, (slots, xb), 0).astype(jnp.float32).astype(jnp.bfloat16)
    across = lax.broadcasted_iota(jnp.int32, (xb, xb), 1)
    across = [(across + half * xb).astype(jnp.float32).astype(jnp.bfloat16) for half in range(slots // xb)]
    turned = jnp.transpose(jnp.concatenate([block_ref[...], jnp.zeros((xb - rows, xb), jnp.float32)], axis=0))
    for r in range(rows):
        at = (r % 2) * xb
        line = jnp.broadcast_to(block_ref[r : r + 1, :], (16, xb)).astype(jnp.bfloat16)
        line = jnp.concatenate([line] * (slots // 16), axis=0)
        onehot_ref[r // 2, :, at : at + xb] = jnp.where(down == line, one, zero)
        line = jnp.broadcast_to(turned[:, r : r + 1], (xb, xb)).astype(jnp.bfloat16)
        for half in range(slots // xb):
            chooser_ref[r // 2, at : at + xb, half * xb : (half + 1) * xb] = jnp.where(across[half] == line, one, zero)


def derived(e, q):
    sin_value, cos_value = sin_cos(q)
    square = e * e
    return cos_value, sin_value, square * cos_value, square * sin_value


def trig_kernel(near_ref, far_ref, inner_ref, trig_ref):
    cz = trig_ref.shape[1]
    for layer in range(cz):
        for p in range(ROWS):
            for j in range(COLS):
                if layer < 2:
                    e, q = ((near_ref, far_ref)[layer][tile(f, p, j)] for f in range(2))
                else:
                    e, q = (inner_ref[f, layer - 2, p, j] for f in range(2))
                for k, value in enumerate(derived(e, q)):
                    trig_ref[k, layer, p, j] = value


def beside(get, up, down, rim_ref, layer, k, p, j):
    here = get(k, p, j)
    yb, xb = here.shape
    row = lax.broadcasted_iota(jnp.int32, (yb, xb), 0)
    at = layer * COLS + j
    x_plus = get(k, p, j + 1) if j + 1 < COLS else pltpu.roll(get(k, p, 0), xb - 1, 1)
    x_minus = get(k, p, j - 1) if j > 0 else pltpu.roll(get(k, p, COLS - 1), 1, 1)
    if p + 1 < ROWS:
        y_plus = get(k, p + 1, j)
    else:
        y_plus = jnp.where(row == yb - 1, rim_ref[1, k, at : at + 1, :], pltpu.roll(get(k, 0, j), yb - 1, 0))
    if p > 0:
        y_minus = get(k, p - 1, j)
    else:
        y_minus = jnp.where(row == 0, rim_ref[0, k, at : at + 1, :], pltpu.roll(get(k, ROWS - 1, j), 1, 0))
    return x_plus, x_minus, y_plus, y_minus, up(k, p, j), down(k, p, j)


def gradients(side, z_half):
    halves = (0.5, 0.5, z_half)
    return [(side[2 * d] - side[2 * d + 1]) * halves[d] for d in range(3)]


def cell_densities(get, up, down, rim_ref, layer, z_half, p, j):
    sides = [beside(get, up, down, rim_ref, layer, k, p, j) for k in (0, 2, 3, 4, 5)]
    e, c, s = get(0, p, j), get(2, p, j), get(3, p, j)
    c_sum, s_sum, a_sum, b_sum = (sum(side) for side in sides[1:])
    misfit = 6.0 - c * c_sum - s * s_sum
    torque = c * b_sum - s * a_sum
    weight = e * misfit
    grads = gradients(sides[0], z_half)
    return [weight * g for g in grads] + [torque, 0.5 + e * e], weight, torque


def cell_locals(get, up, down, rim_ref, layer, z_half, p, j, weight, torque):
    e_side, q_side = (beside(get, up, down, rim_ref, layer, k, p, j) for k in range(2))
    e, q = get(0, p, j), get(1, p, j)
    laplace = sum(e_side) - 6.0 * e
    e_local = e + DIFFUSE * laplace + BARRIER * e * (1.0 - e) * (e - 0.5) - PENALTY * weight
    return [e_local, q + TORSION * torque] + gradients(e_side, z_half) + gradients(q_side, z_half)


def put_sums(totals, at, yb, sums_ref):
    rows = sums_ref.shape[0] // 16
    for k, value in enumerate(totals):
        for part, piece in enumerate(split3(value)):
            start = (part * 5 + k) * rows + at * yb
            sums_ref[start : start + yb, :] = piece.astype(jnp.float32)


def slot_sums(sums_ref, chooser_ref, first_pair):
    rows = sums_ref.shape[0] // 16
    sums_ref[15 * rows : 16 * rows, :] = jnp.zeros((rows, sums_ref.shape[1]), jnp.float32)
    acc = jnp.zeros((16, chooser_ref.shape[2]), jnp.float32)
    for i in range(rows // 2):
        left = jnp.concatenate(
            [sums_ref[pl.ds(2 * i + h, 16, stride=rows), :] for h in range(2)], axis=1
        ).astype(jnp.bfloat16)
        acc = acc + jnp.dot(left, chooser_ref[first_pair + i], preferred_element_type=jnp.float32)
    return acc


def inner_kernel(
    near_ref, far_ref, inner_ref, trig_ref, y_near_ref, y_far_ref, chooser_ref,
    rim_ref, local_ref, acc_ref,
    sums_ref,
):
    _, cz, _, _, yb, xb = trig_ref.shape
    n = cz * COLS
    last = lax.axis_size("gy") - 1
    for side in range(2):
        inside = lax.axis_index("gy") != (0, last)[side]
        from_near = is_odd("gy") == 1 - side
        e, q = (
            jnp.where(
                inside, jnp.where(from_near, y_near_ref[f * n : f * n + n, :], y_far_ref[f * n : f * n + n, :]), 0.0
            )
            for f in range(2)
        )
        for k, value in enumerate((e, q) + derived(e, q)):
            rim_ref[side, k] = value

    def inner(at, k, p, j):
        return inner_ref[k, at, p, j] if k < 2 else trig_ref[k - 2, at + 2, p, j]

    def outer(top, k, p, j):
        is_near = is_odd("gz") == (0 if top else 1)
        if k < 2:
            return jnp.where(is_near, near_ref[tile(k, p, j)], far_ref[tile(k, p, j)])
        return trig_ref[k - 2, jnp.where(is_near, 0, 1), p, j]

    for at in range(cz - 2):
        get = functools.partial(inner, at)
        up = functools.partial(inner, at + 1) if at + 1 < cz - 2 else functools.partial(outer, True)
        down = functools.partial(inner, at - 1) if at > 0 else functools.partial(outer, False)
        totals = None
        for p in range(ROWS):
            for j in range(COLS):
                densities, weight, torque = cell_densities(get, up, down, rim_ref, at + 2, 0.5, p, j)
                totals = densities if totals is None else [a + b for a, b in zip(totals, densities)]
                local = cell_locals(get, up, down, rim_ref, at + 2, 0.5, p, j, weight, torque)
                for k, value in enumerate(local):
                    local_ref[k, at, p, j] = value
        put_sums(totals, at, yb, sums_ref)
    acc_ref[...] = slot_sums(sums_ref, chooser_ref, yb)


def outer_getters(layer, own_ref, inner_ref, trig_ref, halo):
    beside_at = facing(layer, inner_ref.shape[1])

    def get(k, p, j):
        return own_ref[tile(k, p, j)] if k < 2 else trig_ref[k - 2, layer, p, j]

    def inward(k, p, j):
        return inner_ref[k, beside_at, p, j] if k < 2 else trig_ref[k - 2, beside_at + 2, p, j]

    return get, halo, inward


def outer_densities(layer, own_ref, inner_ref, trig_ref, rim_ref, halo_ref, chooser_ref, mixed_ref, trig_halo_ref, sums_ref):
    yb = trig_ref.shape[4]
    for p in range(ROWS):
        for j in range(COLS):
            for k, value in enumerate(derived(*(halo_ref[tile(f, p, j)] for f in range(2)))):
                trig_halo_ref[k, p, j] = value

    def halo(k, p, j):
        return halo_ref[tile(k, p, j)] if k < 2 else trig_halo_ref[k - 2, p, j]

    get, out, inward = outer_getters(layer, own_ref, inner_ref, trig_ref, halo)
    z_half = upward(layer)
    totals = None
    for p in range(ROWS):
        for j in range(COLS):
            densities, weight, torque = cell_densities(get, out, inward, rim_ref, layer, z_half, p, j)
            totals = densities if totals is None else [a + b for a, b in zip(totals, densities)]
            mixed_ref[0, p, j] = weight
            mixed_ref[1, p, j] = torque
    put_sums(totals, 0, yb, sums_ref)
    return slot_sums(sums_ref, chooser_ref, layer * yb // 2)


def near_kernel(
    near_ref, inner_ref, trig_ref, rim_ref, halo_ref, chooser_ref, before_ref,
    mixed_ref, acc_ref,
    trig_halo_ref, sums_ref,
):
    acc_ref[...] = before_ref[...] + outer_densities(
        0, near_ref, inner_ref, trig_ref, rim_ref, halo_ref, chooser_ref, mixed_ref, trig_halo_ref, sums_ref
    )


def far_kernel(
    far_ref, inner_ref, trig_ref, rim_ref, halo_ref, chooser_ref, before_ref,
    mixed_ref, message_ref,
    trig_halo_ref, sums_ref, acc_ref,
):
    acc_ref[...] = before_ref[...] + outer_densities(
        1, far_ref, inner_ref, trig_ref, rim_ref, halo_ref, chooser_ref, mixed_ref, trig_halo_ref, sums_ref
    )
    message_ref[0:5, :] = acc_ref[0:5, :] + acc_ref[5:10, :] + acc_ref[10:15, :]
    message_ref[5:8, :] = jnp.zeros((3, message_ref.shape[1]), jnp.float32)


def outer_local_kernel(
    near_ref, far_ref, inner_ref, trig_ref, rim_ref, near_halo_ref, far_halo_ref, near_mixed_ref, far_mixed_ref, local_ref
):
    for layer in range(2):
        halo_ref = (near_halo_ref, far_halo_ref)[layer]
        mixed_ref = (near_mixed_ref, far_mixed_ref)[layer]

        def halo(k, p, j, halo_ref=halo_ref):
            return halo_ref[tile(k, p, j)]

        get, out, inward = outer_getters(layer, (near_ref, far_ref)[layer], inner_ref, trig_ref, halo)
        z_half = upward(layer)
        for p in range(ROWS):
            for j in range(COLS):
                local = cell_locals(
                    get, out, inward, rim_ref, layer, z_half, p, j, mixed_ref[0, p, j], mixed_ref[1, p, j]
                )
                for k, value in enumerate(local):
                    local_ref[k, layer, p, j] = value


def match_kernel(ids_ref, near_halo_ref, far_halo_ref, match_ref):
    slots = ids_ref.shape[1]
    xb = near_halo_ref.shape[2]
    own = jnp.broadcast_to(ids_ref[...].astype(jnp.float32), (xb, slots))
    for side, ref in enumerate((near_halo_ref, far_halo_ref)):
        for half in range(slots // xb):
            line = ref[2 * ROWS * COLS, half : half + 1, :]
            other = jnp.transpose(jnp.broadcast_to(line, (xb, xb)))
            other = jnp.concatenate([other] * (slots // xb), axis=1)
            start = side * slots + half * xb
            match_ref[start : start + xb, :] = jnp.where(other == own, 1.0, 0.0).astype(jnp.bfloat16)


def stacked(value):
    return jnp.concatenate([part.astype(jnp.float32) for part in split3(value)], axis=0).astype(jnp.bfloat16)


def slot_motion(message_ref, near_ref, far_ref, match_ref, velocity_ref):
    others = jnp.concatenate([stacked(near_ref[...]), stacked(far_ref[...])], axis=1)
    parts = jnp.dot(others, match_ref[...], preferred_element_type=jnp.float32)
    totals = message_ref[...] + parts[0:8] + parts[8:16] + parts[16:24]
    inverse = 1.0 / totals[4:5, :]
    for part, piece in enumerate(split3(TRANSLATE * totals[0:4, :] * inverse)):
        velocity_ref[4 * part : 4 * part + 4, :] = piece.astype(jnp.float32)
    velocity_ref[12:16, :] = jnp.zeros((4, velocity_ref.shape[1]), jnp.float32)


def block_motion(velocity_ref, onehot_ref, motion_ref, first_pair):
    rows = motion_ref.shape[0] // 8
    xb = motion_ref.shape[1]
    velocity = velocity_ref[...].astype(jnp.bfloat16)
    for i in range(rows // 2):
        moved = jnp.dot(velocity, onehot_ref[first_pair + i], preferred_element_type=jnp.float32)
        moved = moved[0:8] + moved[8:16]
        for h in range(2):
            motion_ref[pl.ds(2 * i + h, 8, stride=rows), :] = moved[:, h * xb : (h + 1) * xb]


def layer_motion(motion_ref, at, yb):
    rows = motion_ref.shape[0] // 8
    parts = [motion_ref[k * rows + at * yb : k * rows + (at + 1) * yb, :] for k in range(8)]
    return [parts[k] + parts[4 + k] for k in range(4)]


def advanced(local_ref, motion, at, p, j):
    vx, vy, vz, turn = motion
    g = [local_ref[k, at, p, j] for k in range(2, 8)]
    e = local_ref[0, at, p, j] - (vx * g[0] + vy * g[1] + vz * g[2])
    q = local_ref[1, at, p, j] + turn - (vx * g[3] + vy * g[4] + vz * g[5])
    return e, q


def advance_outer_kernel(
    message_ref, near_message_ref, far_message_ref, match_ref, onehot_ref, local_ref,
    velocity_ref, near_ref, far_ref,
    motion_ref,
):
    slot_motion(message_ref, near_message_ref, far_message_ref, match_ref, velocity_ref)
    block_motion(velocity_ref, onehot_ref, motion_ref, 0)
    for layer, ref in enumerate((near_ref, far_ref)):
        motion = layer_motion(motion_ref, layer, local_ref.shape[4])
        for p in range(ROWS):
            for j in range(COLS):
                ref[tile(0, p, j)], ref[tile(1, p, j)] = advanced(local_ref, motion, layer, p, j)


def advance_inner_kernel(
    velocity_ref, onehot_ref, local_ref, near_ref, far_ref,
    inner_ref, y_near_ref, y_far_ref,
    motion_ref,
):
    layers, yb = local_ref.shape[1], local_ref.shape[4]
    block_motion(velocity_ref, onehot_ref, motion_ref, yb)
    for at in range(layers):
        motion = layer_motion(motion_ref, at, yb)
        for p in range(ROWS):
            for j in range(COLS):
                inner_ref[0, at, p, j], inner_ref[1, at, p, j] = advanced(local_ref, motion, at, p, j)
    put_y_edges(near_ref, far_ref, inner_ref, y_near_ref, y_far_ref)


def finish_kernel(
    message_ref, near_message_ref, far_message_ref, match_ref, onehot_ref, outer_local_ref, inner_local_ref,
    e_hbm, q_hbm,
    velocity_ref, motion_ref, rows_ref, out_ref, sems,
):
    yb, xb = outer_local_ref.shape[4:]
    _, cz, cy, nx = out_ref.shape
    slot_motion(message_ref, near_message_ref, far_message_ref, match_ref, velocity_ref)
    chooser = x_chooser(nx, xb, back=True)
    copies = []
    for part, local_ref in enumerate((outer_local_ref, inner_local_ref)):
        layers = local_ref.shape[1]
        block_motion(velocity_ref, onehot_ref, motion_ref, part * yb)
        for at in range(layers):
            motion = layer_motion(motion_ref, at, yb)
            for p in range(ROWS):
                to = pl.ds(at * cy + p, yb, stride=ROWS)
                for j in range(COLS):
                    e, q = advanced(local_ref, motion, at, p, j)
                    rows_ref[0, j, to, :] = e
                    rows_ref[1, j, to, :] = q
        moved = exact_dot(
            jnp.concatenate(
                [jnp.concatenate([rows_ref[f, j] for j in range(COLS)], axis=1) for f in range(2)], axis=0
            ),
            chooser,
        )
        for f, ref in enumerate((e_hbm, q_hbm)):
            for at in range(layers):
                layer = 2 * part + at
                start = (f * layers + at) * cy
                out_ref[f, layer] = moved[start : start + cy]
                copies.append(
                    pltpu.make_async_copy(out_ref.at[f, layer], ref.at[place(layer, cz)], sems.at[f, layer])
                )
                copies[-1].start()
    for copy in copies:
        copy.wait()


VMEM = pl.BlockSpec(memory_space=pltpu.VMEM)
HBM = pl.BlockSpec(memory_space=pltpu.HBM)
MIB = 1024 * 1024


def call(kernel, name, outs, scratch=(), hbm_in=0, hbm_out=False, limit=24):
    def run(*args):
        return pl.pallas_call(
            kernel,
            name=name,
            in_specs=[HBM] * hbm_in + [VMEM] * (len(args) - hbm_in),
            out_specs=[HBM if hbm_out else VMEM] * len(outs),
            out_shape=[jax.ShapeDtypeStruct(shape, dtype) for shape, dtype in outs],
            scratch_shapes=list(scratch),
            compiler_params=pltpu.CompilerParams(vmem_limit_bytes=limit * MIB),
            cost_estimate=pl.CostEstimate(flops=4 * MIB, bytes_accessed=MIB, transcendentals=0),
        )(*args)

    return run


def swap(array, axis, far):
    size = lax.axis_size(axis)
    pairs = [(i, (((i + 1) ^ 1) - 1) % size if far else i ^ 1) for i in range(size)]
    return lax.ppermute(array, axis, pairs)


def both(near, far, axis):
    far = swap(far, axis, True)
    return swap(near, axis, False), far


def shards(order_param, orientation, cell_slot, tile_grains):
    cz, cy, nx = order_param.shape
    slots = tile_grains.shape[-1]
    yb, xb = cy // ROWS, nx // COLS
    rows = cz * yb
    f32, bf16 = jnp.float32, jnp.bfloat16
    block = (ROWS, COLS, yb, xb)
    side_out = ((2 * ROWS * COLS, yb, xb), f32)
    first_side_out = ((2 * ROWS * COLS + 1, yb, xb), f32)
    inner_out = ((2, cz - 2) + block, f32)
    y_out = [((2 * cz * COLS, xb), f32)] * 2
    acc_out = ((16, slots), f32)
    mixed_out = ((2,) + block, f32)
    outer_motion = pltpu.VMEM((8 * 2 * yb, xb), f32)
    inner_motion = pltpu.VMEM((8 * (cz - 2) * yb, xb), f32)
    layer_scratch = [pltpu.VMEM((4,) + block, f32), pltpu.VMEM((16 * yb, xb), f32)]
    dma = pltpu.SemaphoreType.DMA
    prepare_outer = call(
        prepare_outer_kernel, "prepare_outer",
        [
            first_side_out, first_side_out, ((2, cz - 2, cy, nx), f32),
            ((cz, cy, nx), jnp.int32), ((1, slots), jnp.int32),
        ],
        [pltpu.VMEM((2, 2, cy, nx), f32), pltpu.VMEM((COLS, 4 * cy, xb), f32), dma((2, 2)), dma((4,))],
        hbm_in=4,
    )
    prepare_inner = call(
        prepare_inner_kernel, "prepare_inner", [inner_out] + y_out + [((rows, xb), f32)],
        [pltpu.VMEM((COLS, 2 * (cz - 2) * cy, xb), f32), pltpu.VMEM((cz * cy, xb), f32)],
    )
    onehots = call(onehot_kernel, "onehots", [((rows // 2, slots, 2 * xb), bf16), ((rows // 2, 2 * xb, slots), bf16)])
    trigs = call(trig_kernel, "trigs", [((4, cz) + block, f32)])
    inner_terms = call(
        inner_kernel, "inner_terms", [((2, 6, cz * COLS, xb), f32), ((8, cz - 2) + block, f32), acc_out],
        [pltpu.VMEM((16 * (cz - 2) * yb, xb), f32)],
    )
    near_terms = call(near_kernel, "near_terms", [mixed_out, acc_out], layer_scratch)
    far_terms = call(
        far_kernel, "far_terms", [mixed_out, ((8, slots), f32)], layer_scratch + [pltpu.VMEM((16, slots), f32)]
    )
    outer_locals = call(outer_local_kernel, "outer_locals", [((8, 2) + block, f32)])
    matches = call(match_kernel, "matches", [((2 * slots, slots), bf16)])
    advance_outer = call(
        advance_outer_kernel, "advance_outer", [((16, slots), f32), side_out, side_out], [outer_motion]
    )
    advance_inner = call(advance_inner_kernel, "advance_inner", [inner_out] + y_out, [inner_motion])
    finish = call(
        finish_kernel, "finish", [((cz, cy, nx), f32)] * 2,
        [
            pltpu.VMEM((16, slots), f32), outer_motion, pltpu.VMEM((2, COLS, 2 * cy, xb), f32), pltpu.VMEM((2, cz, cy, nx), f32), dma((2, cz)),
        ],
        hbm_out=True,
    )

    inputs = (order_param, orientation, cell_slot, tile_grains.reshape(1, slots))
    near, far, raw, raw_slots, ids = prepare_outer(
        *(pltpu.with_memory_space_constraint(array, pltpu.HBM) for array in inputs)
    )
    for step in range(STEPS):
        near_halo, far_halo = both(near, far, "gz")
        if step == 0:
            inner, y_near, y_far, blocks = prepare_inner(raw, raw_slots, near, far)
        else:
            inner, y_near, y_far = advance_inner(velocity, onehot, inner_local, near, far)
        y_near, y_far = both(y_near, y_far, "gy")
        if step == 0:
            onehot, chooser = onehots(blocks)
        (trig,) = trigs(near, far, inner)
        rim, inner_local, acc = inner_terms(near, far, inner, trig, y_near, y_far, chooser)
        near_mixed, acc = near_terms(near, inner, trig, rim, near_halo, chooser, acc)
        far_mixed, message = far_terms(far, inner, trig, rim, far_halo, chooser, acc)
        near_message, far_message = both(message, message, "gz")
        if step == 0:
            (match,) = matches(ids, near_halo, far_halo)
        (outer_local,) = outer_locals(near, far, inner, trig, rim, near_halo, far_halo, near_mixed, far_mixed)
        if step < STEPS - 1:
            velocity, near, far = advance_outer(message, near_message, far_message, match, onehot, outer_local)
    return tuple(finish(message, near_message, far_message, match, onehot, outer_local, inner_local))


def solution(mesh):
    spec = P("gz", "gy", None)
    return jax.shard_map(shards, mesh=mesh, in_specs=(spec,) * 4, out_specs=(spec,) * 2, check_vma=False)
```

```python
import functools

import jax
import jax.numpy as jnp
from jax import lax
from jax.experimental import pallas as pl
from jax.experimental.pallas import tpu as pltpu
from jax.sharding import PartitionSpec as P

STEPS = 3

DIFFUSE = 0.1
BARRIER = 0.5
PENALTY = 0.05
TORSION = 0.1
TRANSLATE = 2.0
ROTATE = 2.0

ROWS = 2
COLS = 4


def split3(value):
    high = value.astype(jnp.bfloat16)
    rest = value - high.astype(jnp.float32)
    middle = rest.astype(jnp.bfloat16)
    low = (rest - middle.astype(jnp.float32)).astype(jnp.bfloat16)
    return high, middle, low


def exact_dot(value, chooser):
    rows = value.shape[0]
    parts = jnp.dot(jnp.concatenate(split3(value), axis=0), chooser, preferred_element_type=jnp.float32)
    return parts[:rows] + parts[rows : 2 * rows] + parts[2 * rows :]


def sin_cos(angle):
    turns = jnp.floor(angle * 0.6366197723675814 + 0.5)
    rest = angle - turns * 1.5703125
    rest = rest - turns * 4.837512969970703125e-4
    rest = rest - turns * 7.54978995489188216e-8
    square = rest * rest
    sine = ((-1.9515295891e-4 * square + 8.3321608736e-3) * square - 1.6666654611e-1) * square * rest + rest
    cosine = ((2.443315711809948e-5 * square - 1.388731625493765e-3) * square + 4.166664568298827e-2) * square * square
    cosine = cosine - 0.5 * square + 1.0
    quarter = turns.astype(jnp.int32)
    odd = (quarter & 1) == 1
    sin_value = jnp.where(odd, cosine, sine)
    cos_value = jnp.where(odd, sine, cosine)
    sin_value = jnp.where((quarter & 2) == 2, -sin_value, sin_value)
    cos_value = jnp.where(((quarter + 1) & 2) == 2, -cos_value, cos_value)
    return sin_value, cos_value


def is_odd(axis):
    return lax.axis_index(axis) & 1


def place(layer, cz):
    odd = is_odd("gz")
    if layer == 0:
        return (1 - odd) * (cz - 1)
    if layer == 1:
        return odd * (cz - 1)
    return layer - 1


def facing(layer, layers):
    odd = is_odd("gz")
    return ((1 - odd) if layer == 0 else odd) * (layers - 1)


def upward(layer):
    half = 0.5 - is_odd("gz").astype(jnp.float32)
    return half if layer == 0 else -half


def tile(f, p, j):
    return (f * ROWS + p) * COLS + j


def put_y_edges(near_ref, far_ref, inner_ref, y_near_ref, y_far_ref):
    layers, yb = inner_ref.shape[1], inner_ref.shape[4]
    cz = layers + 2
    first_to_near = is_odd("gy") == 1
    for f in range(2):
        for layer in range(cz):
            for j in range(COLS):
                at = (f * cz + layer) * COLS + j
                if layer < 2:
                    ref = (near_ref, far_ref)[layer]
                    first, last = ref[tile(f, 0, j), 0:1], ref[tile(f, ROWS - 1, j), yb - 1 : yb]
                else:
                    first = inner_ref[f, layer - 2, 0, j, 0:1]
                    last = inner_ref[f, layer - 2, ROWS - 1, j, yb - 1 : yb]
                y_near_ref[at : at + 1, :] = jnp.where(first_to_near, first, last)
                y_far_ref[at : at + 1, :] = jnp.where(first_to_near, last, first)


def x_chooser(nx, xb, back=False):
    first = lax.broadcasted_iota(jnp.int32, (nx, nx), 1 if back else 0)
    second = lax.broadcasted_iota(jnp.int32, (nx, nx), 0 if back else 1)
    return jnp.where(first == COLS * (second & (xb - 1)) + (second >> (xb.bit_length() - 1)), 1.0, 0.0).astype(jnp.bfloat16)


def spread(in_ref, chooser, rows_ref, put):
    _, layers, cy, nx = in_ref.shape
    yb, xb = cy // ROWS, nx // COLS
    moved = exact_dot(in_ref[...].reshape(2 * layers * cy, nx), chooser)
    for j in range(COLS):
        rows_ref[j] = moved[:, j * xb : (j + 1) * xb]
    for f in range(2):
        for at in range(layers):
            for p in range(ROWS):
                for j in range(COLS):
                    start = (f * layers + at) * cy + p
                    put(f, at, p, j, rows_ref[j, pl.ds(start, yb, stride=ROWS), :])


def prepare_outer_kernel(
    e_hbm, q_hbm, slot_hbm, ids_hbm,
    near_ref, far_ref, raw_ref, slot_ref, ids_ref,
    in_ref, rows_ref, sems, raw_sems,
):
    cz = e_hbm.shape[0]
    _, _, cy, nx = in_ref.shape
    yb, xb = cy // ROWS, nx // COLS
    copies = [
        pltpu.make_async_copy(ref.at[place(at, cz)], in_ref.at[f, at], sems.at[f, at])
        for f, ref in enumerate((e_hbm, q_hbm))
        for at in range(2)
    ]
    copies.append(pltpu.make_async_copy(ids_hbm, ids_ref, raw_sems.at[0]))
    later = [
        pltpu.make_async_copy(e_hbm.at[1 : cz - 1], raw_ref.at[0], raw_sems.at[1]),
        pltpu.make_async_copy(q_hbm.at[1 : cz - 1], raw_ref.at[1], raw_sems.at[2]),
        pltpu.make_async_copy(slot_hbm, slot_ref, raw_sems.at[3]),
    ]
    for copy in copies + later:
        copy.start()
    chooser = x_chooser(nx, xb)
    for copy in copies:
        copy.wait()
    for ref in (near_ref, far_ref):
        ref[2 * ROWS * COLS] = jnp.zeros((yb, xb), jnp.float32)
        for half in range(ids_ref.shape[1] // xb):
            ref[2 * ROWS * COLS, half : half + 1, :] = ids_ref[:, half * xb : (half + 1) * xb].astype(jnp.float32)

    def put(f, at, p, j, value):
        (near_ref, far_ref)[at][tile(f, p, j)] = value

    spread(in_ref, chooser, rows_ref, put)
    for copy in later:
        copy.wait()


def prepare_inner_kernel(
    raw_ref, slot_ref, near_ref, far_ref,
    inner_ref, y_near_ref, y_far_ref, block_ref,
    rows_ref, slot_rows_ref,
):
    _, layers, cy, nx = raw_ref.shape
    cz = layers + 2
    yb, xb = cy // ROWS, nx // COLS
    chooser = x_chooser(nx, xb)

    def put(f, at, p, j, value):
        inner_ref[f, at, p, j] = value

    spread(raw_ref, chooser, rows_ref, put)
    put_y_edges(near_ref, far_ref, inner_ref, y_near_ref, y_far_ref)
    values = jnp.concatenate([slot_ref[place(layer, cz)] for layer in range(cz)], axis=0)
    values = values.astype(jnp.float32).astype(jnp.bfloat16)
    slot_rows_ref[...] = jnp.dot(values, chooser[:, :xb], preferred_element_type=jnp.float32)
    block_ref[...] = slot_rows_ref[pl.ds(0, cz * yb, stride=ROWS), :].astype(jnp.int32)


def chooser_kernel(block_ref, chooser_ref):
    rows, xb = block_ref.shape
    slots = chooser_ref.shape[2]
    one, zero = jnp.ones((), jnp.bfloat16), jnp.zeros((), jnp.bfloat16)
    across = lax.broadcasted_iota(jnp.int32, (xb, xb), 1)
    across = [(across + half * xb).astype(jnp.float32).astype(jnp.bfloat16) for half in range(slots // xb)]
    blocks = block_ref[...].astype(jnp.float32)
    turned = jnp.transpose(jnp.concatenate([blocks, jnp.zeros((xb - rows, xb), jnp.float32)], axis=0))
    for r in range(rows):
        at = (r % 2) * xb
        line = jnp.broadcast_to(turned[:, r : r + 1], (xb, xb)).astype(jnp.bfloat16)
        for half in range(slots // xb):
            chooser_ref[r // 2, at : at + xb, half * xb : (half + 1) * xb] = jnp.where(across[half] == line, one, zero)


def derived(e, q):
    sin_value, cos_value = sin_cos(q)
    square = e * e
    return cos_value, sin_value, square * cos_value, square * sin_value


def trig_kernel(near_ref, far_ref, inner_ref, trig_ref):
    cz = trig_ref.shape[1]
    for layer in range(cz):
        for p in range(ROWS):
            for j in range(COLS):
                if layer < 2:
                    e, q = ((near_ref, far_ref)[layer][tile(f, p, j)] for f in range(2))
                else:
                    e, q = (inner_ref[f, layer - 2, p, j] for f in range(2))
                for k, value in enumerate(derived(e, q)):
                    trig_ref[k, layer, p, j] = value


def beside(get, up, down, rim_ref, layer, k, p, j):
    here = get(k, p, j)
    yb, xb = here.shape
    row = lax.broadcasted_iota(jnp.int32, (yb, xb), 0)
    at = layer * COLS + j
    x_plus = get(k, p, j + 1) if j + 1 < COLS else pltpu.roll(get(k, p, 0), xb - 1, 1)
    x_minus = get(k, p, j - 1) if j > 0 else pltpu.roll(get(k, p, COLS - 1), 1, 1)
    if p + 1 < ROWS:
        y_plus = get(k, p + 1, j)
    else:
        y_plus = jnp.where(row == yb - 1, rim_ref[1, k, at : at + 1, :], pltpu.roll(get(k, 0, j), yb - 1, 0))
    if p > 0:
        y_minus = get(k, p - 1, j)
    else:
        y_minus = jnp.where(row == 0, rim_ref[0, k, at : at + 1, :], pltpu.roll(get(k, ROWS - 1, j), 1, 0))
    return x_plus, x_minus, y_plus, y_minus, up(k, p, j), down(k, p, j)


def gradients(side, z_half):
    halves = (0.5, 0.5, z_half)
    return [(side[2 * d] - side[2 * d + 1]) * halves[d] for d in range(3)]


def cell_densities(get, up, down, rim_ref, layer, z_half, p, j):
    sides = [beside(get, up, down, rim_ref, layer, k, p, j) for k in (0, 2, 3, 4, 5)]
    e, c, s = get(0, p, j), get(2, p, j), get(3, p, j)
    c_sum, s_sum, a_sum, b_sum = (sum(side) for side in sides[1:])
    misfit = 6.0 - c * c_sum - s * s_sum
    torque = c * b_sum - s * a_sum
    weight = e * misfit
    grads = gradients(sides[0], z_half)
    return [weight * g for g in grads] + [torque, 0.5 + e * e], weight, torque


def cell_locals(get, up, down, rim_ref, layer, z_half, p, j, weight, torque):
    e_side, q_side = (beside(get, up, down, rim_ref, layer, k, p, j) for k in range(2))
    e, q = get(0, p, j), get(1, p, j)
    laplace = sum(e_side) - 6.0 * e
    e_local = e + DIFFUSE * laplace + BARRIER * e * (1.0 - e) * (e - 0.5) - PENALTY * weight
    return [e_local, q + TORSION * torque] + gradients(e_side, z_half) + gradients(q_side, z_half)


def put_sums(totals, at, yb, sums_ref):
    rows = sums_ref.shape[0] // 16
    for k, value in enumerate(totals):
        for part, piece in enumerate(split3(value)):
            start = (part * 5 + k) * rows + at * yb
            sums_ref[start : start + yb, :] = piece.astype(jnp.float32)


def slot_sums(sums_ref, chooser_ref, first_pair):
    rows = sums_ref.shape[0] // 16
    sums_ref[15 * rows : 16 * rows, :] = jnp.zeros((rows, sums_ref.shape[1]), jnp.float32)
    acc = jnp.zeros((16, chooser_ref.shape[2]), jnp.float32)
    for i in range(rows // 2):
        left = jnp.concatenate(
            [sums_ref[pl.ds(2 * i + h, 16, stride=rows), :] for h in range(2)], axis=1
        ).astype(jnp.bfloat16)
        acc = acc + jnp.dot(left, chooser_ref[first_pair + i], preferred_element_type=jnp.float32)
    return acc


def inner_kernel(
    near_ref, far_ref, inner_ref, trig_ref, y_near_ref, y_far_ref, chooser_ref,
    rim_ref, local_ref, acc_ref,
    sums_ref,
):
    _, cz, _, _, yb, xb = trig_ref.shape
    n = cz * COLS
    last = lax.axis_size("gy") - 1
    for side in range(2):
        inside = lax.axis_index("gy") != (0, last)[side]
        from_near = is_odd("gy") == 1 - side
        e, q = (
            jnp.where(
                inside, jnp.where(from_near, y_near_ref[f * n : f * n + n, :], y_far_ref[f * n : f * n + n, :]), 0.0
            )
            for f in range(2)
        )
        for k, value in enumerate((e, q) + derived(e, q)):
            rim_ref[side, k] = value

    def inner(at, k, p, j):
        return inner_ref[k, at, p, j] if k < 2 else trig_ref[k - 2, at + 2, p, j]

    def outer(top, k, p, j):
        is_near = is_odd("gz") == (0 if top else 1)
        if k < 2:
            return jnp.where(is_near, near_ref[tile(k, p, j)], far_ref[tile(k, p, j)])
        return trig_ref[k - 2, jnp.where(is_near, 0, 1), p, j]

    for at in range(cz - 2):
        get = functools.partial(inner, at)
        up = functools.partial(inner, at + 1) if at + 1 < cz - 2 else functools.partial(outer, True)
        down = functools.partial(inner, at - 1) if at > 0 else functools.partial(outer, False)
        totals = None
        for p in range(ROWS):
            for j in range(COLS):
                densities, weight, torque = cell_densities(get, up, down, rim_ref, at + 2, 0.5, p, j)
                totals = densities if totals is None else [a + b for a, b in zip(totals, densities)]
                local = cell_locals(get, up, down, rim_ref, at + 2, 0.5, p, j, weight, torque)
                for k, value in enumerate(local):
                    local_ref[k, at, p, j] = value
        put_sums(totals, at, yb, sums_ref)
    acc_ref[...] = slot_sums(sums_ref, chooser_ref, yb)


def outer_getters(layer, own_ref, inner_ref, trig_ref, halo):
    beside_at = facing(layer, inner_ref.shape[1])

    def get(k, p, j):
        return own_ref[tile(k, p, j)] if k < 2 else trig_ref[k - 2, layer, p, j]

    def inward(k, p, j):
        return inner_ref[k, beside_at, p, j] if k < 2 else trig_ref[k - 2, beside_at + 2, p, j]

    return get, halo, inward


def outer_densities(layer, own_ref, inner_ref, trig_ref, rim_ref, halo_ref, chooser_ref, mixed_ref, trig_halo_ref, sums_ref):
    yb = trig_ref.shape[4]
    for p in range(ROWS):
        for j in range(COLS):
            for k, value in enumerate(derived(*(halo_ref[tile(f, p, j)] for f in range(2)))):
                trig_halo_ref[k, p, j] = value

    def halo(k, p, j):
        return halo_ref[tile(k, p, j)] if k < 2 else trig_halo_ref[k - 2, p, j]

    get, out, inward = outer_getters(layer, own_ref, inner_ref, trig_ref, halo)
    z_half = upward(layer)
    totals = None
    for p in range(ROWS):
        for j in range(COLS):
            densities, weight, torque = cell_densities(get, out, inward, rim_ref, layer, z_half, p, j)
            totals = densities if totals is None else [a + b for a, b in zip(totals, densities)]
            mixed_ref[0, p, j] = weight
            mixed_ref[1, p, j] = torque
    put_sums(totals, 0, yb, sums_ref)
    return slot_sums(sums_ref, chooser_ref, layer * yb // 2)


def near_kernel(
    near_ref, inner_ref, trig_ref, rim_ref, halo_ref, chooser_ref, before_ref,
    mixed_ref, acc_ref,
    trig_halo_ref, sums_ref,
):
    acc_ref[...] = before_ref[...] + outer_densities(
        0, near_ref, inner_ref, trig_ref, rim_ref, halo_ref, chooser_ref, mixed_ref, trig_halo_ref, sums_ref
    )


def far_kernel(
    far_ref, inner_ref, trig_ref, rim_ref, halo_ref, chooser_ref, before_ref,
    mixed_ref, message_ref,
    trig_halo_ref, sums_ref, acc_ref,
):
    acc_ref[...] = before_ref[...] + outer_densities(
        1, far_ref, inner_ref, trig_ref, rim_ref, halo_ref, chooser_ref, mixed_ref, trig_halo_ref, sums_ref
    )
    message_ref[0:5, :] = acc_ref[0:5, :] + acc_ref[5:10, :] + acc_ref[10:15, :]
    message_ref[5:8, :] = jnp.zeros((3, message_ref.shape[1]), jnp.float32)


def outer_local_kernel(
    near_ref, far_ref, inner_ref, trig_ref, rim_ref, near_halo_ref, far_halo_ref, near_mixed_ref, far_mixed_ref, local_ref
):
    for layer in range(2):
        halo_ref = (near_halo_ref, far_halo_ref)[layer]
        mixed_ref = (near_mixed_ref, far_mixed_ref)[layer]

        def halo(k, p, j, halo_ref=halo_ref):
            return halo_ref[tile(k, p, j)]

        get, out, inward = outer_getters(layer, (near_ref, far_ref)[layer], inner_ref, trig_ref, halo)
        z_half = upward(layer)
        for p in range(ROWS):
            for j in range(COLS):
                local = cell_locals(
                    get, out, inward, rim_ref, layer, z_half, p, j, mixed_ref[0, p, j], mixed_ref[1, p, j]
                )
                for k, value in enumerate(local):
                    local_ref[k, layer, p, j] = value


def match_kernel(ids_ref, near_halo_ref, far_halo_ref, match_ref):
    slots = ids_ref.shape[1]
    xb = near_halo_ref.shape[2]
    own = jnp.broadcast_to(ids_ref[...].astype(jnp.float32), (xb, slots))
    for side, ref in enumerate((near_halo_ref, far_halo_ref)):
        for half in range(slots // xb):
            line = ref[2 * ROWS * COLS, half : half + 1, :]
            other = jnp.transpose(jnp.broadcast_to(line, (xb, xb)))
            other = jnp.concatenate([other] * (slots // xb), axis=1)
            start = side * slots + half * xb
            match_ref[start : start + xb, :] = jnp.where(other == own, 1.0, 0.0).astype(jnp.bfloat16)


def stacked(value):
    return jnp.concatenate([part.astype(jnp.float32) for part in split3(value)], axis=0).astype(jnp.bfloat16)


def slot_motion(message_ref, near_ref, far_ref, match_ref, velocity_ref):
    others = jnp.concatenate([stacked(near_ref[...]), stacked(far_ref[...])], axis=1)
    parts = jnp.dot(others, match_ref[...], preferred_element_type=jnp.float32)
    totals = message_ref[...] + parts[0:8] + parts[8:16] + parts[16:24]
    inverse = 1.0 / totals[4:5, :]
    velocity_ref[...] = TRANSLATE * totals * inverse


def layer_motion(velocity_ref, block_ref, layer, yb):
    xb = block_ref.shape[1]
    slot = block_ref[layer * yb : (layer + 1) * yb, :]
    within = slot & (xb - 1)
    motion = []
    for k in range(4):
        value = None
        for part in range(velocity_ref.shape[1] // xb):
            table = jnp.broadcast_to(velocity_ref[k : k + 1, part * xb : (part + 1) * xb], slot.shape)
            found = jnp.take_along_axis(table, within, axis=1, mode="promise_in_bounds")
            value = found if value is None else jnp.where(slot >= part * xb, found, value)
        motion.append(value)
    return motion


def advanced(local_ref, motion, at, p, j):
    vx, vy, vz, turn = motion
    g = [local_ref[k, at, p, j] for k in range(2, 8)]
    e = local_ref[0, at, p, j] - (vx * g[0] + vy * g[1] + vz * g[2])
    q = local_ref[1, at, p, j] + turn - (vx * g[3] + vy * g[4] + vz * g[5])
    return e, q


def advance_outer_kernel(
    message_ref, near_message_ref, far_message_ref, match_ref, block_ref, local_ref,
    velocity_ref, near_ref, far_ref,
):
    slot_motion(message_ref, near_message_ref, far_message_ref, match_ref, velocity_ref)
    for layer, ref in enumerate((near_ref, far_ref)):
        motion = layer_motion(velocity_ref, block_ref, layer, local_ref.shape[4])
        for p in range(ROWS):
            for j in range(COLS):
                ref[tile(0, p, j)], ref[tile(1, p, j)] = advanced(local_ref, motion, layer, p, j)


def advance_inner_kernel(
    velocity_ref, block_ref, local_ref, near_ref, far_ref,
    inner_ref, y_near_ref, y_far_ref,
):
    layers, yb = local_ref.shape[1], local_ref.shape[4]
    for at in range(layers):
        motion = layer_motion(velocity_ref, block_ref, at + 2, yb)
        for p in range(ROWS):
            for j in range(COLS):
                inner_ref[0, at, p, j], inner_ref[1, at, p, j] = advanced(local_ref, motion, at, p, j)
    put_y_edges(near_ref, far_ref, inner_ref, y_near_ref, y_far_ref)


def finish_kernel(
    message_ref, near_message_ref, far_message_ref, match_ref, block_ref, outer_local_ref, inner_local_ref,
    e_hbm, q_hbm,
    velocity_ref, rows_ref, out_ref, sems,
):
    yb, xb = outer_local_ref.shape[4:]
    _, cz, cy, nx = out_ref.shape
    slot_motion(message_ref, near_message_ref, far_message_ref, match_ref, velocity_ref)
    chooser = x_chooser(nx, xb, back=True)
    copies = []
    for part, local_ref in enumerate((outer_local_ref, inner_local_ref)):
        layers = local_ref.shape[1]
        for at in range(layers):
            motion = layer_motion(velocity_ref, block_ref, 2 * part + at, yb)
            for p in range(ROWS):
                to = pl.ds(at * cy + p, yb, stride=ROWS)
                for j in range(COLS):
                    e, q = advanced(local_ref, motion, at, p, j)
                    rows_ref[0, j, to, :] = e
                    rows_ref[1, j, to, :] = q
        moved = exact_dot(
            jnp.concatenate(
                [jnp.concatenate([rows_ref[f, j] for j in range(COLS)], axis=1) for f in range(2)], axis=0
            ),
            chooser,
        )
        for f, ref in enumerate((e_hbm, q_hbm)):
            for at in range(layers):
                layer = 2 * part + at
                start = (f * layers + at) * cy
                out_ref[f, layer] = moved[start : start + cy]
                copies.append(
                    pltpu.make_async_copy(out_ref.at[f, layer], ref.at[place(layer, cz)], sems.at[f, layer])
                )
                copies[-1].start()
    for copy in copies:
        copy.wait()


VMEM = pl.BlockSpec(memory_space=pltpu.VMEM)
HBM = pl.BlockSpec(memory_space=pltpu.HBM)
MIB = 1024 * 1024


def call(kernel, name, outs, scratch=(), hbm_in=0, hbm_out=False, limit=24):
    def run(*args):
        return pl.pallas_call(
            kernel,
            name=name,
            in_specs=[HBM] * hbm_in + [VMEM] * (len(args) - hbm_in),
            out_specs=[HBM if hbm_out else VMEM] * len(outs),
            out_shape=[jax.ShapeDtypeStruct(shape, dtype) for shape, dtype in outs],
            scratch_shapes=list(scratch),
            compiler_params=pltpu.CompilerParams(vmem_limit_bytes=limit * MIB),
            cost_estimate=pl.CostEstimate(flops=4 * MIB, bytes_accessed=MIB, transcendentals=0),
        )(*args)

    return run


def swap(array, axis, far):
    size = lax.axis_size(axis)
    pairs = [(i, (((i + 1) ^ 1) - 1) % size if far else i ^ 1) for i in range(size)]
    return lax.ppermute(array, axis, pairs)


def both(near, far, axis):
    far = swap(far, axis, True)
    return swap(near, axis, False), far


def shards(order_param, orientation, cell_slot, tile_grains):
    cz, cy, nx = order_param.shape
    slots = tile_grains.shape[-1]
    yb, xb = cy // ROWS, nx // COLS
    rows = cz * yb
    f32, bf16 = jnp.float32, jnp.bfloat16
    block = (ROWS, COLS, yb, xb)
    side_out = ((2 * ROWS * COLS, yb, xb), f32)
    first_side_out = ((2 * ROWS * COLS + 1, yb, xb), f32)
    inner_out = ((2, cz - 2) + block, f32)
    y_out = [((2 * cz * COLS, xb), f32)] * 2
    acc_out = ((16, slots), f32)
    mixed_out = ((2,) + block, f32)
    layer_scratch = [pltpu.VMEM((4,) + block, f32), pltpu.VMEM((16 * yb, xb), f32)]
    dma = pltpu.SemaphoreType.DMA
    prepare_outer = call(
        prepare_outer_kernel, "prepare_outer",
        [
            first_side_out, first_side_out, ((2, cz - 2, cy, nx), f32),
            ((cz, cy, nx), jnp.int32), ((1, slots), jnp.int32),
        ],
        [pltpu.VMEM((2, 2, cy, nx), f32), pltpu.VMEM((COLS, 4 * cy, xb), f32), dma((2, 2)), dma((4,))],
        hbm_in=4,
    )
    prepare_inner = call(
        prepare_inner_kernel, "prepare_inner", [inner_out] + y_out + [((rows, xb), jnp.int32)],
        [pltpu.VMEM((COLS, 2 * (cz - 2) * cy, xb), f32), pltpu.VMEM((cz * cy, xb), f32)],
    )
    choosers = call(chooser_kernel, "choosers", [((rows // 2, 2 * xb, slots), bf16)])
    trigs = call(trig_kernel, "trigs", [((4, cz) + block, f32)])
    inner_terms = call(
        inner_kernel, "inner_terms", [((2, 6, cz * COLS, xb), f32), ((8, cz - 2) + block, f32), acc_out],
        [pltpu.VMEM((16 * (cz - 2) * yb, xb), f32)],
    )
    near_terms = call(near_kernel, "near_terms", [mixed_out, acc_out], layer_scratch)
    far_terms = call(
        far_kernel, "far_terms", [mixed_out, ((8, slots), f32)], layer_scratch + [pltpu.VMEM((16, slots), f32)]
    )
    outer_locals = call(outer_local_kernel, "outer_locals", [((8, 2) + block, f32)])
    matches = call(match_kernel, "matches", [((2 * slots, slots), bf16)])
    advance_outer = call(
        advance_outer_kernel, "advance_outer", [((8, slots), f32), side_out, side_out]
    )
    advance_inner = call(advance_inner_kernel, "advance_inner", [inner_out] + y_out)
    finish = call(
        finish_kernel, "finish", [((cz, cy, nx), f32)] * 2,
        [
            pltpu.VMEM((8, slots), f32), pltpu.VMEM((2, COLS, 2 * cy, xb), f32), pltpu.VMEM((2, cz, cy, nx), f32), dma((2, cz)),
        ],
        hbm_out=True,
    )

    inputs = (order_param, orientation, cell_slot, tile_grains.reshape(1, slots))
    near, far, raw, raw_slots, ids = prepare_outer(
        *(pltpu.with_memory_space_constraint(array, pltpu.HBM) for array in inputs)
    )
    for step in range(STEPS):
        near_halo, far_halo = both(near, far, "gz")
        if step == 0:
            inner, y_near, y_far, blocks = prepare_inner(raw, raw_slots, near, far)
        else:
            inner, y_near, y_far = advance_inner(velocity, blocks, inner_local, near, far)
        y_near, y_far = both(y_near, y_far, "gy")
        if step == 0:
            (chooser,) = choosers(blocks)
        (trig,) = trigs(near, far, inner)
        rim, inner_local, acc = inner_terms(near, far, inner, trig, y_near, y_far, chooser)
        near_mixed, acc = near_terms(near, inner, trig, rim, near_halo, chooser, acc)
        far_mixed, message = far_terms(far, inner, trig, rim, far_halo, chooser, acc)
        near_message, far_message = both(message, message, "gz")
        if step == 0:
            (match,) = matches(ids, near_halo, far_halo)
        (outer_local,) = outer_locals(near, far, inner, trig, rim, near_halo, far_halo, near_mixed, far_mixed)
        if step < STEPS - 1:
            velocity, near, far = advance_outer(message, near_message, far_message, match, blocks, outer_local)
    return tuple(finish(message, near_message, far_message, match, blocks, outer_local, inner_local))


def solution(mesh):
    spec = P("gz", "gy", None)
    return jax.shard_map(shards, mesh=mesh, in_specs=(spec,) * 4, out_specs=(spec,) * 2, check_vma=False)
```

```python
import functools

import jax
import jax.numpy as jnp
from jax import lax
from jax.experimental import pallas as pl
from jax.experimental.pallas import tpu as pltpu
from jax.sharding import PartitionSpec as P

STEPS = 3

DIFFUSE = 0.1
BARRIER = 0.5
PENALTY = 0.05
TORSION = 0.1
TRANSLATE = 2.0
ROTATE = 2.0

ROWS = 2
COLS = 4


def split3(value):
    high = value.astype(jnp.bfloat16)
    rest = value - high.astype(jnp.float32)
    middle = rest.astype(jnp.bfloat16)
    low = (rest - middle.astype(jnp.float32)).astype(jnp.bfloat16)
    return high, middle, low


def exact_dot(value, chooser):
    rows = value.shape[0]
    parts = jnp.dot(jnp.concatenate(split3(value), axis=0), chooser, preferred_element_type=jnp.float32)
    return parts[:rows] + parts[rows : 2 * rows] + parts[2 * rows :]


def sin_cos(angle):
    turns = jnp.floor(angle * 0.6366197723675814 + 0.5)
    rest = angle - turns * 1.5703125
    rest = rest - turns * 4.837512969970703125e-4
    rest = rest - turns * 7.54978995489188216e-8
    square = rest * rest
    sine = ((-1.9515295891e-4 * square + 8.3321608736e-3) * square - 1.6666654611e-1) * square * rest + rest
    cosine = ((2.443315711809948e-5 * square - 1.388731625493765e-3) * square + 4.166664568298827e-2) * square * square
    cosine = cosine - 0.5 * square + 1.0
    quarter = turns.astype(jnp.int32)
    odd = (quarter & 1) == 1
    sin_value = jnp.where(odd, cosine, sine)
    cos_value = jnp.where(odd, sine, cosine)
    sin_value = jnp.where((quarter & 2) == 2, -sin_value, sin_value)
    cos_value = jnp.where(((quarter + 1) & 2) == 2, -cos_value, cos_value)
    return sin_value, cos_value


def is_odd(axis):
    return lax.axis_index(axis) & 1


def place(layer, cz):
    odd = is_odd("gz")
    if layer == 0:
        return (1 - odd) * (cz - 1)
    if layer == 1:
        return odd * (cz - 1)
    return layer - 1


def facing(layer, layers):
    odd = is_odd("gz")
    return ((1 - odd) if layer == 0 else odd) * (layers - 1)


def upward(layer):
    half = 0.5 - is_odd("gz").astype(jnp.float32)
    return half if layer == 0 else -half


def tile(f, p, j):
    return (f * ROWS + p) * COLS + j


def put_y_edges(near_ref, far_ref, inner_ref, y_near_ref, y_far_ref):
    layers, yb = inner_ref.shape[1], inner_ref.shape[4]
    cz = layers + 2
    first_to_near = is_odd("gy") == 1
    for f in range(2):
        for layer in range(cz):
            for j in range(COLS):
                at = (f * cz + layer) * COLS + j
                if layer < 2:
                    ref = (near_ref, far_ref)[layer]
                    first, last = ref[tile(f, 0, j), 0:1], ref[tile(f, ROWS - 1, j), yb - 1 : yb]
                else:
                    first = inner_ref[f, layer - 2, 0, j, 0:1]
                    last = inner_ref[f, layer - 2, ROWS - 1, j, yb - 1 : yb]
                y_near_ref[at : at + 1, :] = jnp.where(first_to_near, first, last)
                y_far_ref[at : at + 1, :] = jnp.where(first_to_near, last, first)


def x_chooser(nx, xb, back=False):
    first = lax.broadcasted_iota(jnp.int32, (nx, nx), 1 if back else 0)
    second = lax.broadcasted_iota(jnp.int32, (nx, nx), 0 if back else 1)
    return jnp.where(first == COLS * (second & (xb - 1)) + (second >> (xb.bit_length() - 1)), 1.0, 0.0).astype(jnp.bfloat16)


def spread(in_ref, chooser, rows_ref, put):
    _, layers, cy, nx = in_ref.shape
    yb, xb = cy // ROWS, nx // COLS
    moved = exact_dot(in_ref[...].reshape(2 * layers * cy, nx), chooser)
    for j in range(COLS):
        rows_ref[j] = moved[:, j * xb : (j + 1) * xb]
    for f in range(2):
        for at in range(layers):
            for p in range(ROWS):
                for j in range(COLS):
                    start = (f * layers + at) * cy + p
                    put(f, at, p, j, rows_ref[j, pl.ds(start, yb, stride=ROWS), :])


def prepare_outer_kernel(
    e_hbm, q_hbm, slot_hbm, ids_hbm,
    near_ref, far_ref, raw_ref, slot_ref, ids_ref,
    in_ref, rows_ref, sems, raw_sems,
):
    cz = e_hbm.shape[0]
    _, _, cy, nx = in_ref.shape
    yb, xb = cy // ROWS, nx // COLS
    copies = [
        pltpu.make_async_copy(ref.at[place(at, cz)], in_ref.at[f, at], sems.at[f, at])
        for f, ref in enumerate((e_hbm, q_hbm))
        for at in range(2)
    ]
    copies.append(pltpu.make_async_copy(ids_hbm, ids_ref, raw_sems.at[0]))
    later = [
        pltpu.make_async_copy(e_hbm.at[1 : cz - 1], raw_ref.at[0], raw_sems.at[1]),
        pltpu.make_async_copy(q_hbm.at[1 : cz - 1], raw_ref.at[1], raw_sems.at[2]),
        pltpu.make_async_copy(slot_hbm, slot_ref, raw_sems.at[3]),
    ]
    for copy in copies + later:
        copy.start()
    chooser = x_chooser(nx, xb)
    for copy in copies:
        copy.wait()
    for ref in (near_ref, far_ref):
        ref[2 * ROWS * COLS] = jnp.zeros((yb, xb), jnp.float32)
        for half in range(ids_ref.shape[1] // xb):
            ref[2 * ROWS * COLS, half : half + 1, :] = ids_ref[:, half * xb : (half + 1) * xb].astype(jnp.float32)

    def put(f, at, p, j, value):
        (near_ref, far_ref)[at][tile(f, p, j)] = value

    spread(in_ref, chooser, rows_ref, put)
    for copy in later:
        copy.wait()


def prepare_inner_kernel(
    raw_ref, slot_ref, near_ref, far_ref,
    inner_ref, y_near_ref, y_far_ref, block_ref,
    rows_ref, slot_rows_ref,
):
    _, layers, cy, nx = raw_ref.shape
    cz = layers + 2
    yb, xb = cy // ROWS, nx // COLS
    chooser = x_chooser(nx, xb)

    def put(f, at, p, j, value):
        inner_ref[f, at, p, j] = value

    spread(raw_ref, chooser, rows_ref, put)
    put_y_edges(near_ref, far_ref, inner_ref, y_near_ref, y_far_ref)
    values = jnp.concatenate([slot_ref[place(layer, cz)] for layer in range(cz)], axis=0)
    values = values.astype(jnp.float32).astype(jnp.bfloat16)
    slot_rows_ref[...] = jnp.dot(values, chooser[:, :xb], preferred_element_type=jnp.float32)
    block_ref[...] = slot_rows_ref[pl.ds(0, cz * yb, stride=ROWS), :].astype(jnp.int32)


def chooser_kernel(block_ref, chooser_ref):
    rows, xb = block_ref.shape
    slots = chooser_ref.shape[2]
    one, zero = jnp.ones((), jnp.bfloat16), jnp.zeros((), jnp.bfloat16)
    across = lax.broadcasted_iota(jnp.int32, (xb, xb), 1)
    across = [(across + half * xb).astype(jnp.float32).astype(jnp.bfloat16) for half in range(slots // xb)]
    blocks = block_ref[...].astype(jnp.float32)
    turned = jnp.transpose(jnp.concatenate([blocks, jnp.zeros((xb - rows, xb), jnp.float32)], axis=0))
    for r in range(rows):
        at = (r % 2) * xb
        line = jnp.broadcast_to(turned[:, r : r + 1], (xb, xb)).astype(jnp.bfloat16)
        for half in range(slots // xb):
            chooser_ref[r // 2, at : at + xb, half * xb : (half + 1) * xb] = jnp.where(across[half] == line, one, zero)


def derived(e, q):
    sin_value, cos_value = sin_cos(q)
    square = e * e
    return cos_value, sin_value, square * cos_value, square * sin_value


def trig_kernel(near_ref, far_ref, inner_ref, trig_ref):
    cz = trig_ref.shape[1]
    for layer in range(cz):
        for p in range(ROWS):
            for j in range(COLS):
                if layer < 2:
                    e, q = ((near_ref, far_ref)[layer][tile(f, p, j)] for f in range(2))
                else:
                    e, q = (inner_ref[f, layer - 2, p, j] for f in range(2))
                for k, value in enumerate(derived(e, q)):
                    trig_ref[k, layer, p, j] = value


def beside(get, up, down, rim_ref, layer, k, p, j):
    here = get(k, p, j)
    yb, xb = here.shape
    row = lax.broadcasted_iota(jnp.int32, (yb, xb), 0)
    at = layer * COLS + j
    x_plus = get(k, p, j + 1) if j + 1 < COLS else pltpu.roll(get(k, p, 0), xb - 1, 1)
    x_minus = get(k, p, j - 1) if j > 0 else pltpu.roll(get(k, p, COLS - 1), 1, 1)
    if p + 1 < ROWS:
        y_plus = get(k, p + 1, j)
    else:
        y_plus = jnp.where(row == yb - 1, rim_ref[1, k, at : at + 1, :], pltpu.roll(get(k, 0, j), yb - 1, 0))
    if p > 0:
        y_minus = get(k, p - 1, j)
    else:
        y_minus = jnp.where(row == 0, rim_ref[0, k, at : at + 1, :], pltpu.roll(get(k, ROWS - 1, j), 1, 0))
    return x_plus, x_minus, y_plus, y_minus, up(k, p, j), down(k, p, j)


def gradients(side, z_half):
    halves = (0.5, 0.5, z_half)
    return [(side[2 * d] - side[2 * d + 1]) * halves[d] for d in range(3)]


def cell_densities(get, up, down, rim_ref, layer, z_half, p, j):
    sides = [beside(get, up, down, rim_ref, layer, k, p, j) for k in (0, 2, 3, 4, 5)]
    e, c, s = get(0, p, j), get(2, p, j), get(3, p, j)
    c_sum, s_sum, a_sum, b_sum = (sum(side) for side in sides[1:])
    misfit = 6.0 - c * c_sum - s * s_sum
    torque = c * b_sum - s * a_sum
    weight = e * misfit
    grads = gradients(sides[0], z_half)
    return [weight * g for g in grads] + [torque, 0.5 + e * e], weight, torque


def cell_locals(get, up, down, rim_ref, layer, z_half, p, j, weight, torque):
    e_side, q_side = (beside(get, up, down, rim_ref, layer, k, p, j) for k in range(2))
    e, q = get(0, p, j), get(1, p, j)
    laplace = sum(e_side) - 6.0 * e
    e_local = e + DIFFUSE * laplace + BARRIER * e * (1.0 - e) * (e - 0.5) - PENALTY * weight
    return [e_local, q + TORSION * torque] + gradients(e_side, z_half) + gradients(q_side, z_half)


def put_sums(totals, at, yb, sums_ref):
    rows = sums_ref.shape[0] // 16
    for k, value in enumerate(totals):
        for part, piece in enumerate(split3(value)):
            start = (part * 5 + k) * rows + at * yb
            sums_ref[start : start + yb, :] = piece.astype(jnp.float32)


def slot_sums(sums_ref, chooser_ref, first_pair):
    rows = sums_ref.shape[0] // 16
    sums_ref[15 * rows : 16 * rows, :] = jnp.zeros((rows, sums_ref.shape[1]), jnp.float32)
    acc = jnp.zeros((16, chooser_ref.shape[2]), jnp.float32)
    for i in range(rows // 2):
        left = jnp.concatenate(
            [sums_ref[pl.ds(2 * i + h, 16, stride=rows), :] for h in range(2)], axis=1
        ).astype(jnp.bfloat16)
        acc = acc + jnp.dot(left, chooser_ref[first_pair + i], preferred_element_type=jnp.float32)
    return acc


def inner_kernel(
    near_ref, far_ref, inner_ref, trig_ref, y_near_ref, y_far_ref, chooser_ref,
    rim_ref, local_ref, acc_ref, part_ref,
    sums_ref,
):
    _, cz, _, _, yb, xb = trig_ref.shape
    n = cz * COLS
    last = lax.axis_size("gy") - 1
    for side in range(2):
        inside = lax.axis_index("gy") != (0, last)[side]
        from_near = is_odd("gy") == 1 - side
        e, q = (
            jnp.where(
                inside, jnp.where(from_near, y_near_ref[f * n : f * n + n, :], y_far_ref[f * n : f * n + n, :]), 0.0
            )
            for f in range(2)
        )
        for k, value in enumerate((e, q) + derived(e, q)):
            rim_ref[side, k] = value

    def inner(at, k, p, j):
        return inner_ref[k, at, p, j] if k < 2 else trig_ref[k - 2, at + 2, p, j]

    def outer(top, k, p, j):
        is_near = is_odd("gz") == (0 if top else 1)
        if k < 2:
            return jnp.where(is_near, near_ref[tile(k, p, j)], far_ref[tile(k, p, j)])
        return trig_ref[k - 2, jnp.where(is_near, 0, 1), p, j]

    for at in range(cz - 2):
        get = functools.partial(inner, at)
        up = functools.partial(inner, at + 1) if at + 1 < cz - 2 else functools.partial(outer, True)
        down = functools.partial(inner, at - 1) if at > 0 else functools.partial(outer, False)
        totals = None
        for p in range(ROWS):
            for j in range(COLS):
                densities, weight, torque = cell_densities(get, up, down, rim_ref, at + 2, 0.5, p, j)
                totals = densities if totals is None else [a + b for a, b in zip(totals, densities)]
                local = cell_locals(get, up, down, rim_ref, at + 2, 0.5, p, j, weight, torque)
                for k, value in enumerate(local):
                    local_ref[k, at, p, j] = value
        put_sums(totals, at, yb, sums_ref)
    acc_ref[...] = slot_sums(sums_ref, chooser_ref, yb)

    get, _, inward = outer_getters(1, far_ref, inner_ref, trig_ref, None)
    for p in range(ROWS):
        for j in range(COLS):
            sides = [beside(get, inward, inward, rim_ref, 1, k, p, j)[:5] for k in (2, 3, 4, 5, 0)]
            grads = gradients(sides[4] + (sides[4][4],), 0.0)[:2]
            for k, value in enumerate([sum(side) for side in sides[:4]] + grads):
                part_ref[k, p, j] = value


def outer_getters(layer, own_ref, inner_ref, trig_ref, halo):
    beside_at = facing(layer, inner_ref.shape[1])

    def get(k, p, j):
        return own_ref[tile(k, p, j)] if k < 2 else trig_ref[k - 2, layer, p, j]

    def inward(k, p, j):
        return inner_ref[k, beside_at, p, j] if k < 2 else trig_ref[k - 2, beside_at + 2, p, j]

    return get, halo, inward


def outer_densities(layer, own_ref, inner_ref, trig_ref, rim_ref, halo_ref, chooser_ref, mixed_ref, trig_halo_ref, sums_ref):
    yb = trig_ref.shape[4]
    for p in range(ROWS):
        for j in range(COLS):
            for k, value in enumerate(derived(*(halo_ref[tile(f, p, j)] for f in range(2)))):
                trig_halo_ref[k, p, j] = value

    def halo(k, p, j):
        return halo_ref[tile(k, p, j)] if k < 2 else trig_halo_ref[k - 2, p, j]

    get, out, inward = outer_getters(layer, own_ref, inner_ref, trig_ref, halo)
    z_half = upward(layer)
    totals = None
    for p in range(ROWS):
        for j in range(COLS):
            densities, weight, torque = cell_densities(get, out, inward, rim_ref, layer, z_half, p, j)
            totals = densities if totals is None else [a + b for a, b in zip(totals, densities)]
            mixed_ref[0, p, j] = weight
            mixed_ref[1, p, j] = torque
    put_sums(totals, 0, yb, sums_ref)
    return slot_sums(sums_ref, chooser_ref, layer * yb // 2)


def near_kernel(
    near_ref, inner_ref, trig_ref, rim_ref, halo_ref, chooser_ref, before_ref,
    mixed_ref, acc_ref,
    trig_halo_ref, sums_ref,
):
    acc_ref[...] = before_ref[...] + outer_densities(
        0, near_ref, inner_ref, trig_ref, rim_ref, halo_ref, chooser_ref, mixed_ref, trig_halo_ref, sums_ref
    )


def far_kernel(
    far_ref, inner_ref, trig_ref, part_ref, halo_ref, chooser_ref, before_ref,
    mixed_ref, message_ref,
    sums_ref, acc_ref,
):
    yb = trig_ref.shape[4]
    get, _, inward = outer_getters(1, far_ref, inner_ref, trig_ref, None)
    z_half = upward(1)
    totals = None
    for p in range(ROWS):
        for j in range(COLS):
            e_out, q_out = (halo_ref[tile(f, p, j)] for f in range(2))
            c_sum, s_sum, a_sum, b_sum = (
                part_ref[k, p, j] + value for k, value in enumerate(derived(e_out, q_out))
            )
            e, c, s = get(0, p, j), get(2, p, j), get(3, p, j)
            weight = e * (6.0 - c * c_sum - s * s_sum)
            torque = c * b_sum - s * a_sum
            grads = [part_ref[4, p, j], part_ref[5, p, j], (e_out - inward(0, p, j)) * z_half]
            densities = [weight * g for g in grads] + [torque, 0.5 + e * e]
            totals = densities if totals is None else [x + y for x, y in zip(totals, densities)]
            mixed_ref[0, p, j] = weight
            mixed_ref[1, p, j] = torque
    put_sums(totals, 0, yb, sums_ref)
    acc_ref[...] = before_ref[...] + slot_sums(sums_ref, chooser_ref, yb // 2)
    message_ref[0:5, :] = acc_ref[0:5, :] + acc_ref[5:10, :] + acc_ref[10:15, :]
    message_ref[5:8, :] = jnp.zeros((3, message_ref.shape[1]), jnp.float32)


def outer_local_kernel(
    near_ref, far_ref, inner_ref, trig_ref, rim_ref, near_halo_ref, far_halo_ref, near_mixed_ref, far_mixed_ref, local_ref
):
    for layer in range(2):
        halo_ref = (near_halo_ref, far_halo_ref)[layer]
        mixed_ref = (near_mixed_ref, far_mixed_ref)[layer]

        def halo(k, p, j, halo_ref=halo_ref):
            return halo_ref[tile(k, p, j)]

        get, out, inward = outer_getters(layer, (near_ref, far_ref)[layer], inner_ref, trig_ref, halo)
        z_half = upward(layer)
        for p in range(ROWS):
            for j in range(COLS):
                local = cell_locals(
                    get, out, inward, rim_ref, layer, z_half, p, j, mixed_ref[0, p, j], mixed_ref[1, p, j]
                )
                for k, value in enumerate(local):
                    local_ref[k, layer, p, j] = value


def match_kernel(ids_ref, near_halo_ref, far_halo_ref, match_ref, back_ref):
    slots = ids_ref.shape[1]
    xb = near_halo_ref.shape[2]
    own = jnp.broadcast_to(ids_ref[...].astype(jnp.float32), (xb, slots))
    for side, ref in enumerate((near_halo_ref, far_halo_ref)):
        for half in range(slots // xb):
            line = ref[2 * ROWS * COLS, half : half + 1, :]
            other = jnp.transpose(jnp.broadcast_to(line, (xb, xb)))
            other = jnp.concatenate([other] * (slots // xb), axis=1)
            start = side * slots + half * xb
            match_ref[start : start + xb, :] = jnp.where(other == own, 1.0, 0.0).astype(jnp.bfloat16)
    back_ref[...] = x_chooser(back_ref.shape[0], xb, back=True)


def stacked(value):
    return jnp.concatenate([part.astype(jnp.float32) for part in split3(value)], axis=0).astype(jnp.bfloat16)


def slot_motion(message_ref, near_ref, far_ref, match_ref, velocity_ref):
    others = jnp.concatenate([stacked(near_ref[...]), stacked(far_ref[...])], axis=1)
    parts = jnp.dot(others, match_ref[...], preferred_element_type=jnp.float32)
    totals = message_ref[...] + parts[0:8] + parts[8:16] + parts[16:24]
    inverse = 1.0 / totals[4:5, :]
    velocity_ref[...] = TRANSLATE * totals * inverse


def layer_motion(velocity_ref, block_ref, layer, yb):
    xb = block_ref.shape[1]
    slot = block_ref[layer * yb : (layer + 1) * yb, :]
    within = slot & (xb - 1)
    motion = []
    for k in range(4):
        value = None
        for part in range(velocity_ref.shape[1] // xb):
            table = jnp.broadcast_to(velocity_ref[k : k + 1, part * xb : (part + 1) * xb], slot.shape)
            found = jnp.take_along_axis(table, within, axis=1, mode="promise_in_bounds")
            value = found if value is None else jnp.where(slot >= part * xb, found, value)
        motion.append(value)
    return motion


def advanced(local_ref, motion, at, p, j):
    vx, vy, vz, turn = motion
    g = [local_ref[k, at, p, j] for k in range(2, 8)]
    e = local_ref[0, at, p, j] - (vx * g[0] + vy * g[1] + vz * g[2])
    q = local_ref[1, at, p, j] + turn - (vx * g[3] + vy * g[4] + vz * g[5])
    return e, q


def advance_outer_kernel(
    message_ref, near_message_ref, far_message_ref, match_ref, block_ref, local_ref,
    velocity_ref, near_ref, far_ref,
):
    slot_motion(message_ref, near_message_ref, far_message_ref, match_ref, velocity_ref)
    for layer, ref in enumerate((near_ref, far_ref)):
        motion = layer_motion(velocity_ref, block_ref, layer, local_ref.shape[4])
        for p in range(ROWS):
            for j in range(COLS):
                ref[tile(0, p, j)], ref[tile(1, p, j)] = advanced(local_ref, motion, layer, p, j)


def advance_inner_kernel(
    velocity_ref, block_ref, local_ref, near_ref, far_ref,
    inner_ref, y_near_ref, y_far_ref,
):
    layers, yb = local_ref.shape[1], local_ref.shape[4]
    for at in range(layers):
        motion = layer_motion(velocity_ref, block_ref, at + 2, yb)
        for p in range(ROWS):
            for j in range(COLS):
                inner_ref[0, at, p, j], inner_ref[1, at, p, j] = advanced(local_ref, motion, at, p, j)
    put_y_edges(near_ref, far_ref, inner_ref, y_near_ref, y_far_ref)


def finish_kernel(
    message_ref, near_message_ref, far_message_ref, match_ref, back_ref, block_ref, outer_local_ref, inner_local_ref,
    e_hbm, q_hbm,
    velocity_ref, rows_ref, out_ref, sems,
):
    yb, xb = outer_local_ref.shape[4:]
    _, cz, cy, nx = out_ref.shape
    slot_motion(message_ref, near_message_ref, far_message_ref, match_ref, velocity_ref)
    chooser = back_ref[...]
    copies = []
    for first, count in [(layer, 1) for layer in range(cz)]:
        for at in range(count):
            layer = first + at
            motion = layer_motion(velocity_ref, block_ref, layer, yb)
            local_ref, inside = (outer_local_ref, layer) if layer < 2 else (inner_local_ref, layer - 2)
            for p in range(ROWS):
                to = pl.ds(at * cy + p, yb, stride=ROWS)
                for j in range(COLS):
                    e, q = advanced(local_ref, motion, inside, p, j)
                    rows_ref[0, j, to, :] = e
                    rows_ref[1, j, to, :] = q
        moved = exact_dot(
            jnp.concatenate(
                [
                    jnp.concatenate([rows_ref[f, j, : count * cy, :] for j in range(COLS)], axis=1)
                    for f in range(2)
                ],
                axis=0,
            ),
            chooser,
        )
        for f, ref in enumerate((e_hbm, q_hbm)):
            for at in range(count):
                layer = first + at
                start = (f * count + at) * cy
                out_ref[f, layer] = moved[start : start + cy]
                copies.append(
                    pltpu.make_async_copy(out_ref.at[f, layer], ref.at[place(layer, cz)], sems.at[f, layer])
                )
                copies[-1].start()
    for copy in copies:
        copy.wait()


VMEM = pl.BlockSpec(memory_space=pltpu.VMEM)
HBM = pl.BlockSpec(memory_space=pltpu.HBM)
MIB = 1024 * 1024


def call(kernel, name, outs, scratch=(), hbm_in=0, hbm_out=False, limit=24):
    def run(*args):
        return pl.pallas_call(
            kernel,
            name=name,
            in_specs=[HBM] * hbm_in + [VMEM] * (len(args) - hbm_in),
            out_specs=[HBM if hbm_out else VMEM] * len(outs),
            out_shape=[jax.ShapeDtypeStruct(shape, dtype) for shape, dtype in outs],
            scratch_shapes=list(scratch),
            compiler_params=pltpu.CompilerParams(vmem_limit_bytes=limit * MIB),
            cost_estimate=pl.CostEstimate(flops=4 * MIB, bytes_accessed=MIB, transcendentals=0),
        )(*args)

    return run


def swap(array, axis, far):
    size = lax.axis_size(axis)
    pairs = [(i, (((i + 1) ^ 1) - 1) % size if far else i ^ 1) for i in range(size)]
    return lax.ppermute(array, axis, pairs)


def both(near, far, axis):
    far = swap(far, axis, True)
    return swap(near, axis, False), far


def shards(order_param, orientation, cell_slot, tile_grains):
    cz, cy, nx = order_param.shape
    slots = tile_grains.shape[-1]
    yb, xb = cy // ROWS, nx // COLS
    rows = cz * yb
    f32, bf16 = jnp.float32, jnp.bfloat16
    block = (ROWS, COLS, yb, xb)
    side_out = ((2 * ROWS * COLS, yb, xb), f32)
    first_side_out = ((2 * ROWS * COLS + 1, yb, xb), f32)
    inner_out = ((2, cz - 2) + block, f32)
    y_out = [((2 * cz * COLS, xb), f32)] * 2
    acc_out = ((16, slots), f32)
    mixed_out = ((2,) + block, f32)
    layer_scratch = [pltpu.VMEM((4,) + block, f32), pltpu.VMEM((16 * yb, xb), f32)]
    dma = pltpu.SemaphoreType.DMA
    prepare_outer = call(
        prepare_outer_kernel, "prepare_outer",
        [
            first_side_out, first_side_out, ((2, cz - 2, cy, nx), f32),
            ((cz, cy, nx), jnp.int32), ((1, slots), jnp.int32),
        ],
        [pltpu.VMEM((2, 2, cy, nx), f32), pltpu.VMEM((COLS, 4 * cy, xb), f32), dma((2, 2)), dma((4,))],
        hbm_in=4,
    )
    prepare_inner = call(
        prepare_inner_kernel, "prepare_inner", [inner_out] + y_out + [((rows, xb), jnp.int32)],
        [pltpu.VMEM((COLS, 2 * (cz - 2) * cy, xb), f32), pltpu.VMEM((cz * cy, xb), f32)],
    )
    choosers = call(chooser_kernel, "choosers", [((rows // 2, 2 * xb, slots), bf16)])
    trigs = call(trig_kernel, "trigs", [((4, cz) + block, f32)])
    inner_terms = call(
        inner_kernel, "inner_terms", [((2, 6, cz * COLS, xb), f32), ((8, cz - 2) + block, f32), acc_out, ((6,) + block, f32)],
        [pltpu.VMEM((16 * (cz - 2) * yb, xb), f32)],
    )
    near_terms = call(near_kernel, "near_terms", [mixed_out, acc_out], layer_scratch)
    far_terms = call(
        far_kernel, "far_terms", [mixed_out, ((8, slots), f32)], [layer_scratch[1], pltpu.VMEM((16, slots), f32)]
    )
    outer_locals = call(outer_local_kernel, "outer_locals", [((8, 2) + block, f32)])
    matches = call(match_kernel, "matches", [((2 * slots, slots), bf16), ((nx, nx), bf16)])
    advance_outer = call(
        advance_outer_kernel, "advance_outer", [((8, slots), f32), side_out, side_out]
    )
    advance_inner = call(advance_inner_kernel, "advance_inner", [inner_out] + y_out)
    finish = call(
        finish_kernel, "finish", [((cz, cy, nx), f32)] * 2,
        [
            pltpu.VMEM((8, slots), f32), pltpu.VMEM((2, COLS, cy, xb), f32), pltpu.VMEM((2, cz, cy, nx), f32), dma((2, cz)),
        ],
        hbm_out=True,
    )

    inputs = (order_param, orientation, cell_slot, tile_grains.reshape(1, slots))
    near, far, raw, raw_slots, ids = prepare_outer(
        *(pltpu.with_memory_space_constraint(array, pltpu.HBM) for array in inputs)
    )
    for step in range(STEPS):
        near_halo, far_halo = both(near, far, "gz")
        if step == 0:
            inner, y_near, y_far, blocks = prepare_inner(raw, raw_slots, near, far)
        else:
            inner, y_near, y_far = advance_inner(velocity, blocks, inner_local, near, far)
        y_near, y_far = both(y_near, y_far, "gy")
        if step == 0:
            (chooser,) = choosers(blocks)
        (trig,) = trigs(near, far, inner)
        rim, inner_local, acc, part = inner_terms(near, far, inner, trig, y_near, y_far, chooser)
        near_mixed, acc = near_terms(near, inner, trig, rim, near_halo, chooser, acc)
        far_mixed, message = far_terms(far, inner, trig, part, far_halo, chooser, acc)
        near_message, far_message = both(message, message, "gz")
        if step == 0:
            match, back = matches(ids, near_halo, far_halo)
        (outer_local,) = outer_locals(near, far, inner, trig, rim, near_halo, far_halo, near_mixed, far_mixed)
        if step < STEPS - 1:
            velocity, near, far = advance_outer(message, near_message, far_message, match, blocks, outer_local)
    return tuple(finish(message, near_message, far_message, match, back, blocks, outer_local, inner_local))


def solution(mesh):
    spec = P("gz", "gy", None)
    return jax.shard_map(shards, mesh=mesh, in_specs=(spec,) * 4, out_specs=(spec,) * 2, check_vma=False)
```

```python
import functools

import jax
import jax.numpy as jnp
from jax import lax
from jax.experimental import pallas as pl
from jax.experimental.pallas import tpu as pltpu
from jax.sharding import PartitionSpec as P

STEPS = 3

DIFFUSE = 0.1
BARRIER = 0.5
PENALTY = 0.05
TORSION = 0.1
TRANSLATE = 2.0
ROTATE = 2.0

ROWS = 2
COLS = 4


def split3(value):
    high = value.astype(jnp.bfloat16)
    rest = value - high.astype(jnp.float32)
    middle = rest.astype(jnp.bfloat16)
    low = (rest - middle.astype(jnp.float32)).astype(jnp.bfloat16)
    return high, middle, low


def exact_dot(value, chooser):
    rows = value.shape[0]
    parts = jnp.dot(jnp.concatenate(split3(value), axis=0), chooser, preferred_element_type=jnp.float32)
    return parts[:rows] + parts[rows : 2 * rows] + parts[2 * rows :]


def sin_cos(angle):
    turns = jnp.floor(angle * 0.6366197723675814 + 0.5)
    rest = angle - turns * 1.5703125
    rest = rest - turns * 4.837512969970703125e-4
    rest = rest - turns * 7.54978995489188216e-8
    square = rest * rest
    sine = ((-1.9515295891e-4 * square + 8.3321608736e-3) * square - 1.6666654611e-1) * square * rest + rest
    cosine = ((2.443315711809948e-5 * square - 1.388731625493765e-3) * square + 4.166664568298827e-2) * square * square
    cosine = cosine - 0.5 * square + 1.0
    quarter = turns.astype(jnp.int32)
    odd = (quarter & 1) == 1
    sin_value = jnp.where(odd, cosine, sine)
    cos_value = jnp.where(odd, sine, cosine)
    sin_value = jnp.where((quarter & 2) == 2, -sin_value, sin_value)
    cos_value = jnp.where(((quarter + 1) & 2) == 2, -cos_value, cos_value)
    return sin_value, cos_value


def is_odd(axis):
    return lax.axis_index(axis) & 1


def place(layer, cz):
    odd = is_odd("gz")
    if layer == 0:
        return (1 - odd) * (cz - 1)
    if layer == 1:
        return odd * (cz - 1)
    return layer - 1


def facing(layer, layers):
    odd = is_odd("gz")
    return ((1 - odd) if layer == 0 else odd) * (layers - 1)


def upward(layer):
    half = 0.5 - is_odd("gz").astype(jnp.float32)
    return half if layer == 0 else -half


def tile(f, p, j):
    return (f * ROWS + p) * COLS + j


def put_y_edges(near_ref, far_ref, inner_ref, y_near_ref, y_far_ref):
    layers, yb = inner_ref.shape[1], inner_ref.shape[4]
    cz = layers + 2
    first_to_near = is_odd("gy") == 1
    for f in range(2):
        for layer in range(cz):
            for j in range(COLS):
                at = (f * cz + layer) * COLS + j
                if layer < 2:
                    ref = (near_ref, far_ref)[layer]
                    first, last = ref[tile(f, 0, j), 0:1], ref[tile(f, ROWS - 1, j), yb - 1 : yb]
                else:
                    first = inner_ref[f, layer - 2, 0, j, 0:1]
                    last = inner_ref[f, layer - 2, ROWS - 1, j, yb - 1 : yb]
                y_near_ref[at : at + 1, :] = jnp.where(first_to_near, first, last)
                y_far_ref[at : at + 1, :] = jnp.where(first_to_near, last, first)


def x_chooser(nx, xb, back=False):
    first = lax.broadcasted_iota(jnp.int32, (nx, nx), 1 if back else 0)
    second = lax.broadcasted_iota(jnp.int32, (nx, nx), 0 if back else 1)
    return jnp.where(first == COLS * (second & (xb - 1)) + (second >> (xb.bit_length() - 1)), 1.0, 0.0).astype(jnp.bfloat16)


def spread(in_ref, chooser, rows_ref, put):
    _, layers, cy, nx = in_ref.shape
    yb, xb = cy // ROWS, nx // COLS
    moved = exact_dot(in_ref[...].reshape(2 * layers * cy, nx), chooser)
    for j in range(COLS):
        rows_ref[j] = moved[:, j * xb : (j + 1) * xb]
    for f in range(2):
        for at in range(layers):
            for p in range(ROWS):
                for j in range(COLS):
                    start = (f * layers + at) * cy + p
                    put(f, at, p, j, rows_ref[j, pl.ds(start, yb, stride=ROWS), :])


def prepare_outer_kernel(
    e_hbm, q_hbm, slot_hbm, ids_hbm,
    near_ref, far_ref, raw_ref, slot_ref, ids_ref,
    in_ref, rows_ref, sems, raw_sems,
):
    cz = e_hbm.shape[0]
    _, _, cy, nx = in_ref.shape
    yb, xb = cy // ROWS, nx // COLS
    copies = [
        pltpu.make_async_copy(ref.at[place(at, cz)], in_ref.at[f, at], sems.at[f, at])
        for f, ref in enumerate((e_hbm, q_hbm))
        for at in range(2)
    ]
    copies.append(pltpu.make_async_copy(ids_hbm, ids_ref, raw_sems.at[0]))
    later = [
        pltpu.make_async_copy(e_hbm.at[1 : cz - 1], raw_ref.at[0], raw_sems.at[1]),
        pltpu.make_async_copy(q_hbm.at[1 : cz - 1], raw_ref.at[1], raw_sems.at[2]),
        pltpu.make_async_copy(slot_hbm, slot_ref, raw_sems.at[3]),
    ]
    for copy in copies + later:
        copy.start()
    chooser = x_chooser(nx, xb)
    for copy in copies:
        copy.wait()
    for ref in (near_ref, far_ref):
        ref[2 * ROWS * COLS] = jnp.zeros((yb, xb), jnp.float32)
        for half in range(ids_ref.shape[1] // xb):
            ref[2 * ROWS * COLS, half : half + 1, :] = ids_ref[:, half * xb : (half + 1) * xb].astype(jnp.float32)

    def put(f, at, p, j, value):
        (near_ref, far_ref)[at][tile(f, p, j)] = value

    spread(in_ref, chooser, rows_ref, put)
    for copy in later:
        copy.wait()


def prepare_inner_kernel(
    raw_ref, slot_ref, near_ref, far_ref,
    inner_ref, y_near_ref, y_far_ref, block_ref,
    rows_ref, slot_rows_ref,
):
    _, layers, cy, nx = raw_ref.shape
    cz = layers + 2
    yb, xb = cy // ROWS, nx // COLS
    chooser = x_chooser(nx, xb)

    def put(f, at, p, j, value):
        inner_ref[f, at, p, j] = value

    spread(raw_ref, chooser, rows_ref, put)
    put_y_edges(near_ref, far_ref, inner_ref, y_near_ref, y_far_ref)
    values = jnp.concatenate([slot_ref[place(layer, cz)] for layer in range(cz)], axis=0)
    values = values.astype(jnp.float32).astype(jnp.bfloat16)
    slot_rows_ref[...] = jnp.dot(values, chooser[:, :xb], preferred_element_type=jnp.float32)
    block_ref[...] = slot_rows_ref[pl.ds(0, cz * yb, stride=ROWS), :].astype(jnp.int32)


def chooser_kernel(block_ref, chooser_ref):
    rows, xb = block_ref.shape
    slots = chooser_ref.shape[2]
    one, zero = jnp.ones((), jnp.bfloat16), jnp.zeros((), jnp.bfloat16)
    across = lax.broadcasted_iota(jnp.int32, (xb, xb), 1)
    across = [(across + half * xb).astype(jnp.float32).astype(jnp.bfloat16) for half in range(slots // xb)]
    blocks = block_ref[...].astype(jnp.float32)
    turned = jnp.transpose(jnp.concatenate([blocks, jnp.zeros((xb - rows, xb), jnp.float32)], axis=0))
    for r in range(rows):
        at = (r % 2) * xb
        line = jnp.broadcast_to(turned[:, r : r + 1], (xb, xb)).astype(jnp.bfloat16)
        for half in range(slots // xb):
            chooser_ref[r // 2, at : at + xb, half * xb : (half + 1) * xb] = jnp.where(across[half] == line, one, zero)


def derived(e, q):
    sin_value, cos_value = sin_cos(q)
    square = e * e
    return cos_value, sin_value, square * cos_value, square * sin_value


def trig_kernel(near_ref, far_ref, inner_ref, trig_ref):
    cz = trig_ref.shape[1]
    for layer in range(cz):
        for p in range(ROWS):
            for j in range(COLS):
                if layer < 2:
                    e, q = ((near_ref, far_ref)[layer][tile(f, p, j)] for f in range(2))
                else:
                    e, q = (inner_ref[f, layer - 2, p, j] for f in range(2))
                for k, value in enumerate(derived(e, q)):
                    trig_ref[k, layer, p, j] = value


def beside(get, up, down, rim_ref, layer, k, p, j):
    here = get(k, p, j)
    yb, xb = here.shape
    row = lax.broadcasted_iota(jnp.int32, (yb, xb), 0)
    at = layer * COLS + j
    x_plus = get(k, p, j + 1) if j + 1 < COLS else pltpu.roll(get(k, p, 0), xb - 1, 1)
    x_minus = get(k, p, j - 1) if j > 0 else pltpu.roll(get(k, p, COLS - 1), 1, 1)
    if p + 1 < ROWS:
        y_plus = get(k, p + 1, j)
    else:
        y_plus = jnp.where(row == yb - 1, rim_ref[1, k, at : at + 1, :], pltpu.roll(get(k, 0, j), yb - 1, 0))
    if p > 0:
        y_minus = get(k, p - 1, j)
    else:
        y_minus = jnp.where(row == 0, rim_ref[0, k, at : at + 1, :], pltpu.roll(get(k, ROWS - 1, j), 1, 0))
    return x_plus, x_minus, y_plus, y_minus, up(k, p, j), down(k, p, j)


def gradients(side, z_half):
    halves = (0.5, 0.5, z_half)
    return [(side[2 * d] - side[2 * d + 1]) * halves[d] for d in range(3)]


def cell_densities(get, up, down, rim_ref, layer, z_half, p, j):
    sides = [beside(get, up, down, rim_ref, layer, k, p, j) for k in (0, 2, 3, 4, 5)]
    e, c, s = get(0, p, j), get(2, p, j), get(3, p, j)
    c_sum, s_sum, a_sum, b_sum = (sum(side) for side in sides[1:])
    misfit = 6.0 - c * c_sum - s * s_sum
    torque = c * b_sum - s * a_sum
    weight = e * misfit
    grads = gradients(sides[0], z_half)
    return [weight * g for g in grads] + [torque, 0.5 + e * e], weight, torque


def cell_locals(get, up, down, rim_ref, layer, z_half, p, j, weight, torque):
    e_side, q_side = (beside(get, up, down, rim_ref, layer, k, p, j) for k in range(2))
    e, q = get(0, p, j), get(1, p, j)
    laplace = sum(e_side) - 6.0 * e
    e_local = e + DIFFUSE * laplace + BARRIER * e * (1.0 - e) * (e - 0.5) - PENALTY * weight
    return [e_local, q + TORSION * torque] + gradients(e_side, z_half) + gradients(q_side, z_half)


def put_sums(totals, at, yb, sums_ref):
    rows = sums_ref.shape[0] // 16
    for k, value in enumerate(totals):
        for part, piece in enumerate(split3(value)):
            start = (part * 5 + k) * rows + at * yb
            sums_ref[start : start + yb, :] = piece.astype(jnp.float32)


def slot_sums(sums_ref, chooser_ref, first_pair):
    rows = sums_ref.shape[0] // 16
    sums_ref[15 * rows : 16 * rows, :] = jnp.zeros((rows, sums_ref.shape[1]), jnp.float32)
    acc = jnp.zeros((16, chooser_ref.shape[2]), jnp.float32)
    for i in range(rows // 2):
        left = jnp.concatenate(
            [sums_ref[pl.ds(2 * i + h, 16, stride=rows), :] for h in range(2)], axis=1
        ).astype(jnp.bfloat16)
        acc = acc + jnp.dot(left, chooser_ref[first_pair + i], preferred_element_type=jnp.float32)
    return acc


def inner_kernel(
    near_ref, far_ref, inner_ref, trig_ref, y_near_ref, y_far_ref, chooser_ref,
    rim_ref, local_ref, acc_ref, part_ref,
    sums_ref,
):
    _, cz, _, _, yb, xb = trig_ref.shape
    n = cz * COLS
    last = lax.axis_size("gy") - 1
    for side in range(2):
        inside = lax.axis_index("gy") != (0, last)[side]
        from_near = is_odd("gy") == 1 - side
        e, q = (
            jnp.where(
                inside, jnp.where(from_near, y_near_ref[f * n : f * n + n, :], y_far_ref[f * n : f * n + n, :]), 0.0
            )
            for f in range(2)
        )
        for k, value in enumerate((e, q) + derived(e, q)):
            rim_ref[side, k] = value

    def inner(at, k, p, j):
        return inner_ref[k, at, p, j] if k < 2 else trig_ref[k - 2, at + 2, p, j]

    def outer(top, k, p, j):
        is_near = is_odd("gz") == (0 if top else 1)
        if k < 2:
            return jnp.where(is_near, near_ref[tile(k, p, j)], far_ref[tile(k, p, j)])
        return trig_ref[k - 2, jnp.where(is_near, 0, 1), p, j]

    for at in range(cz - 2):
        get = functools.partial(inner, at)
        up = functools.partial(inner, at + 1) if at + 1 < cz - 2 else functools.partial(outer, True)
        down = functools.partial(inner, at - 1) if at > 0 else functools.partial(outer, False)
        totals = None
        for p in range(ROWS):
            for j in range(COLS):
                densities, weight, torque = cell_densities(get, up, down, rim_ref, at + 2, 0.5, p, j)
                totals = densities if totals is None else [a + b for a, b in zip(totals, densities)]
                local = cell_locals(get, up, down, rim_ref, at + 2, 0.5, p, j, weight, torque)
                for k, value in enumerate(local):
                    local_ref[k, at, p, j] = value
        put_sums(totals, at, yb, sums_ref)
    acc_ref[...] = slot_sums(sums_ref, chooser_ref, yb)

    get, _, inward = outer_getters(1, far_ref, inner_ref, trig_ref, None)
    for p in range(ROWS):
        for j in range(COLS):
            sides = [beside(get, inward, inward, rim_ref, 1, k, p, j)[:5] for k in (2, 3, 4, 5, 0)]
            grads = gradients(sides[4] + (sides[4][4],), 0.0)[:2]
            for k, value in enumerate([sum(side) for side in sides[:4]] + grads):
                part_ref[k, p, j] = value


def outer_getters(layer, own_ref, inner_ref, trig_ref, halo):
    beside_at = facing(layer, inner_ref.shape[1])

    def get(k, p, j):
        return own_ref[tile(k, p, j)] if k < 2 else trig_ref[k - 2, layer, p, j]

    def inward(k, p, j):
        return inner_ref[k, beside_at, p, j] if k < 2 else trig_ref[k - 2, beside_at + 2, p, j]

    return get, halo, inward


def outer_densities(layer, own_ref, inner_ref, trig_ref, rim_ref, halo_ref, chooser_ref, mixed_ref, trig_halo_ref, sums_ref):
    yb = trig_ref.shape[4]
    for p in range(ROWS):
        for j in range(COLS):
            for k, value in enumerate(derived(*(halo_ref[tile(f, p, j)] for f in range(2)))):
                trig_halo_ref[k, p, j] = value

    def halo(k, p, j):
        return halo_ref[tile(k, p, j)] if k < 2 else trig_halo_ref[k - 2, p, j]

    get, out, inward = outer_getters(layer, own_ref, inner_ref, trig_ref, halo)
    z_half = upward(layer)
    totals = None
    for p in range(ROWS):
        for j in range(COLS):
            densities, weight, torque = cell_densities(get, out, inward, rim_ref, layer, z_half, p, j)
            totals = densities if totals is None else [a + b for a, b in zip(totals, densities)]
            mixed_ref[0, p, j] = weight
            mixed_ref[1, p, j] = torque
    put_sums(totals, 0, yb, sums_ref)
    return slot_sums(sums_ref, chooser_ref, layer * yb // 2)


def near_kernel(
    near_ref, inner_ref, trig_ref, rim_ref, halo_ref, chooser_ref, before_ref,
    mixed_ref, acc_ref,
    trig_halo_ref, sums_ref,
):
    acc_ref[...] = before_ref[...] + outer_densities(
        0, near_ref, inner_ref, trig_ref, rim_ref, halo_ref, chooser_ref, mixed_ref, trig_halo_ref, sums_ref
    )


def far_kernel(
    far_ref, inner_ref, trig_ref, part_ref, halo_ref, chooser_ref, before_ref,
    mixed_ref, message_ref,
    sums_ref, acc_ref,
):
    yb = trig_ref.shape[4]
    get, _, inward = outer_getters(1, far_ref, inner_ref, trig_ref, None)
    z_half = upward(1)
    totals = None
    for p in range(ROWS):
        for j in range(COLS):
            e_out, q_out = (halo_ref[tile(f, p, j)] for f in range(2))
            c_sum, s_sum, a_sum, b_sum = (
                part_ref[k, p, j] + value for k, value in enumerate(derived(e_out, q_out))
            )
            e, c, s = get(0, p, j), get(2, p, j), get(3, p, j)
            weight = e * (6.0 - c * c_sum - s * s_sum)
            torque = c * b_sum - s * a_sum
            grads = [part_ref[4, p, j], part_ref[5, p, j], (e_out - inward(0, p, j)) * z_half]
            densities = [weight * g for g in grads] + [torque, 0.5 + e * e]
            totals = densities if totals is None else [x + y for x, y in zip(totals, densities)]
            mixed_ref[0, p, j] = weight
            mixed_ref[1, p, j] = torque
    put_sums(totals, 0, yb, sums_ref)
    acc_ref[...] = before_ref[...] + slot_sums(sums_ref, chooser_ref, yb // 2)
    message_ref[0:5, :] = acc_ref[0:5, :] + acc_ref[5:10, :] + acc_ref[10:15, :]
    message_ref[5:8, :] = jnp.zeros((3, message_ref.shape[1]), jnp.float32)


def outer_local_kernel(
    near_ref, far_ref, inner_ref, trig_ref, rim_ref, near_halo_ref, far_halo_ref, near_mixed_ref, far_mixed_ref, local_ref
):
    for layer in range(2):
        halo_ref = (near_halo_ref, far_halo_ref)[layer]
        mixed_ref = (near_mixed_ref, far_mixed_ref)[layer]

        def halo(k, p, j, halo_ref=halo_ref):
            return halo_ref[tile(k, p, j)]

        get, out, inward = outer_getters(layer, (near_ref, far_ref)[layer], inner_ref, trig_ref, halo)
        z_half = upward(layer)
        for p in range(ROWS):
            for j in range(COLS):
                local = cell_locals(
                    get, out, inward, rim_ref, layer, z_half, p, j, mixed_ref[0, p, j], mixed_ref[1, p, j]
                )
                for k, value in enumerate(local):
                    local_ref[k, layer, p, j] = value


def match_kernel(ids_ref, near_halo_ref, far_halo_ref, match_ref, back_ref):
    slots = ids_ref.shape[1]
    xb = near_halo_ref.shape[2]
    own = jnp.broadcast_to(ids_ref[...].astype(jnp.float32), (xb, slots))
    number = lax.broadcasted_iota(jnp.int32, (xb, slots), 0)
    for side, ref in enumerate((near_halo_ref, far_halo_ref)):
        where = jnp.full((1, slots), -1, jnp.int32)
        for half in range(slots // xb):
            line = ref[2 * ROWS * COLS, half : half + 1, :]
            other = jnp.transpose(jnp.broadcast_to(line, (xb, xb)))
            other = jnp.concatenate([other] * (slots // xb), axis=1)
            found = jnp.where(other == own, number + half * xb, -1)
            where = jnp.maximum(where, jnp.max(found, axis=0, keepdims=True))
        match_ref[side] = jnp.broadcast_to(where, (8, slots))
    back_ref[...] = x_chooser(back_ref.shape[0], xb, back=True)


def looked_up(tables, slot):
    lanes = slot.shape[1]
    within = slot & (lanes - 1)
    value = None
    for part, table in enumerate(tables):
        found = jnp.take_along_axis(table, within, axis=1, mode="promise_in_bounds")
        inside = (slot >= part * lanes) & (slot < (part + 1) * lanes)
        value = jnp.where(inside, found, 0.0 if value is None else value)
    return value


def slot_motion(message_ref, near_ref, far_ref, match_ref, velocity_ref, lanes):
    for start in range(0, message_ref.shape[1], lanes):
        at = slice(start, start + lanes)
        totals = message_ref[:, at]
        for side, ref in enumerate((near_ref, far_ref)):
            tables = [ref[:, part : part + lanes] for part in range(0, ref.shape[1], lanes)]
            totals = totals + looked_up(tables, match_ref[side, :, at])
        inverse = 1.0 / totals[4:5, :]
        velocity_ref[:, at] = TRANSLATE * totals * inverse


def layer_motion(velocity_ref, block_ref, layer, yb):
    xb = block_ref.shape[1]
    slot = block_ref[layer * yb : (layer + 1) * yb, :]
    within = slot & (xb - 1)
    motion = []
    for k in range(4):
        value = None
        for part in range(velocity_ref.shape[1] // xb):
            table = jnp.broadcast_to(velocity_ref[k : k + 1, part * xb : (part + 1) * xb], slot.shape)
            found = jnp.take_along_axis(table, within, axis=1, mode="promise_in_bounds")
            value = found if value is None else jnp.where(slot >= part * xb, found, value)
        motion.append(value)
    return motion


def advanced(local_ref, motion, at, p, j):
    vx, vy, vz, turn = motion
    g = [local_ref[k, at, p, j] for k in range(2, 8)]
    e = local_ref[0, at, p, j] - (vx * g[0] + vy * g[1] + vz * g[2])
    q = local_ref[1, at, p, j] + turn - (vx * g[3] + vy * g[4] + vz * g[5])
    return e, q


def advance_outer_kernel(
    message_ref, near_message_ref, far_message_ref, match_ref, block_ref, local_ref,
    velocity_ref, near_ref, far_ref,
):
    slot_motion(message_ref, near_message_ref, far_message_ref, match_ref, velocity_ref, block_ref.shape[1])
    for layer, ref in enumerate((near_ref, far_ref)):
        motion = layer_motion(velocity_ref, block_ref, layer, local_ref.shape[4])
        for p in range(ROWS):
            for j in range(COLS):
                ref[tile(0, p, j)], ref[tile(1, p, j)] = advanced(local_ref, motion, layer, p, j)


def advance_inner_kernel(
    velocity_ref, block_ref, local_ref, near_ref, far_ref,
    inner_ref, y_near_ref, y_far_ref,
):
    layers, yb = local_ref.shape[1], local_ref.shape[4]
    for at in range(layers):
        motion = layer_motion(velocity_ref, block_ref, at + 2, yb)
        for p in range(ROWS):
            for j in range(COLS):
                inner_ref[0, at, p, j], inner_ref[1, at, p, j] = advanced(local_ref, motion, at, p, j)
    put_y_edges(near_ref, far_ref, inner_ref, y_near_ref, y_far_ref)


def finish_kernel(
    message_ref, near_message_ref, far_message_ref, match_ref, back_ref, block_ref, outer_local_ref, inner_local_ref,
    e_hbm, q_hbm,
    velocity_ref, rows_ref, out_ref, sems,
):
    yb, xb = outer_local_ref.shape[4:]
    _, cz, cy, nx = out_ref.shape
    slot_motion(message_ref, near_message_ref, far_message_ref, match_ref, velocity_ref, xb)
    chooser = back_ref[...]
    copies = []
    for first, count in [(layer, 1) for layer in range(cz)]:
        for at in range(count):
            layer = first + at
            motion = layer_motion(velocity_ref, block_ref, layer, yb)
            local_ref, inside = (outer_local_ref, layer) if layer < 2 else (inner_local_ref, layer - 2)
            for p in range(ROWS):
                to = pl.ds(at * cy + p, yb, stride=ROWS)
                for j in range(COLS):
                    e, q = advanced(local_ref, motion, inside, p, j)
                    rows_ref[0, j, to, :] = e
                    rows_ref[1, j, to, :] = q
        moved = exact_dot(
            jnp.concatenate(
                [
                    jnp.concatenate([rows_ref[f, j, : count * cy, :] for j in range(COLS)], axis=1)
                    for f in range(2)
                ],
                axis=0,
            ),
            chooser,
        )
        for f, ref in enumerate((e_hbm, q_hbm)):
            for at in range(count):
                layer = first + at
                start = (f * count + at) * cy
                out_ref[f, layer] = moved[start : start + cy]
                copies.append(
                    pltpu.make_async_copy(out_ref.at[f, layer], ref.at[place(layer, cz)], sems.at[f, layer])
                )
                copies[-1].start()
    for copy in copies:
        copy.wait()


VMEM = pl.BlockSpec(memory_space=pltpu.VMEM)
HBM = pl.BlockSpec(memory_space=pltpu.HBM)
MIB = 1024 * 1024


def call(kernel, name, outs, scratch=(), hbm_in=0, hbm_out=False, limit=24):
    def run(*args):
        return pl.pallas_call(
            kernel,
            name=name,
            in_specs=[HBM] * hbm_in + [VMEM] * (len(args) - hbm_in),
            out_specs=[HBM if hbm_out else VMEM] * len(outs),
            out_shape=[jax.ShapeDtypeStruct(shape, dtype) for shape, dtype in outs],
            scratch_shapes=list(scratch),
            compiler_params=pltpu.CompilerParams(vmem_limit_bytes=limit * MIB),
            cost_estimate=pl.CostEstimate(flops=4 * MIB, bytes_accessed=MIB, transcendentals=0),
        )(*args)

    return run


def swap(array, axis, far):
    size = lax.axis_size(axis)
    pairs = [(i, (((i + 1) ^ 1) - 1) % size if far else i ^ 1) for i in range(size)]
    return lax.ppermute(array, axis, pairs)


def both(near, far, axis):
    far = swap(far, axis, True)
    return swap(near, axis, False), far


def shards(order_param, orientation, cell_slot, tile_grains):
    cz, cy, nx = order_param.shape
    slots = tile_grains.shape[-1]
    yb, xb = cy // ROWS, nx // COLS
    rows = cz * yb
    f32, bf16 = jnp.float32, jnp.bfloat16
    block = (ROWS, COLS, yb, xb)
    side_out = ((2 * ROWS * COLS, yb, xb), f32)
    first_side_out = ((2 * ROWS * COLS + 1, yb, xb), f32)
    inner_out = ((2, cz - 2) + block, f32)
    y_out = [((2 * cz * COLS, xb), f32)] * 2
    acc_out = ((16, slots), f32)
    mixed_out = ((2,) + block, f32)
    layer_scratch = [pltpu.VMEM((4,) + block, f32), pltpu.VMEM((16 * yb, xb), f32)]
    dma = pltpu.SemaphoreType.DMA
    prepare_outer = call(
        prepare_outer_kernel, "prepare_outer",
        [
            first_side_out, first_side_out, ((2, cz - 2, cy, nx), f32),
            ((cz, cy, nx), jnp.int32), ((1, slots), jnp.int32),
        ],
        [pltpu.VMEM((2, 2, cy, nx), f32), pltpu.VMEM((COLS, 4 * cy, xb), f32), dma((2, 2)), dma((4,))],
        hbm_in=4,
    )
    prepare_inner = call(
        prepare_inner_kernel, "prepare_inner", [inner_out] + y_out + [((rows, xb), jnp.int32)],
        [pltpu.VMEM((COLS, 2 * (cz - 2) * cy, xb), f32), pltpu.VMEM((cz * cy, xb), f32)],
    )
    choosers = call(chooser_kernel, "choosers", [((rows // 2, 2 * xb, slots), bf16)])
    trigs = call(trig_kernel, "trigs", [((4, cz) + block, f32)])
    inner_terms = call(
        inner_kernel, "inner_terms", [((2, 6, cz * COLS, xb), f32), ((8, cz - 2) + block, f32), acc_out, ((6,) + block, f32)],
        [pltpu.VMEM((16 * (cz - 2) * yb, xb), f32)],
    )
    near_terms = call(near_kernel, "near_terms", [mixed_out, acc_out], layer_scratch)
    far_terms = call(
        far_kernel, "far_terms", [mixed_out, ((8, slots), f32)], [layer_scratch[1], pltpu.VMEM((16, slots), f32)]
    )
    outer_locals = call(outer_local_kernel, "outer_locals", [((8, 2) + block, f32)])
    matches = call(match_kernel, "matches", [((2, 8, slots), jnp.int32), ((nx, nx), bf16)])
    advance_outer = call(
        advance_outer_kernel, "advance_outer", [((8, slots), f32), side_out, side_out]
    )
    advance_inner = call(advance_inner_kernel, "advance_inner", [inner_out] + y_out)
    finish = call(
        finish_kernel, "finish", [((cz, cy, nx), f32)] * 2,
        [
            pltpu.VMEM((8, slots), f32), pltpu.VMEM((2, COLS, cy, xb), f32), pltpu.VMEM((2, cz, cy, nx), f32), dma((2, cz)),
        ],
        hbm_out=True,
    )

    inputs = (order_param, orientation, cell_slot, tile_grains.reshape(1, slots))
    near, far, raw, raw_slots, ids = prepare_outer(
        *(pltpu.with_memory_space_constraint(array, pltpu.HBM) for array in inputs)
    )
    for step in range(STEPS):
        near_halo, far_halo = both(near, far, "gz")
        if step == 0:
            inner, y_near, y_far, blocks = prepare_inner(raw, raw_slots, near, far)
        else:
            inner, y_near, y_far = advance_inner(velocity, blocks, inner_local, near, far)
        y_near, y_far = both(y_near, y_far, "gy")
        if step == 0:
            (chooser,) = choosers(blocks)
        (trig,) = trigs(near, far, inner)
        rim, inner_local, acc, part = inner_terms(near, far, inner, trig, y_near, y_far, chooser)
        near_mixed, acc = near_terms(near, inner, trig, rim, near_halo, chooser, acc)
        far_mixed, message = far_terms(far, inner, trig, part, far_halo, chooser, acc)
        near_message, far_message = both(message, message, "gz")
        if step == 0:
            match, back = matches(ids, near_halo, far_halo)
        (outer_local,) = outer_locals(near, far, inner, trig, rim, near_halo, far_halo, near_mixed, far_mixed)
        if step < STEPS - 1:
            velocity, near, far = advance_outer(message, near_message, far_message, match, blocks, outer_local)
    return tuple(finish(message, near_message, far_message, match, back, blocks, outer_local, inner_local))


def solution(mesh):
    spec = P("gz", "gy", None)
    return jax.shard_map(shards, mesh=mesh, in_specs=(spec,) * 4, out_specs=(spec,) * 2, check_vma=False)
```

```python
import functools

import jax
import jax.numpy as jnp
from jax import lax
from jax.experimental import pallas as pl
from jax.experimental.pallas import tpu as pltpu
from jax.sharding import PartitionSpec as P

STEPS = 3

DIFFUSE = 0.1
BARRIER = 0.5
PENALTY = 0.05
TORSION = 0.1
TRANSLATE = 2.0
ROTATE = 2.0

ROWS = 2
COLS = 4


def split3(value):
    high = value.astype(jnp.bfloat16)
    rest = value - high.astype(jnp.float32)
    middle = rest.astype(jnp.bfloat16)
    low = (rest - middle.astype(jnp.float32)).astype(jnp.bfloat16)
    return high, middle, low


def exact_dot(value, chooser):
    rows = value.shape[0]
    parts = jnp.dot(jnp.concatenate(split3(value), axis=0), chooser, preferred_element_type=jnp.float32)
    return parts[:rows] + parts[rows : 2 * rows] + parts[2 * rows :]


def sin_cos(angle):
    turns = jnp.floor(angle * 0.6366197723675814 + 0.5)
    rest = angle - turns * 1.5703125
    rest = rest - turns * 4.837512969970703125e-4
    rest = rest - turns * 7.54978995489188216e-8
    square = rest * rest
    sine = ((-1.9515295891e-4 * square + 8.3321608736e-3) * square - 1.6666654611e-1) * square * rest + rest
    cosine = ((2.443315711809948e-5 * square - 1.388731625493765e-3) * square + 4.166664568298827e-2) * square * square
    cosine = cosine - 0.5 * square + 1.0
    quarter = turns.astype(jnp.int32)
    odd = (quarter & 1) == 1
    sin_value = jnp.where(odd, cosine, sine)
    cos_value = jnp.where(odd, sine, cosine)
    sin_value = jnp.where((quarter & 2) == 2, -sin_value, sin_value)
    cos_value = jnp.where(((quarter + 1) & 2) == 2, -cos_value, cos_value)
    return sin_value, cos_value


def is_odd(axis):
    return lax.axis_index(axis) & 1


def place(layer, cz):
    odd = is_odd("gz")
    if layer == 0:
        return (1 - odd) * (cz - 1)
    if layer == 1:
        return odd * (cz - 1)
    return layer - 1


def facing(layer, layers):
    odd = is_odd("gz")
    return ((1 - odd) if layer == 0 else odd) * (layers - 1)


def upward(layer):
    half = 0.5 - is_odd("gz").astype(jnp.float32)
    return half if layer == 0 else -half


def tile(f, p, j):
    return (f * ROWS + p) * COLS + j


def put_y_edges(near_ref, far_ref, inner_ref, y_near_ref, y_far_ref):
    layers, yb = inner_ref.shape[1], inner_ref.shape[4]
    cz = layers + 2
    first_to_near = is_odd("gy") == 1
    for f in range(2):
        for layer in range(cz):
            for j in range(COLS):
                at = (f * cz + layer) * COLS + j
                if layer < 2:
                    ref = (near_ref, far_ref)[layer]
                    first, last = ref[tile(f, 0, j), 0:1], ref[tile(f, ROWS - 1, j), yb - 1 : yb]
                else:
                    first = inner_ref[f, layer - 2, 0, j, 0:1]
                    last = inner_ref[f, layer - 2, ROWS - 1, j, yb - 1 : yb]
                y_near_ref[at : at + 1, :] = jnp.where(first_to_near, first, last)
                y_far_ref[at : at + 1, :] = jnp.where(first_to_near, last, first)


def x_chooser(nx, xb, back=False):
    first = lax.broadcasted_iota(jnp.int32, (nx, nx), 1 if back else 0)
    second = lax.broadcasted_iota(jnp.int32, (nx, nx), 0 if back else 1)
    return jnp.where(first == COLS * (second & (xb - 1)) + (second >> (xb.bit_length() - 1)), 1.0, 0.0).astype(jnp.bfloat16)


def spread(in_ref, chooser, rows_ref, put):
    _, layers, cy, nx = in_ref.shape
    yb, xb = cy // ROWS, nx // COLS
    moved = exact_dot(in_ref[...].reshape(2 * layers * cy, nx), chooser)
    for j in range(COLS):
        rows_ref[j] = moved[:, j * xb : (j + 1) * xb]
    for f in range(2):
        for at in range(layers):
            for p in range(ROWS):
                for j in range(COLS):
                    start = (f * layers + at) * cy + p
                    put(f, at, p, j, rows_ref[j, pl.ds(start, yb, stride=ROWS), :])


def prepare_outer_kernel(
    e_hbm, q_hbm, slot_hbm, ids_hbm,
    near_ref, far_ref, raw_ref, slot_ref, ids_ref,
    in_ref, rows_ref, sems, raw_sems,
):
    cz = e_hbm.shape[0]
    _, _, cy, nx = in_ref.shape
    yb, xb = cy // ROWS, nx // COLS
    copies = [
        pltpu.make_async_copy(ref.at[place(at, cz)], in_ref.at[f, at], sems.at[f, at])
        for f, ref in enumerate((e_hbm, q_hbm))
        for at in range(2)
    ]
    copies.append(pltpu.make_async_copy(ids_hbm, ids_ref, raw_sems.at[0]))
    later = [
        pltpu.make_async_copy(e_hbm.at[1 : cz - 1], raw_ref.at[0], raw_sems.at[1]),
        pltpu.make_async_copy(q_hbm.at[1 : cz - 1], raw_ref.at[1], raw_sems.at[2]),
        pltpu.make_async_copy(slot_hbm, slot_ref, raw_sems.at[3]),
    ]
    for copy in copies + later:
        copy.start()
    chooser = x_chooser(nx, xb)
    for copy in copies:
        copy.wait()
    for ref in (near_ref, far_ref):
        ref[2 * ROWS * COLS] = jnp.zeros((yb, xb), jnp.float32)
        for half in range(ids_ref.shape[1] // xb):
            ref[2 * ROWS * COLS, half : half + 1, :] = ids_ref[:, half * xb : (half + 1) * xb].astype(jnp.float32)

    def put(f, at, p, j, value):
        (near_ref, far_ref)[at][tile(f, p, j)] = value

    spread(in_ref, chooser, rows_ref, put)
    for copy in later:
        copy.wait()


def prepare_inner_kernel(
    raw_ref, slot_ref, near_ref, far_ref,
    inner_ref, y_near_ref, y_far_ref, block_ref,
    rows_ref, slot_rows_ref,
):
    _, layers, cy, nx = raw_ref.shape
    cz = layers + 2
    yb, xb = cy // ROWS, nx // COLS
    chooser = x_chooser(nx, xb)

    def put(f, at, p, j, value):
        inner_ref[f, at, p, j] = value

    spread(raw_ref, chooser, rows_ref, put)
    put_y_edges(near_ref, far_ref, inner_ref, y_near_ref, y_far_ref)
    values = jnp.concatenate([slot_ref[place(layer, cz)] for layer in range(cz)], axis=0)
    values = values.astype(jnp.float32).astype(jnp.bfloat16)
    slot_rows_ref[...] = jnp.dot(values, chooser[:, :xb], preferred_element_type=jnp.float32)
    block_ref[...] = slot_rows_ref[pl.ds(0, cz * yb, stride=ROWS), :].astype(jnp.int32)


def chooser_kernel(block_ref, chooser_ref):
    rows, xb = block_ref.shape
    slots = chooser_ref.shape[2]
    one, zero = jnp.ones((), jnp.bfloat16), jnp.zeros((), jnp.bfloat16)
    across = lax.broadcasted_iota(jnp.int32, (xb, xb), 1)
    across = [(across + half * xb).astype(jnp.float32).astype(jnp.bfloat16) for half in range(slots // xb)]
    blocks = block_ref[...].astype(jnp.float32)
    turned = jnp.transpose(jnp.concatenate([blocks, jnp.zeros((xb - rows, xb), jnp.float32)], axis=0))
    for r in range(rows):
        at = (r % 2) * xb
        line = jnp.broadcast_to(turned[:, r : r + 1], (xb, xb)).astype(jnp.bfloat16)
        for half in range(slots // xb):
            chooser_ref[r // 2, at : at + xb, half * xb : (half + 1) * xb] = jnp.where(across[half] == line, one, zero)


def derived(e, q):
    sin_value, cos_value = sin_cos(q)
    square = e * e
    return cos_value, sin_value, square * cos_value, square * sin_value


def trig_kernel(near_ref, far_ref, inner_ref, trig_ref):
    cz = trig_ref.shape[1]
    for layer in range(cz):
        for p in range(ROWS):
            for j in range(COLS):
                if layer < 2:
                    e, q = ((near_ref, far_ref)[layer][tile(f, p, j)] for f in range(2))
                else:
                    e, q = (inner_ref[f, layer - 2, p, j] for f in range(2))
                for k, value in enumerate(derived(e, q)):
                    trig_ref[k, layer, p, j] = value


def beside(get, up, down, rim_ref, layer, k, p, j):
    here = get(k, p, j)
    yb, xb = here.shape
    row = lax.broadcasted_iota(jnp.int32, (yb, xb), 0)
    at = layer * COLS + j
    x_plus = get(k, p, j + 1) if j + 1 < COLS else pltpu.roll(get(k, p, 0), xb - 1, 1)
    x_minus = get(k, p, j - 1) if j > 0 else pltpu.roll(get(k, p, COLS - 1), 1, 1)
    if p + 1 < ROWS:
        y_plus = get(k, p + 1, j)
    else:
        y_plus = jnp.where(row == yb - 1, rim_ref[1, k, at : at + 1, :], pltpu.roll(get(k, 0, j), yb - 1, 0))
    if p > 0:
        y_minus = get(k, p - 1, j)
    else:
        y_minus = jnp.where(row == 0, rim_ref[0, k, at : at + 1, :], pltpu.roll(get(k, ROWS - 1, j), 1, 0))
    return x_plus, x_minus, y_plus, y_minus, up(k, p, j), down(k, p, j)


def gradients(side, z_half):
    halves = (0.5, 0.5, z_half)
    return [(side[2 * d] - side[2 * d + 1]) * halves[d] for d in range(3)]


def cell_densities(get, up, down, rim_ref, layer, z_half, p, j):
    sides = [beside(get, up, down, rim_ref, layer, k, p, j) for k in (0, 2, 3, 4, 5)]
    e, c, s = get(0, p, j), get(2, p, j), get(3, p, j)
    c_sum, s_sum, a_sum, b_sum = (sum(side) for side in sides[1:])
    misfit = 6.0 - c * c_sum - s * s_sum
    torque = c * b_sum - s * a_sum
    weight = e * misfit
    grads = gradients(sides[0], z_half)
    return [weight * g for g in grads] + [torque, 0.5 + e * e], weight, torque


def cell_locals(get, up, down, rim_ref, layer, z_half, p, j, weight, torque):
    e_side, q_side = (beside(get, up, down, rim_ref, layer, k, p, j) for k in range(2))
    e, q = get(0, p, j), get(1, p, j)
    laplace = sum(e_side) - 6.0 * e
    e_local = e + DIFFUSE * laplace + BARRIER * e * (1.0 - e) * (e - 0.5) - PENALTY * weight
    return [e_local, q + TORSION * torque] + gradients(e_side, z_half) + gradients(q_side, z_half)


def put_sums(totals, at, yb, sums_ref):
    rows = sums_ref.shape[0] // 16
    for k, value in enumerate(totals):
        for part, piece in enumerate(split3(value)):
            start = (part * 5 + k) * rows + at * yb
            sums_ref[start : start + yb, :] = piece.astype(jnp.float32)


def slot_sums(sums_ref, chooser_ref, first_pair):
    rows = sums_ref.shape[0] // 16
    sums_ref[15 * rows : 16 * rows, :] = jnp.zeros((rows, sums_ref.shape[1]), jnp.float32)
    acc = jnp.zeros((16, chooser_ref.shape[2]), jnp.float32)
    for i in range(rows // 2):
        left = jnp.concatenate(
            [sums_ref[pl.ds(2 * i + h, 16, stride=rows), :] for h in range(2)], axis=1
        ).astype(jnp.bfloat16)
        acc = acc + jnp.dot(left, chooser_ref[first_pair + i], preferred_element_type=jnp.float32)
    return acc


def inner_kernel(
    near_ref, far_ref, inner_ref, trig_ref, y_near_ref, y_far_ref, chooser_ref,
    rim_ref, local_ref, acc_ref, part_ref,
    sums_ref,
):
    _, cz, _, _, yb, xb = trig_ref.shape
    n = cz * COLS
    last = lax.axis_size("gy") - 1
    for side in range(2):
        inside = lax.axis_index("gy") != (0, last)[side]
        from_near = is_odd("gy") == 1 - side
        e, q = (
            jnp.where(
                inside, jnp.where(from_near, y_near_ref[f * n : f * n + n, :], y_far_ref[f * n : f * n + n, :]), 0.0
            )
            for f in range(2)
        )
        for k, value in enumerate((e, q) + derived(e, q)):
            rim_ref[side, k] = value

    def inner(at, k, p, j):
        return inner_ref[k, at, p, j] if k < 2 else trig_ref[k - 2, at + 2, p, j]

    def outer(top, k, p, j):
        is_near = is_odd("gz") == (0 if top else 1)
        if k < 2:
            return jnp.where(is_near, near_ref[tile(k, p, j)], far_ref[tile(k, p, j)])
        return trig_ref[k - 2, jnp.where(is_near, 0, 1), p, j]

    for at in range(cz - 2):
        get = functools.partial(inner, at)
        up = functools.partial(inner, at + 1) if at + 1 < cz - 2 else functools.partial(outer, True)
        down = functools.partial(inner, at - 1) if at > 0 else functools.partial(outer, False)
        totals = None
        for p in range(ROWS):
            for j in range(COLS):
                densities, weight, torque = cell_densities(get, up, down, rim_ref, at + 2, 0.5, p, j)
                totals = densities if totals is None else [a + b for a, b in zip(totals, densities)]
                local = cell_locals(get, up, down, rim_ref, at + 2, 0.5, p, j, weight, torque)
                for k, value in enumerate(local):
                    local_ref[k, at, p, j] = value
        put_sums(totals, at, yb, sums_ref)
    acc_ref[...] = slot_sums(sums_ref, chooser_ref, yb)

    get, _, inward = outer_getters(1, far_ref, inner_ref, trig_ref, None)
    for p in range(ROWS):
        for j in range(COLS):
            sides = [beside(get, inward, inward, rim_ref, 1, k, p, j)[:5] for k in (2, 3, 4, 5, 0)]
            grads = gradients(sides[4] + (sides[4][4],), 0.0)[:2]
            for k, value in enumerate([sum(side) for side in sides[:4]] + grads):
                part_ref[k, p, j] = value


def outer_getters(layer, own_ref, inner_ref, trig_ref, halo):
    beside_at = facing(layer, inner_ref.shape[1])

    def get(k, p, j):
        return own_ref[tile(k, p, j)] if k < 2 else trig_ref[k - 2, layer, p, j]

    def inward(k, p, j):
        return inner_ref[k, beside_at, p, j] if k < 2 else trig_ref[k - 2, beside_at + 2, p, j]

    return get, halo, inward


def outer_densities(layer, own_ref, inner_ref, trig_ref, rim_ref, halo_ref, chooser_ref, mixed_ref, trig_halo_ref, sums_ref):
    yb = trig_ref.shape[4]
    for p in range(ROWS):
        for j in range(COLS):
            for k, value in enumerate(derived(*(halo_ref[tile(f, p, j)] for f in range(2)))):
                trig_halo_ref[k, p, j] = value

    def halo(k, p, j):
        return halo_ref[tile(k, p, j)] if k < 2 else trig_halo_ref[k - 2, p, j]

    get, out, inward = outer_getters(layer, own_ref, inner_ref, trig_ref, halo)
    z_half = upward(layer)
    totals = None
    for p in range(ROWS):
        for j in range(COLS):
            densities, weight, torque = cell_densities(get, out, inward, rim_ref, layer, z_half, p, j)
            totals = densities if totals is None else [a + b for a, b in zip(totals, densities)]
            mixed_ref[0, p, j] = weight
            mixed_ref[1, p, j] = torque
    put_sums(totals, 0, yb, sums_ref)
    return slot_sums(sums_ref, chooser_ref, layer * yb // 2)


def near_kernel(
    near_ref, inner_ref, trig_ref, rim_ref, halo_ref, chooser_ref, before_ref,
    mixed_ref, acc_ref,
    trig_halo_ref, sums_ref,
):
    acc_ref[...] = before_ref[...] + outer_densities(
        0, near_ref, inner_ref, trig_ref, rim_ref, halo_ref, chooser_ref, mixed_ref, trig_halo_ref, sums_ref
    )


def far_kernel(
    far_ref, inner_ref, trig_ref, part_ref, halo_ref, chooser_ref, before_ref,
    mixed_ref, message_ref,
    sums_ref, acc_ref,
):
    yb = trig_ref.shape[4]
    get, _, inward = outer_getters(1, far_ref, inner_ref, trig_ref, None)
    z_half = upward(1)
    totals = None
    for p in range(ROWS):
        for j in range(COLS):
            e_out, q_out = (halo_ref[tile(f, p, j)] for f in range(2))
            c_sum, s_sum, a_sum, b_sum = (
                part_ref[k, p, j] + value for k, value in enumerate(derived(e_out, q_out))
            )
            e, c, s = get(0, p, j), get(2, p, j), get(3, p, j)
            weight = e * (6.0 - c * c_sum - s * s_sum)
            torque = c * b_sum - s * a_sum
            grads = [part_ref[4, p, j], part_ref[5, p, j], (e_out - inward(0, p, j)) * z_half]
            densities = [weight * g for g in grads] + [torque, 0.5 + e * e]
            totals = densities if totals is None else [x + y for x, y in zip(totals, densities)]
            mixed_ref[0, p, j] = weight
            mixed_ref[1, p, j] = torque
    put_sums(totals, 0, yb, sums_ref)
    acc_ref[...] = before_ref[...] + slot_sums(sums_ref, chooser_ref, yb // 2)
    message_ref[0:5, :] = acc_ref[0:5, :] + acc_ref[5:10, :] + acc_ref[10:15, :]
    message_ref[5:8, :] = jnp.zeros((3, message_ref.shape[1]), jnp.float32)


def outer_local_kernel(
    near_ref, far_ref, inner_ref, trig_ref, rim_ref, near_halo_ref, far_halo_ref, near_mixed_ref, far_mixed_ref, local_ref
):
    for layer in range(2):
        halo_ref = (near_halo_ref, far_halo_ref)[layer]
        mixed_ref = (near_mixed_ref, far_mixed_ref)[layer]

        def halo(k, p, j, halo_ref=halo_ref):
            return halo_ref[tile(k, p, j)]

        get, out, inward = outer_getters(layer, (near_ref, far_ref)[layer], inner_ref, trig_ref, halo)
        z_half = upward(layer)
        for p in range(ROWS):
            for j in range(COLS):
                local = cell_locals(
                    get, out, inward, rim_ref, layer, z_half, p, j, mixed_ref[0, p, j], mixed_ref[1, p, j]
                )
                for k, value in enumerate(local):
                    local_ref[k, layer, p, j] = value


def match_kernel(ids_ref, near_halo_ref, far_halo_ref, match_ref, back_ref):
    slots = ids_ref.shape[1]
    xb = near_halo_ref.shape[2]
    own = jnp.broadcast_to(ids_ref[...].astype(jnp.float32), (xb, slots))
    number = lax.broadcasted_iota(jnp.int32, (xb, slots), 0)
    for side, ref in enumerate((near_halo_ref, far_halo_ref)):
        where = jnp.full((1, slots), -1, jnp.int32)
        for half in range(slots // xb):
            line = ref[2 * ROWS * COLS, half : half + 1, :]
            other = jnp.transpose(jnp.broadcast_to(line, (xb, xb)))
            other = jnp.concatenate([other] * (slots // xb), axis=1)
            found = jnp.where(other == own, number + half * xb, -1)
            where = jnp.maximum(where, jnp.max(found, axis=0, keepdims=True))
        match_ref[side] = jnp.broadcast_to(where, (8, slots))
    back_ref[...] = x_chooser(back_ref.shape[0], xb, back=True)


def looked_up(tables, slot):
    lanes = slot.shape[1]
    within = slot & (lanes - 1)
    value = None
    for part, table in enumerate(tables):
        found = jnp.take_along_axis(table, within, axis=1, mode="promise_in_bounds")
        inside = (slot >= part * lanes) & (slot < (part + 1) * lanes)
        value = jnp.where(inside, found, 0.0 if value is None else value)
    return value


def slot_motion(message_ref, near_ref, far_ref, match_ref, velocity_ref, lanes):
    for start in range(0, message_ref.shape[1], lanes):
        at = slice(start, start + lanes)
        totals = message_ref[:, at]
        for side, ref in enumerate((near_ref, far_ref)):
            tables = [ref[:, part : part + lanes] for part in range(0, ref.shape[1], lanes)]
            totals = totals + looked_up(tables, match_ref[side, :, at])
        inverse = 1.0 / totals[4:5, :]
        velocity_ref[:, at] = TRANSLATE * totals * inverse


def motion_at(velocity_ref, slot):
    lanes = slot.shape[1]
    within = slot & (lanes - 1)
    motion = []
    for k in range(4):
        value = None
        for start in range(0, velocity_ref.shape[1], lanes):
            table = jnp.broadcast_to(velocity_ref[k : k + 1, start : start + lanes], slot.shape)
            found = jnp.take_along_axis(table, within, axis=1, mode="promise_in_bounds")
            value = found if value is None else jnp.where(slot >= start, found, value)
        motion.append(value)
    return motion


def layer_motion(velocity_ref, block_ref, layer, yb):
    return motion_at(velocity_ref, block_ref[layer * yb : (layer + 1) * yb, :])


def moved_on(local, motion):
    vx, vy, vz, turn = motion
    e = local[0] - (vx * local[2] + vy * local[3] + vz * local[4])
    q = local[1] + turn - (vx * local[5] + vy * local[6] + vz * local[7])
    return e, q


def advanced(local_ref, motion, at, p, j):
    return moved_on([local_ref[k, at, p, j] for k in range(8)], motion)


def advance_outer_kernel(
    message_ref, near_message_ref, far_message_ref, match_ref, block_ref, local_ref,
    velocity_ref, near_ref, far_ref,
):
    slot_motion(message_ref, near_message_ref, far_message_ref, match_ref, velocity_ref, block_ref.shape[1])
    for layer, ref in enumerate((near_ref, far_ref)):
        motion = layer_motion(velocity_ref, block_ref, layer, local_ref.shape[4])
        for p in range(ROWS):
            for j in range(COLS):
                ref[tile(0, p, j)], ref[tile(1, p, j)] = advanced(local_ref, motion, layer, p, j)


def advance_inner_kernel(
    velocity_ref, block_ref, local_ref, near_ref, far_ref,
    inner_ref, y_near_ref, y_far_ref,
):
    layers, yb = local_ref.shape[1], local_ref.shape[4]
    for at in range(layers):
        motion = layer_motion(velocity_ref, block_ref, at + 2, yb)
        for p in range(ROWS):
            for j in range(COLS):
                inner_ref[0, at, p, j], inner_ref[1, at, p, j] = advanced(local_ref, motion, at, p, j)
    put_y_edges(near_ref, far_ref, inner_ref, y_near_ref, y_far_ref)


def natural_kernel(outer_local_ref, inner_local_ref, back_ref, natural_ref, widen_ref, rows_ref):
    fields, cz, cy, nx = natural_ref.shape
    yb, xb = outer_local_ref.shape[4:]
    group = rows_ref.shape[0]
    x = lax.broadcasted_iota(jnp.int32, (xb, nx), 1)
    wide = jnp.where(x // COLS == lax.broadcasted_iota(jnp.int32, (xb, nx), 0), 1.0, 0.0).astype(jnp.bfloat16)
    for part in range(3):
        widen_ref[part * xb : (part + 1) * xb, :] = wide
    for first in range(0, fields, group):
        for f in range(group):
            for layer in range(cz):
                ref, inside = (outer_local_ref, layer) if layer < 2 else (inner_local_ref, layer - 2)
                for p in range(ROWS):
                    for j in range(COLS):
                        rows_ref[f, j, pl.ds(layer * cy + p, yb, stride=ROWS), :] = ref[first + f, inside, p, j]
        moved = exact_dot(
            jnp.concatenate(
                [jnp.concatenate([rows_ref[f, j] for j in range(COLS)], axis=1) for f in range(group)], axis=0
            ),
            back_ref[...],
        )
        for f in range(group):
            natural_ref[first + f] = moved[f * cz * cy : (f + 1) * cz * cy].reshape(cz, cy, nx)


def finish_kernel(
    message_ref, near_message_ref, far_message_ref, match_ref, block_ref, natural_ref, widen_ref,
    e_hbm, q_hbm,
    velocity_ref, rows_ref, out_ref, sems,
):
    _, cz, cy, nx = out_ref.shape
    xb = nx // COLS
    slot_motion(message_ref, near_message_ref, far_message_ref, match_ref, velocity_ref, xb)
    for layer in range(cz):
        for k, value in enumerate(layer_motion(velocity_ref, block_ref, layer, cy // ROWS)):
            for p in range(ROWS):
                rows_ref[pl.ds((layer * 4 + k) * cy + p, cy // ROWS, stride=ROWS), :] = value
    copies = []
    group = 1
    for first in range(0, cz, group):
        rows = rows_ref[first * 4 * cy : (first + group) * 4 * cy, :]
        wide = jnp.dot(jnp.concatenate(split3(rows), axis=1), widen_ref[...], preferred_element_type=jnp.float32)
        for layer in range(first, first + group):
            start = (layer - first) * 4
            motion = [wide[(start + k) * cy : (start + k + 1) * cy] for k in range(4)]
            out_ref[0, layer], out_ref[1, layer] = moved_on([natural_ref[k, layer] for k in range(8)], motion)
            for f, ref in enumerate((e_hbm, q_hbm)):
                copies.append(pltpu.make_async_copy(out_ref.at[f, layer], ref.at[place(layer, cz)], sems.at[f, layer]))
                copies[-1].start()
    for copy in copies:
        copy.wait()


VMEM = pl.BlockSpec(memory_space=pltpu.VMEM)
HBM = pl.BlockSpec(memory_space=pltpu.HBM)
MIB = 1024 * 1024


def call(kernel, name, outs, scratch=(), hbm_in=0, hbm_out=False, limit=24):
    def run(*args):
        return pl.pallas_call(
            kernel,
            name=name,
            in_specs=[HBM] * hbm_in + [VMEM] * (len(args) - hbm_in),
            out_specs=[HBM if hbm_out else VMEM] * len(outs),
            out_shape=[jax.ShapeDtypeStruct(shape, dtype) for shape, dtype in outs],
            scratch_shapes=list(scratch),
            compiler_params=pltpu.CompilerParams(vmem_limit_bytes=limit * MIB),
            cost_estimate=pl.CostEstimate(flops=4 * MIB, bytes_accessed=MIB, transcendentals=0),
        )(*args)

    return run


def swap(array, axis, far):
    size = lax.axis_size(axis)
    pairs = [(i, (((i + 1) ^ 1) - 1) % size if far else i ^ 1) for i in range(size)]
    return lax.ppermute(array, axis, pairs)


def both(near, far, axis):
    far = swap(far, axis, True)
    return swap(near, axis, False), far


def shards(order_param, orientation, cell_slot, tile_grains):
    cz, cy, nx = order_param.shape
    slots = tile_grains.shape[-1]
    yb, xb = cy // ROWS, nx // COLS
    rows = cz * yb
    f32, bf16 = jnp.float32, jnp.bfloat16
    block = (ROWS, COLS, yb, xb)
    side_out = ((2 * ROWS * COLS, yb, xb), f32)
    first_side_out = ((2 * ROWS * COLS + 1, yb, xb), f32)
    inner_out = ((2, cz - 2) + block, f32)
    y_out = [((2 * cz * COLS, xb), f32)] * 2
    acc_out = ((16, slots), f32)
    mixed_out = ((2,) + block, f32)
    layer_scratch = [pltpu.VMEM((4,) + block, f32), pltpu.VMEM((16 * yb, xb), f32)]
    dma = pltpu.SemaphoreType.DMA
    prepare_outer = call(
        prepare_outer_kernel, "prepare_outer",
        [
            first_side_out, first_side_out, ((2, cz - 2, cy, nx), f32),
            ((cz, cy, nx), jnp.int32), ((1, slots), jnp.int32),
        ],
        [pltpu.VMEM((2, 2, cy, nx), f32), pltpu.VMEM((COLS, 4 * cy, xb), f32), dma((2, 2)), dma((4,))],
        hbm_in=4,
    )
    prepare_inner = call(
        prepare_inner_kernel, "prepare_inner", [inner_out] + y_out + [((rows, xb), jnp.int32)],
        [pltpu.VMEM((COLS, 2 * (cz - 2) * cy, xb), f32), pltpu.VMEM((cz * cy, xb), f32)],
    )
    choosers = call(chooser_kernel, "choosers", [((rows // 2, 2 * xb, slots), bf16)])
    trigs = call(trig_kernel, "trigs", [((4, cz) + block, f32)])
    inner_terms = call(
        inner_kernel, "inner_terms", [((2, 6, cz * COLS, xb), f32), ((8, cz - 2) + block, f32), acc_out, ((6,) + block, f32)],
        [pltpu.VMEM((16 * (cz - 2) * yb, xb), f32)],
    )
    near_terms = call(near_kernel, "near_terms", [mixed_out, acc_out], layer_scratch)
    far_terms = call(
        far_kernel, "far_terms", [mixed_out, ((8, slots), f32)], [layer_scratch[1], pltpu.VMEM((16, slots), f32)]
    )
    outer_locals = call(outer_local_kernel, "outer_locals", [((8, 2) + block, f32)])
    matches = call(match_kernel, "matches", [((2, 8, slots), jnp.int32), ((nx, nx), bf16)])
    advance_outer = call(
        advance_outer_kernel, "advance_outer", [((8, slots), f32), side_out, side_out]
    )
    advance_inner = call(advance_inner_kernel, "advance_inner", [inner_out] + y_out)
    naturals = call(
        natural_kernel, "naturals", [((8, cz, cy, nx), f32), ((3 * xb, nx), bf16)], [pltpu.VMEM((2, COLS, cz * cy, xb), f32)]
    )
    finish = call(
        finish_kernel, "finish", [((cz, cy, nx), f32)] * 2,
        [pltpu.VMEM((8, slots), f32), pltpu.VMEM((4 * cz * cy, xb), f32), pltpu.VMEM((2, cz, cy, nx), f32), dma((2, cz))],
        hbm_out=True,
    )

    inputs = (order_param, orientation, cell_slot, tile_grains.reshape(1, slots))
    near, far, raw, raw_slots, ids = prepare_outer(
        *(pltpu.with_memory_space_constraint(array, pltpu.HBM) for array in inputs)
    )
    for step in range(STEPS):
        near_halo, far_halo = both(near, far, "gz")
        if step == 0:
            inner, y_near, y_far, blocks = prepare_inner(raw, raw_slots, near, far)
        else:
            inner, y_near, y_far = advance_inner(velocity, blocks, inner_local, near, far)
        y_near, y_far = both(y_near, y_far, "gy")
        if step == 0:
            (chooser,) = choosers(blocks)
        (trig,) = trigs(near, far, inner)
        rim, inner_local, acc, part = inner_terms(near, far, inner, trig, y_near, y_far, chooser)
        near_mixed, acc = near_terms(near, inner, trig, rim, near_halo, chooser, acc)
        far_mixed, message = far_terms(far, inner, trig, part, far_halo, chooser, acc)
        near_message, far_message = both(message, message, "gz")
        if step == 0:
            match, back = matches(ids, near_halo, far_halo)
        (outer_local,) = outer_locals(near, far, inner, trig, rim, near_halo, far_halo, near_mixed, far_mixed)
        if step < STEPS - 1:
            velocity, near, far = advance_outer(message, near_message, far_message, match, blocks, outer_local)
    natural, widen = naturals(outer_local, inner_local, back)
    return tuple(finish(message, near_message, far_message, match, blocks, natural, widen))


def solution(mesh):
    spec = P("gz", "gy", None)
    return jax.shard_map(shards, mesh=mesh, in_specs=(spec,) * 4, out_specs=(spec,) * 2, check_vma=False)
```

```python
import functools

import jax
import jax.numpy as jnp
from jax import lax
from jax.experimental import pallas as pl
from jax.experimental.pallas import tpu as pltpu
from jax.sharding import PartitionSpec as P

STEPS = 3

DIFFUSE = 0.1
BARRIER = 0.5
PENALTY = 0.05
TORSION = 0.1
TRANSLATE = 2.0
ROTATE = 2.0

ROWS = 2
COLS = 4


def split3(value):
    high = value.astype(jnp.bfloat16)
    rest = value - high.astype(jnp.float32)
    middle = rest.astype(jnp.bfloat16)
    low = (rest - middle.astype(jnp.float32)).astype(jnp.bfloat16)
    return high, middle, low


def exact_dot(value, chooser):
    rows = value.shape[0]
    parts = jnp.dot(jnp.concatenate(split3(value), axis=0), chooser, preferred_element_type=jnp.float32)
    return parts[:rows] + parts[rows : 2 * rows] + parts[2 * rows :]


def sin_cos(angle):
    turns = jnp.floor(angle * 0.6366197723675814 + 0.5)
    rest = angle - turns * 1.5703125
    rest = rest - turns * 4.837512969970703125e-4
    rest = rest - turns * 7.54978995489188216e-8
    square = rest * rest
    sine = ((-1.9515295891e-4 * square + 8.3321608736e-3) * square - 1.6666654611e-1) * square * rest + rest
    cosine = ((2.443315711809948e-5 * square - 1.388731625493765e-3) * square + 4.166664568298827e-2) * square * square
    cosine = cosine - 0.5 * square + 1.0
    quarter = turns.astype(jnp.int32)
    odd = (quarter & 1) == 1
    sin_value = jnp.where(odd, cosine, sine)
    cos_value = jnp.where(odd, sine, cosine)
    sin_value = jnp.where((quarter & 2) == 2, -sin_value, sin_value)
    cos_value = jnp.where(((quarter + 1) & 2) == 2, -cos_value, cos_value)
    return sin_value, cos_value


def is_odd(axis):
    return lax.axis_index(axis) & 1


def place(layer, cz):
    odd = is_odd("gz")
    if layer == 0:
        return (1 - odd) * (cz - 1)
    if layer == 1:
        return odd * (cz - 1)
    return layer - 1


def facing(layer, layers):
    odd = is_odd("gz")
    return ((1 - odd) if layer == 0 else odd) * (layers - 1)


def upward(layer):
    half = 0.5 - is_odd("gz").astype(jnp.float32)
    return half if layer == 0 else -half


def tile(f, p, j):
    return (f * ROWS + p) * COLS + j


def put_y_edges(near_ref, far_ref, inner_ref, y_near_ref, y_far_ref):
    layers, yb = inner_ref.shape[1], inner_ref.shape[4]
    cz = layers + 2
    first_to_near = is_odd("gy") == 1
    for f in range(2):
        for layer in range(cz):
            for j in range(COLS):
                at = (f * cz + layer) * COLS + j
                if layer < 2:
                    ref = (near_ref, far_ref)[layer]
                    first, last = ref[tile(f, 0, j), 0:1], ref[tile(f, ROWS - 1, j), yb - 1 : yb]
                else:
                    first = inner_ref[f, layer - 2, 0, j, 0:1]
                    last = inner_ref[f, layer - 2, ROWS - 1, j, yb - 1 : yb]
                y_near_ref[at : at + 1, :] = jnp.where(first_to_near, first, last)
                y_far_ref[at : at + 1, :] = jnp.where(first_to_near, last, first)


def x_chooser(nx, xb, back=False):
    first = lax.broadcasted_iota(jnp.int32, (nx, nx), 1 if back else 0)
    second = lax.broadcasted_iota(jnp.int32, (nx, nx), 0 if back else 1)
    return jnp.where(first == COLS * (second & (xb - 1)) + (second >> (xb.bit_length() - 1)), 1.0, 0.0).astype(jnp.bfloat16)


def spread(in_ref, chooser, rows_ref, put):
    _, layers, cy, nx = in_ref.shape
    yb, xb = cy // ROWS, nx // COLS
    moved = exact_dot(in_ref[...].reshape(2 * layers * cy, nx), chooser)
    for j in range(COLS):
        rows_ref[j] = moved[:, j * xb : (j + 1) * xb]
    for f in range(2):
        for at in range(layers):
            for p in range(ROWS):
                for j in range(COLS):
                    start = (f * layers + at) * cy + p
                    put(f, at, p, j, rows_ref[j, pl.ds(start, yb, stride=ROWS), :])


def prepare_outer_kernel(
    e_hbm, q_hbm, slot_hbm, ids_hbm,
    near_ref, far_ref, raw_ref, slot_ref, ids_ref,
    in_ref, rows_ref, sems, raw_sems,
):
    cz = e_hbm.shape[0]
    _, _, cy, nx = in_ref.shape
    yb, xb = cy // ROWS, nx // COLS
    copies = [
        pltpu.make_async_copy(ref.at[place(at, cz)], in_ref.at[f, at], sems.at[f, at])
        for f, ref in enumerate((e_hbm, q_hbm))
        for at in range(2)
    ]
    copies.append(pltpu.make_async_copy(ids_hbm, ids_ref, raw_sems.at[0]))
    later = [
        pltpu.make_async_copy(e_hbm.at[1 : cz - 1], raw_ref.at[0], raw_sems.at[1]),
        pltpu.make_async_copy(q_hbm.at[1 : cz - 1], raw_ref.at[1], raw_sems.at[2]),
        pltpu.make_async_copy(slot_hbm, slot_ref, raw_sems.at[3]),
    ]
    for copy in copies:
        copy.start()
    for copy in later:
        copy.start(priority=1)
    chooser = x_chooser(nx, xb)
    for copy in copies:
        copy.wait()
    for ref in (near_ref, far_ref):
        ref[2 * ROWS * COLS] = jnp.zeros((yb, xb), jnp.float32)
        for half in range(ids_ref.shape[1] // xb):
            ref[2 * ROWS * COLS, half : half + 1, :] = ids_ref[:, half * xb : (half + 1) * xb].astype(jnp.float32)

    def put(f, at, p, j, value):
        (near_ref, far_ref)[at][tile(f, p, j)] = value

    spread(in_ref, chooser, rows_ref, put)
    for copy in later:
        copy.wait()


def prepare_inner_kernel(
    raw_ref, slot_ref, near_ref, far_ref,
    inner_ref, y_near_ref, y_far_ref, block_ref,
    rows_ref, slot_rows_ref,
):
    _, layers, cy, nx = raw_ref.shape
    cz = layers + 2
    yb, xb = cy // ROWS, nx // COLS
    chooser = x_chooser(nx, xb)

    def put(f, at, p, j, value):
        inner_ref[f, at, p, j] = value

    spread(raw_ref, chooser, rows_ref, put)
    put_y_edges(near_ref, far_ref, inner_ref, y_near_ref, y_far_ref)
    values = jnp.concatenate([slot_ref[place(layer, cz)] for layer in range(cz)], axis=0)
    values = values.astype(jnp.float32).astype(jnp.bfloat16)
    slot_rows_ref[...] = jnp.dot(values, chooser[:, :xb], preferred_element_type=jnp.float32)
    block_ref[...] = slot_rows_ref[pl.ds(0, cz * yb, stride=ROWS), :].astype(jnp.int32)


def chooser_kernel(block_ref, chooser_ref):
    rows, xb = block_ref.shape
    slots = chooser_ref.shape[2]
    one, zero = jnp.ones((), jnp.bfloat16), jnp.zeros((), jnp.bfloat16)
    across = lax.broadcasted_iota(jnp.int32, (xb, xb), 1)
    across = [(across + half * xb).astype(jnp.float32).astype(jnp.bfloat16) for half in range(slots // xb)]
    blocks = block_ref[...].astype(jnp.float32)
    turned = jnp.transpose(jnp.concatenate([blocks, jnp.zeros((xb - rows, xb), jnp.float32)], axis=0))
    for r in range(rows):
        at = (r % 2) * xb
        line = jnp.broadcast_to(turned[:, r : r + 1], (xb, xb)).astype(jnp.bfloat16)
        for half in range(slots // xb):
            chooser_ref[r // 2, at : at + xb, half * xb : (half + 1) * xb] = jnp.where(across[half] == line, one, zero)


def derived(e, q):
    sin_value, cos_value = sin_cos(q)
    square = e * e
    return cos_value, sin_value, square * cos_value, square * sin_value


def trig_kernel(near_ref, far_ref, inner_ref, trig_ref):
    cz = trig_ref.shape[1]
    for layer in range(cz):
        for p in range(ROWS):
            for j in range(COLS):
                if layer < 2:
                    e, q = ((near_ref, far_ref)[layer][tile(f, p, j)] for f in range(2))
                else:
                    e, q = (inner_ref[f, layer - 2, p, j] for f in range(2))
                for k, value in enumerate(derived(e, q)):
                    trig_ref[k, layer, p, j] = value


def beside(get, up, down, rim_ref, layer, k, p, j):
    here = get(k, p, j)
    yb, xb = here.shape
    row = lax.broadcasted_iota(jnp.int32, (yb, xb), 0)
    at = layer * COLS + j
    x_plus = get(k, p, j + 1) if j + 1 < COLS else pltpu.roll(get(k, p, 0), xb - 1, 1)
    x_minus = get(k, p, j - 1) if j > 0 else pltpu.roll(get(k, p, COLS - 1), 1, 1)
    if p + 1 < ROWS:
        y_plus = get(k, p + 1, j)
    else:
        y_plus = jnp.where(row == yb - 1, rim_ref[1, k, at : at + 1, :], pltpu.roll(get(k, 0, j), yb - 1, 0))
    if p > 0:
        y_minus = get(k, p - 1, j)
    else:
        y_minus = jnp.where(row == 0, rim_ref[0, k, at : at + 1, :], pltpu.roll(get(k, ROWS - 1, j), 1, 0))
    return x_plus, x_minus, y_plus, y_minus, up(k, p, j), down(k, p, j)


def gradients(side, z_half):
    halves = (0.5, 0.5, z_half)
    return [(side[2 * d] - side[2 * d + 1]) * halves[d] for d in range(3)]


def cell_densities(get, up, down, rim_ref, layer, z_half, p, j):
    sides = [beside(get, up, down, rim_ref, layer, k, p, j) for k in (0, 2, 3, 4, 5)]
    e, c, s = get(0, p, j), get(2, p, j), get(3, p, j)
    c_sum, s_sum, a_sum, b_sum = (sum(side) for side in sides[1:])
    misfit = 6.0 - c * c_sum - s * s_sum
    torque = c * b_sum - s * a_sum
    weight = e * misfit
    grads = gradients(sides[0], z_half)
    return [weight * g for g in grads] + [torque, 0.5 + e * e], weight, torque


def cell_locals(get, up, down, rim_ref, layer, z_half, p, j, weight, torque):
    e_side, q_side = (beside(get, up, down, rim_ref, layer, k, p, j) for k in range(2))
    e, q = get(0, p, j), get(1, p, j)
    laplace = sum(e_side) - 6.0 * e
    e_local = e + DIFFUSE * laplace + BARRIER * e * (1.0 - e) * (e - 0.5) - PENALTY * weight
    return [e_local, q + TORSION * torque] + gradients(e_side, z_half) + gradients(q_side, z_half)


def put_sums(totals, at, yb, sums_ref):
    rows = sums_ref.shape[0] // 16
    for k, value in enumerate(totals):
        for part, piece in enumerate(split3(value)):
            start = (part * 5 + k) * rows + at * yb
            sums_ref[start : start + yb, :] = piece.astype(jnp.float32)


def slot_sums(sums_ref, chooser_ref, first_pair):
    rows = sums_ref.shape[0] // 16
    sums_ref[15 * rows : 16 * rows, :] = jnp.zeros((rows, sums_ref.shape[1]), jnp.float32)
    acc = jnp.zeros((16, chooser_ref.shape[2]), jnp.float32)
    for i in range(rows // 2):
        left = jnp.concatenate(
            [sums_ref[pl.ds(2 * i + h, 16, stride=rows), :] for h in range(2)], axis=1
        ).astype(jnp.bfloat16)
        acc = acc + jnp.dot(left, chooser_ref[first_pair + i], preferred_element_type=jnp.float32)
    return acc


def inner_kernel(
    near_ref, far_ref, inner_ref, trig_ref, y_near_ref, y_far_ref, chooser_ref,
    rim_ref, local_ref, acc_ref, part_ref,
    sums_ref,
):
    _, cz, _, _, yb, xb = trig_ref.shape
    n = cz * COLS
    last = lax.axis_size("gy") - 1
    for side in range(2):
        inside = lax.axis_index("gy") != (0, last)[side]
        from_near = is_odd("gy") == 1 - side
        e, q = (
            jnp.where(
                inside, jnp.where(from_near, y_near_ref[f * n : f * n + n, :], y_far_ref[f * n : f * n + n, :]), 0.0
            )
            for f in range(2)
        )
        for k, value in enumerate((e, q) + derived(e, q)):
            rim_ref[side, k] = value

    def inner(at, k, p, j):
        return inner_ref[k, at, p, j] if k < 2 else trig_ref[k - 2, at + 2, p, j]

    def outer(top, k, p, j):
        is_near = is_odd("gz") == (0 if top else 1)
        if k < 2:
            return jnp.where(is_near, near_ref[tile(k, p, j)], far_ref[tile(k, p, j)])
        return trig_ref[k - 2, jnp.where(is_near, 0, 1), p, j]

    for at in range(cz - 2):
        get = functools.partial(inner, at)
        up = functools.partial(inner, at + 1) if at + 1 < cz - 2 else functools.partial(outer, True)
        down = functools.partial(inner, at - 1) if at > 0 else functools.partial(outer, False)
        totals = None
        for p in range(ROWS):
            for j in range(COLS):
                densities, weight, torque = cell_densities(get, up, down, rim_ref, at + 2, 0.5, p, j)
                totals = densities if totals is None else [a + b for a, b in zip(totals, densities)]
                local = cell_locals(get, up, down, rim_ref, at + 2, 0.5, p, j, weight, torque)
                for k, value in enumerate(local):
                    local_ref[k, at, p, j] = value
        put_sums(totals, at, yb, sums_ref)
    acc_ref[...] = slot_sums(sums_ref, chooser_ref, yb)

    get, _, inward = outer_getters(1, far_ref, inner_ref, trig_ref, None)
    for p in range(ROWS):
        for j in range(COLS):
            sides = [beside(get, inward, inward, rim_ref, 1, k, p, j)[:5] for k in (2, 3, 4, 5, 0)]
            grads = gradients(sides[4] + (sides[4][4],), 0.0)[:2]
            for k, value in enumerate([sum(side) for side in sides[:4]] + grads):
                part_ref[k, p, j] = value


def outer_getters(layer, own_ref, inner_ref, trig_ref, halo):
    beside_at = facing(layer, inner_ref.shape[1])

    def get(k, p, j):
        return own_ref[tile(k, p, j)] if k < 2 else trig_ref[k - 2, layer, p, j]

    def inward(k, p, j):
        return inner_ref[k, beside_at, p, j] if k < 2 else trig_ref[k - 2, beside_at + 2, p, j]

    return get, halo, inward


def outer_densities(layer, own_ref, inner_ref, trig_ref, rim_ref, halo_ref, chooser_ref, mixed_ref, trig_halo_ref, sums_ref):
    yb = trig_ref.shape[4]
    for p in range(ROWS):
        for j in range(COLS):
            for k, value in enumerate(derived(*(halo_ref[tile(f, p, j)] for f in range(2)))):
                trig_halo_ref[k, p, j] = value

    def halo(k, p, j):
        return halo_ref[tile(k, p, j)] if k < 2 else trig_halo_ref[k - 2, p, j]

    get, out, inward = outer_getters(layer, own_ref, inner_ref, trig_ref, halo)
    z_half = upward(layer)
    totals = None
    for p in range(ROWS):
        for j in range(COLS):
            densities, weight, torque = cell_densities(get, out, inward, rim_ref, layer, z_half, p, j)
            totals = densities if totals is None else [a + b for a, b in zip(totals, densities)]
            mixed_ref[0, p, j] = weight
            mixed_ref[1, p, j] = torque
    put_sums(totals, 0, yb, sums_ref)
    return slot_sums(sums_ref, chooser_ref, layer * yb // 2)


def near_kernel(
    near_ref, inner_ref, trig_ref, rim_ref, halo_ref, chooser_ref, before_ref,
    mixed_ref, acc_ref,
    trig_halo_ref, sums_ref,
):
    acc_ref[...] = before_ref[...] + outer_densities(
        0, near_ref, inner_ref, trig_ref, rim_ref, halo_ref, chooser_ref, mixed_ref, trig_halo_ref, sums_ref
    )


def far_kernel(
    far_ref, inner_ref, trig_ref, part_ref, halo_ref, chooser_ref, before_ref,
    mixed_ref, message_ref,
    sums_ref, acc_ref,
):
    yb = trig_ref.shape[4]
    get, _, inward = outer_getters(1, far_ref, inner_ref, trig_ref, None)
    z_half = upward(1)
    totals = None
    for p in range(ROWS):
        for j in range(COLS):
            e_out, q_out = (halo_ref[tile(f, p, j)] for f in range(2))
            c_sum, s_sum, a_sum, b_sum = (
                part_ref[k, p, j] + value for k, value in enumerate(derived(e_out, q_out))
            )
            e, c, s = get(0, p, j), get(2, p, j), get(3, p, j)
            weight = e * (6.0 - c * c_sum - s * s_sum)
            torque = c * b_sum - s * a_sum
            grads = [part_ref[4, p, j], part_ref[5, p, j], (e_out - inward(0, p, j)) * z_half]
            densities = [weight * g for g in grads] + [torque, 0.5 + e * e]
            totals = densities if totals is None else [x + y for x, y in zip(totals, densities)]
            mixed_ref[0, p, j] = weight
            mixed_ref[1, p, j] = torque
    put_sums(totals, 0, yb, sums_ref)
    acc_ref[...] = before_ref[...] + slot_sums(sums_ref, chooser_ref, yb // 2)
    message_ref[0:5, :] = acc_ref[0:5, :] + acc_ref[5:10, :] + acc_ref[10:15, :]
    message_ref[5:8, :] = jnp.zeros((3, message_ref.shape[1]), jnp.float32)


def outer_local_kernel(
    near_ref, far_ref, inner_ref, trig_ref, rim_ref, near_halo_ref, far_halo_ref, near_mixed_ref, far_mixed_ref, local_ref
):
    for layer in range(2):
        halo_ref = (near_halo_ref, far_halo_ref)[layer]
        mixed_ref = (near_mixed_ref, far_mixed_ref)[layer]

        def halo(k, p, j, halo_ref=halo_ref):
            return halo_ref[tile(k, p, j)]

        get, out, inward = outer_getters(layer, (near_ref, far_ref)[layer], inner_ref, trig_ref, halo)
        z_half = upward(layer)
        for p in range(ROWS):
            for j in range(COLS):
                local = cell_locals(
                    get, out, inward, rim_ref, layer, z_half, p, j, mixed_ref[0, p, j], mixed_ref[1, p, j]
                )
                for k, value in enumerate(local):
                    local_ref[k, layer, p, j] = value


def match_kernel(ids_ref, near_halo_ref, far_halo_ref, match_ref, back_ref):
    slots = ids_ref.shape[1]
    xb = near_halo_ref.shape[2]
    own = jnp.broadcast_to(ids_ref[...].astype(jnp.float32), (xb, slots))
    number = lax.broadcasted_iota(jnp.int32, (xb, slots), 0)
    for side, ref in enumerate((near_halo_ref, far_halo_ref)):
        where = jnp.full((1, slots), -1, jnp.int32)
        for half in range(slots // xb):
            line = ref[2 * ROWS * COLS, half : half + 1, :]
            other = jnp.transpose(jnp.broadcast_to(line, (xb, xb)))
            other = jnp.concatenate([other] * (slots // xb), axis=1)
            found = jnp.where(other == own, number + half * xb, -1)
            where = jnp.maximum(where, jnp.max(found, axis=0, keepdims=True))
        match_ref[side] = jnp.broadcast_to(where, (8, slots))
    back_ref[...] = x_chooser(back_ref.shape[0], xb, back=True)


def looked_up(tables, slot):
    lanes = slot.shape[1]
    within = slot & (lanes - 1)
    value = None
    for part, table in enumerate(tables):
        found = jnp.take_along_axis(table, within, axis=1, mode="promise_in_bounds")
        inside = (slot >= part * lanes) & (slot < (part + 1) * lanes)
        value = jnp.where(inside, found, 0.0 if value is None else value)
    return value


def slot_motion(message_ref, near_ref, far_ref, match_ref, velocity_ref, lanes):
    for start in range(0, message_ref.shape[1], lanes):
        at = slice(start, start + lanes)
        totals = message_ref[:, at]
        for side, ref in enumerate((near_ref, far_ref)):
            tables = [ref[:, part : part + lanes] for part in range(0, ref.shape[1], lanes)]
            totals = totals + looked_up(tables, match_ref[side, :, at])
        inverse = 1.0 / totals[4:5, :]
        velocity_ref[:, at] = TRANSLATE * totals * inverse


def motion_at(velocity_ref, slot):
    lanes = slot.shape[1]
    within = slot & (lanes - 1)
    motion = []
    for k in range(4):
        value = None
        for start in range(0, velocity_ref.shape[1], lanes):
            table = jnp.broadcast_to(velocity_ref[k : k + 1, start : start + lanes], slot.shape)
            found = jnp.take_along_axis(table, within, axis=1, mode="promise_in_bounds")
            value = found if value is None else jnp.where(slot >= start, found, value)
        motion.append(value)
    return motion


def layer_motion(velocity_ref, block_ref, layer, yb):
    return motion_at(velocity_ref, block_ref[layer * yb : (layer + 1) * yb, :])


def moved_on(local, motion):
    vx, vy, vz, turn = motion
    e = local[0] - (vx * local[2] + vy * local[3] + vz * local[4])
    q = local[1] + turn - (vx * local[5] + vy * local[6] + vz * local[7])
    return e, q


def advanced(local_ref, motion, at, p, j):
    return moved_on([local_ref[k, at, p, j] for k in range(8)], motion)


def advance_outer_kernel(
    message_ref, near_message_ref, far_message_ref, match_ref, block_ref, local_ref,
    velocity_ref, near_ref, far_ref,
):
    slot_motion(message_ref, near_message_ref, far_message_ref, match_ref, velocity_ref, block_ref.shape[1])
    for layer, ref in enumerate((near_ref, far_ref)):
        motion = layer_motion(velocity_ref, block_ref, layer, local_ref.shape[4])
        for p in range(ROWS):
            for j in range(COLS):
                ref[tile(0, p, j)], ref[tile(1, p, j)] = advanced(local_ref, motion, layer, p, j)


def advance_inner_kernel(
    velocity_ref, block_ref, local_ref, near_ref, far_ref,
    inner_ref, y_near_ref, y_far_ref,
):
    layers, yb = local_ref.shape[1], local_ref.shape[4]
    for at in range(layers):
        motion = layer_motion(velocity_ref, block_ref, at + 2, yb)
        for p in range(ROWS):
            for j in range(COLS):
                inner_ref[0, at, p, j], inner_ref[1, at, p, j] = advanced(local_ref, motion, at, p, j)
    put_y_edges(near_ref, far_ref, inner_ref, y_near_ref, y_far_ref)


def natural_kernel(outer_local_ref, inner_local_ref, back_ref, natural_ref, widen_ref, rows_ref):
    fields, cz, cy, nx = natural_ref.shape
    yb, xb = outer_local_ref.shape[4:]
    group = rows_ref.shape[0]
    x = lax.broadcasted_iota(jnp.int32, (xb, nx), 1)
    wide = jnp.where(x // COLS == lax.broadcasted_iota(jnp.int32, (xb, nx), 0), 1.0, 0.0).astype(jnp.bfloat16)
    for part in range(3):
        widen_ref[part * xb : (part + 1) * xb, :] = wide
    for first in range(0, fields, group):
        for f in range(group):
            for layer in range(cz):
                ref, inside = (outer_local_ref, layer) if layer < 2 else (inner_local_ref, layer - 2)
                for p in range(ROWS):
                    for j in range(COLS):
                        rows_ref[f, j, pl.ds(layer * cy + p, yb, stride=ROWS), :] = ref[first + f, inside, p, j]
        moved = exact_dot(
            jnp.concatenate(
                [jnp.concatenate([rows_ref[f, j] for j in range(COLS)], axis=1) for f in range(group)], axis=0
            ),
            back_ref[...],
        )
        for f in range(group):
            natural_ref[first + f] = moved[f * cz * cy : (f + 1) * cz * cy].reshape(cz, cy, nx)


def finish_kernel(
    message_ref, near_message_ref, far_message_ref, match_ref, block_ref, natural_ref, widen_ref,
    e_hbm, q_hbm,
    velocity_ref, rows_ref, out_ref, sems,
):
    _, cz, cy, nx = out_ref.shape
    xb = nx // COLS
    slot_motion(message_ref, near_message_ref, far_message_ref, match_ref, velocity_ref, xb)
    for layer in range(cz):
        for k, value in enumerate(layer_motion(velocity_ref, block_ref, layer, cy // ROWS)):
            for p in range(ROWS):
                rows_ref[pl.ds((layer * 4 + k) * cy + p, cy // ROWS, stride=ROWS), :] = value
    copies = []
    group = 1
    for first in range(0, cz, group):
        rows = rows_ref[first * 4 * cy : (first + group) * 4 * cy, :]
        wide = jnp.dot(jnp.concatenate(split3(rows), axis=1), widen_ref[...], preferred_element_type=jnp.float32)
        for layer in range(first, first + group):
            start = (layer - first) * 4
            motion = [wide[(start + k) * cy : (start + k + 1) * cy] for k in range(4)]
            out_ref[0, layer], out_ref[1, layer] = moved_on([natural_ref[k, layer] for k in range(8)], motion)
            for f, ref in enumerate((e_hbm, q_hbm)):
                copies.append(pltpu.make_async_copy(out_ref.at[f, layer], ref.at[place(layer, cz)], sems.at[f, layer]))
                copies[-1].start()
    for copy in copies:
        copy.wait()


VMEM = pl.BlockSpec(memory_space=pltpu.VMEM)
HBM = pl.BlockSpec(memory_space=pltpu.HBM)
MIB = 1024 * 1024


def call(kernel, name, outs, scratch=(), hbm_in=0, hbm_out=False, limit=24):
    def run(*args):
        return pl.pallas_call(
            kernel,
            name=name,
            in_specs=[HBM] * hbm_in + [VMEM] * (len(args) - hbm_in),
            out_specs=[HBM if hbm_out else VMEM] * len(outs),
            out_shape=[jax.ShapeDtypeStruct(shape, dtype) for shape, dtype in outs],
            scratch_shapes=list(scratch),
            compiler_params=pltpu.CompilerParams(vmem_limit_bytes=limit * MIB),
            cost_estimate=pl.CostEstimate(flops=4 * MIB, bytes_accessed=MIB, transcendentals=0),
        )(*args)

    return run


def swap(array, axis, far):
    size = lax.axis_size(axis)
    pairs = [(i, (((i + 1) ^ 1) - 1) % size if far else i ^ 1) for i in range(size)]
    return lax.ppermute(array, axis, pairs)


def both(near, far, axis):
    far = swap(far, axis, True)
    return swap(near, axis, False), far


def shards(order_param, orientation, cell_slot, tile_grains):
    cz, cy, nx = order_param.shape
    slots = tile_grains.shape[-1]
    yb, xb = cy // ROWS, nx // COLS
    rows = cz * yb
    f32, bf16 = jnp.float32, jnp.bfloat16
    block = (ROWS, COLS, yb, xb)
    side_out = ((2 * ROWS * COLS, yb, xb), f32)
    first_side_out = ((2 * ROWS * COLS + 1, yb, xb), f32)
    inner_out = ((2, cz - 2) + block, f32)
    y_out = [((2 * cz * COLS, xb), f32)] * 2
    acc_out = ((16, slots), f32)
    mixed_out = ((2,) + block, f32)
    layer_scratch = [pltpu.VMEM((4,) + block, f32), pltpu.VMEM((16 * yb, xb), f32)]
    dma = pltpu.SemaphoreType.DMA
    prepare_outer = call(
        prepare_outer_kernel, "prepare_outer",
        [
            first_side_out, first_side_out, ((2, cz - 2, cy, nx), f32),
            ((cz, cy, nx), jnp.int32), ((1, slots), jnp.int32),
        ],
        [pltpu.VMEM((2, 2, cy, nx), f32), pltpu.VMEM((COLS, 4 * cy, xb), f32), dma((2, 2)), dma((4,))],
        hbm_in=4,
    )
    prepare_inner = call(
        prepare_inner_kernel, "prepare_inner", [inner_out] + y_out + [((rows, xb), jnp.int32)],
        [pltpu.VMEM((COLS, 2 * (cz - 2) * cy, xb), f32), pltpu.VMEM((cz * cy, xb), f32)],
    )
    choosers = call(chooser_kernel, "choosers", [((rows // 2, 2 * xb, slots), bf16)])
    trigs = call(trig_kernel, "trigs", [((4, cz) + block, f32)])
    inner_terms = call(
        inner_kernel, "inner_terms", [((2, 6, cz * COLS, xb), f32), ((8, cz - 2) + block, f32), acc_out, ((6,) + block, f32)],
        [pltpu.VMEM((16 * (cz - 2) * yb, xb), f32)],
    )
    near_terms = call(near_kernel, "near_terms", [mixed_out, acc_out], layer_scratch)
    far_terms = call(
        far_kernel, "far_terms", [mixed_out, ((8, slots), f32)], [layer_scratch[1], pltpu.VMEM((16, slots), f32)]
    )
    outer_locals = call(outer_local_kernel, "outer_locals", [((8, 2) + block, f32)])
    matches = call(match_kernel, "matches", [((2, 8, slots), jnp.int32), ((nx, nx), bf16)])
    advance_outer = call(
        advance_outer_kernel, "advance_outer", [((8, slots), f32), side_out, side_out]
    )
    advance_inner = call(advance_inner_kernel, "advance_inner", [inner_out] + y_out)
    naturals = call(
        natural_kernel, "naturals", [((8, cz, cy, nx), f32), ((3 * xb, nx), bf16)], [pltpu.VMEM((2, COLS, cz * cy, xb), f32)]
    )
    finish = call(
        finish_kernel, "finish", [((cz, cy, nx), f32)] * 2,
        [pltpu.VMEM((8, slots), f32), pltpu.VMEM((4 * cz * cy, xb), f32), pltpu.VMEM((2, cz, cy, nx), f32), dma((2, cz))],
        hbm_out=True,
    )

    inputs = (order_param, orientation, cell_slot, tile_grains.reshape(1, slots))
    near, far, raw, raw_slots, ids = prepare_outer(
        *(pltpu.with_memory_space_constraint(array, pltpu.HBM) for array in inputs)
    )
    for step in range(STEPS):
        near_halo, far_halo = both(near, far, "gz")
        if step == 0:
            inner, y_near, y_far, blocks = prepare_inner(raw, raw_slots, near, far)
        else:
            inner, y_near, y_far = advance_inner(velocity, blocks, inner_local, near, far)
        y_near, y_far = both(y_near, y_far, "gy")
        if step == 0:
            (chooser,) = choosers(blocks)
        (trig,) = trigs(near, far, inner)
        rim, inner_local, acc, part = inner_terms(near, far, inner, trig, y_near, y_far, chooser)
        near_mixed, acc = near_terms(near, inner, trig, rim, near_halo, chooser, acc)
        far_mixed, message = far_terms(far, inner, trig, part, far_halo, chooser, acc)
        near_message, far_message = both(message, message, "gz")
        if step == 0:
            match, back = matches(ids, near_halo, far_halo)
        (outer_local,) = outer_locals(near, far, inner, trig, rim, near_halo, far_halo, near_mixed, far_mixed)
        if step < STEPS - 1:
            velocity, near, far = advance_outer(message, near_message, far_message, match, blocks, outer_local)
    natural, widen = naturals(outer_local, inner_local, back)
    return tuple(finish(message, near_message, far_message, match, blocks, natural, widen))


def solution(mesh):
    spec = P("gz", "gy", None)
    return jax.shard_map(shards, mesh=mesh, in_specs=(spec,) * 4, out_specs=(spec,) * 2, check_vma=False)
```
